32 devices in a mesh: wide: 4 (over z), narrow: 8 (over y, x, core).
Axes of the slice: x: 2, y: 2, z: 4, core: 2. Of those that a mesh axis runs over, the one named last changes fastest.
Arguments:
- layer_entry_input: bfloat16 [4096, 2048], P('wide'), may hold values from -6 to 6
- ln1_gain: float32 [2048], replicated, may hold values from 0.5 to 1.5
- ln1_bias: float32 [2048], replicated, may hold values from -1 to 1
- w_qkv: bfloat16 [2048, 3, 2048], P(None, None, 'narrow'), may hold values from -0.125 to 0.125
- b_qv: float32 [2, 2048], P(None, 'narrow'), may hold values from -1.5 to 1.5
- w_out: bfloat16 [2048, 2048], P('narrow'), may hold values from -2 to 2
- b_out: float32 [2048], replicated, may hold values from -1.5 to 1.5
- ln2_gain: float32 [2048], replicated, may hold values from 0.5 to 1.5
- ln2_bias: float32 [2048], replicated, may hold values from -1 to 1
- w_up: bfloat16 [2048, 8192], P(None, 'narrow'), may hold values from -0.125 to 0.125
- b_up: float32 [8192], P('narrow'), may hold values from -2.5 to 2.5
- w_down: bfloat16 [8192, 2048], P('narrow'), may hold values from -0.0625 to 0.0625
- b_down: float32 [2048], replicated, may hold values from -1.5 to 1.5
- document_index: int32 [4096], replicated, may hold values from 0 to 8, as said below
- positions: int32 [4096], replicated, may hold values from 0 to 767, as said below
- valid: int32 [4096], replicated, may hold values from 0 to 1, as said below
- cotangent: bfloat16 [4096, 2048], P('wide'), may hold values from -6 to 6
Outputs:
- output: bfloat16 [4096, 2048], P('wide')
- grad_input: bfloat16 [4096, 2048], P('wide')
- grad_ln1_gain: float32 [2048], replicated
- grad_ln1_bias: float32 [2048], replicated
- grad_w_qkv: float32 [2048, 3, 2048], P(None, None, 'narrow')
- grad_b_qv: float32 [2, 2048], P(None, 'narrow')
- grad_w_out: float32 [2048, 2048], P('narrow')
- grad_b_out: float32 [2048], replicated
- grad_ln2_gain: float32 [2048], replicated
- grad_ln2_bias: float32 [2048], replicated
- grad_w_up: float32 [2048, 8192], P(None, 'narrow')
- grad_b_up: float32 [8192], P('narrow')
- grad_w_down: float32 [8192, 2048], P('narrow')
- grad_b_down: float32 [2048], replicated
The draws below stay inside these ranges and needn't reach their ends.
Inputs may be any that keep to these rules, and one draw needn't show every extreme that they name: `document_index`: documents are contiguous and numbered in order from 0; each block of 1024 tokens of one index of wide holds exactly two document starts, and every document has at most 768 tokens. `positions`: counts from 0 at the first token of each document, padding included. `valid`: 0 exactly on the last 1 to 64 tokens of each document.
All inputs are finite; a program needn't handle non-finite values.
Results may differ from the reference program's by a relative error of at most 0.019.
Values may be sent and summed in bfloat16 or wider, within the bound.
No kernel may reach another device: no remote copies, remote signals or barrier semaphores. Data moves between devices by JAX's collectives and lax.ppermute only.
A program may use at most 192 MiB of HBM per device.

```python
import jax
import jax.numpy as jnp
from jax import lax

MODEL_WIDTH = 2048
HEADS = 16
HEAD_DIM = 128
FF = 8192
TOK_DEV = 1024
TOTAL_TOKENS = 4096
N_NARROW = 8


def layout_draw(key):
    folded = jax.random.fold_in(key, 11)
    block_count = TOTAL_TOKENS // TOK_DEV
    subkeys = jax.random.split(folded, 3)
    block_ids = jnp.arange(block_count, dtype=jnp.int32)[:, None]
    early_cut = jax.random.randint(subkeys[0], (block_count, 1), TOK_DEV // 8, TOK_DEV // 4 + 1)
    late_cut = jax.random.randint(subkeys[1], (block_count, 1), TOK_DEV // 2, 3 * TOK_DEV // 4 + 1)
    early_cut = jnp.where(block_ids == 1, TOK_DEV // 4, early_cut)
    late_cut = jnp.where(block_ids == 0, TOK_DEV // 2, late_cut)
    cuts = jnp.concatenate([early_cut + block_ids * TOK_DEV, late_cut + block_ids * TOK_DEV], axis=1).reshape(-1)
    placed = jnp.arange(TOTAL_TOKENS, dtype=jnp.int32)
    passed = placed[:, None] >= cuts[None, :]
    document = jnp.sum(passed.astype(jnp.int32), axis=1)
    begins = jnp.max(jnp.where(passed, cuts[None, :], 0), axis=1)
    ends = jnp.min(jnp.where(passed, TOTAL_TOKENS, cuts[None, :]), axis=1)
    ends = jnp.minimum(ends, TOTAL_TOKENS)
    padding_each = jax.random.randint(subkeys[2], (2 * block_count + 1,), 1, max(1, TOK_DEV // 16) + 1)
    padding_tokens = jnp.take(padding_each, document)
    living_flag = (placed < ends - padding_tokens).astype(jnp.int32)
    return (document.astype(jnp.int32), (placed - begins).astype(jnp.int32), living_flag)


def draw_document_index(key, part):
    return layout_draw(key)[0]


def draw_positions(key, part):
    return layout_draw(key)[1]


def draw_valid(key, part):
    return layout_draw(key)[2]


def level_of(stream_key, dims, cuts, low, largest):
    loudness, own = 1.0, jax.random.fold_in(stream_key, 6)
    for axis_at, blocks in cuts:
        heights = jnp.exp(jax.random.uniform(jax.random.fold_in(own, axis_at), (blocks,), jnp.float32, low / len(cuts), largest / len(cuts)))
        loudness = loudness * jnp.repeat(heights, dims[axis_at] // blocks).reshape([-1 if axis == axis_at else 1 for axis in range(len(dims))])
    return loudness


def centred(key, shape, deviation, limit, pieces=(), kind=jnp.bfloat16):
    factor_of = level_of(key, shape, pieces, -0.22, 0.18) if pieces else 1.0
    entries = jax.random.normal(key, shape, jnp.float32) * deviation * factor_of
    return jnp.minimum(jnp.maximum(entries, -limit), limit).astype(kind)


def setup_inputs(seed: int = 0) -> dict:
    key_list = jax.random.split(jax.random.key(seed), 18)
    return {
        "layer_entry_input": centred(key_list[0], (TOTAL_TOKENS, MODEL_WIDTH), 1.0, 6.0, ((0, 4),)),
        "ln1_gain": jnp.clip(1.0 + 0.1 * jax.random.normal(key_list[1], (MODEL_WIDTH,), jnp.float32), 0.5, 1.5),
        "ln1_bias": centred(key_list[2], (MODEL_WIDTH,), 0.2, 1.0, (), jnp.float32),
        "w_qkv": centred(key_list[3], (MODEL_WIDTH, 3, MODEL_WIDTH), MODEL_WIDTH ** -0.5, 0.125, ((2, 8),)),
        "b_qv": centred(key_list[4], (2, MODEL_WIDTH), 0.3, 1.5, ((1, 8),), jnp.float32),
        "w_out": centred(key_list[5], (MODEL_WIDTH, MODEL_WIDTH), (max(MODEL_WIDTH // 256, 1)) ** -0.5, 2.0, ((0, 8),)),
        "b_out": centred(key_list[6], (MODEL_WIDTH,), 0.3, 1.5, (), jnp.float32),
        "ln2_gain": jnp.clip(1.0 + 0.1 * jax.random.normal(key_list[7], (MODEL_WIDTH,), jnp.float32), 0.5, 1.5),
        "ln2_bias": centred(key_list[8], (MODEL_WIDTH,), 0.2, 1.0, (), jnp.float32),
        "w_up": centred(key_list[9], (MODEL_WIDTH, FF), MODEL_WIDTH ** -0.5, 0.125, ((1, 8),)),
        "b_up": centred(key_list[10], (FF,), 0.5, 2.5, ((0, 8),), jnp.float32),
        "w_down": centred(key_list[11], (FF, MODEL_WIDTH), FF ** -0.5, 0.0625, ((0, 8),)),
        "b_down": centred(key_list[12], (MODEL_WIDTH,), 0.3, 1.5, (), jnp.float32),
        "document_index": draw_document_index(jax.random.fold_in(key_list[17], 71), 0),
        "positions": draw_positions(jax.random.fold_in(key_list[17], 71), 0),
        "valid": draw_valid(jax.random.fold_in(key_list[17], 71), 0),
        "cotangent": centred(key_list[16], (TOTAL_TOKENS, MODEL_WIDTH), 1.0, 6.0, ((0, 4),)),
    }


@jax.custom_vjp
def low(v):
    return lax.optimization_barrier(v.astype(jnp.bfloat16)).astype(jnp.float32)

@jax.custom_vjp
def low_back(v):
    return v

def low_keep(v):
    return (low(v), None)

def low_pass(kept, grad):
    return (grad,)

def back_keep(v):
    return (v, None)

def back_low(kept, grad):
    return (low(grad),)
low.defvjp(low_keep, low_pass)
low_back.defvjp(back_keep, back_low)
HIGHEST = lax.Precision.HIGHEST

def layer_norm(values, gain, shift_term):
    center = values - lax.optimization_barrier(jnp.mean(values, axis=-1, keepdims=True))
    spread = lax.optimization_barrier(jnp.mean(center * center, axis=-1, keepdims=True))
    return center * lax.rsqrt(spread + 1e-05) * gain + shift_term

def head_attention(query, keys_in, values_in, allowed):
    scores = jnp.dot(query, keys_in.T, precision=HIGHEST) * HEAD_DIM ** (-0.5)
    scores = low_back(scores)
    scores = jnp.where(allowed, scores, -1e+30)
    weights = jax.nn.softmax(scores, axis=-1)
    return jnp.dot(low(weights), values_in, precision=HIGHEST)

def grouped_sum(inputs, weight_rows):
    split_in = inputs.reshape(inputs.shape[0], N_NARROW, inputs.shape[1] // N_NARROW)
    split_w = weight_rows.reshape(N_NARROW, weight_rows.shape[0] // N_NARROW, weight_rows.shape[1])
    partial_value = jnp.einsum('tgh,ghd->gtd', split_in, split_w, precision=HIGHEST)
    return low_back(lax.optimization_barrier(jnp.sum(low(partial_value), axis=0)))

def row_forward(params, hidden_in, segment_row, position_row, valid_row):
    ln1_gain, ln1_bias, w_qkv, b_qv, w_out, b_out, ln2_gain, ln2_bias, w_up, b_up, w_down, b_down = params
    length = hidden_in.shape[0]
    normed = low(layer_norm(hidden_in, ln1_gain, ln1_bias))
    mixed = jnp.einsum('td,dch->tch', normed, w_qkv, precision=HIGHEST)
    query = low(low_back(mixed[:, 0] + b_qv[0]))
    keys_all = low(low_back(mixed[:, 1]))
    values_all = low(low_back(mixed[:, 2] + b_qv[1]))
    places = jnp.arange(length, dtype=jnp.int32)
    allowed = (segment_row[None, :] == segment_row[:, None]) & (position_row[None, :] <= position_row[:, None]) & ((valid_row[None, :] == 1) | (places[None, :] == places[:, None]))

    def split_heads(values):
        return values.reshape(length, HEADS, HEAD_DIM).transpose(1, 0, 2)

    def one_head(triple):
        return head_attention(triple[0], triple[1], triple[2], allowed)
    attended = lax.map(jax.checkpoint(one_head), (split_heads(query), split_heads(keys_all), split_heads(values_all)))
    attended = low_back(low(attended.transpose(1, 0, 2).reshape(length, MODEL_WIDTH)))
    after_attn = hidden_in + b_out + grouped_sum(attended, w_out)
    normed_two = low(layer_norm(after_attn, ln2_gain, ln2_bias))
    upper = low_back(jnp.dot(normed_two, w_up, precision=HIGHEST) + b_up)
    active = low(jax.nn.gelu(upper))
    return after_attn + b_down + grouped_sum(active, w_down)

def reference(layer_entry_input, ln1_gain, ln1_bias, w_qkv, b_qv, w_out, b_out, ln2_gain, ln2_bias, w_up, b_up, w_down, b_down, document_index, positions, valid, cotangent):
    packed_row_count = 1
    stream_length = layer_entry_input.shape[0]
    params = tuple((entry.astype(jnp.float32) for entry in (ln1_gain, ln1_bias, w_qkv, b_qv, w_out, b_out, ln2_gain, ln2_bias, w_up, b_up, w_down, b_down)))
    hidden_state = layer_entry_input.astype(jnp.float32).reshape(packed_row_count, stream_length, MODEL_WIDTH)
    cotangent_rows = cotangent.astype(jnp.float32).reshape(packed_row_count, stream_length, MODEL_WIDTH)
    segment_rows = document_index.reshape(packed_row_count, stream_length)
    position_rows = positions.reshape(packed_row_count, stream_length)
    valid_row_mask = valid.reshape(packed_row_count, stream_length)

    def one_row(totals, inputs):
        hidden_row, cot_row, seg_row, pos_row, valid_row = inputs

        def forward(weights, row_in):
            return row_forward(weights, row_in, seg_row, pos_row, valid_row)
        output_row, pull = jax.vjp(forward, params, hidden_row)
        weight_grads, input_grad = pull(cot_row)
        totals = jax.tree.map(lambda left, right: left + right, totals, weight_grads)
        return (totals, (output_row.astype(jnp.bfloat16), input_grad.astype(jnp.bfloat16)))
    zeros = jax.tree.map(jnp.zeros_like, params)
    totals, (outputs, grads) = lax.scan(one_row, zeros, (hidden_state, cotangent_rows, segment_rows, position_rows, valid_row_mask))
    return (outputs.reshape(-1, MODEL_WIDTH), grads.reshape(-1, MODEL_WIDTH), totals[0], totals[1], totals[2], totals[3], totals[4], totals[5], totals[6], totals[7], totals[8], totals[9], totals[10], totals[11])
```

```python
import jax
import jax.numpy as jnp
from jax import lax
from jax.experimental import pallas as pl
from jax.experimental.pallas import tpu as pltpu
from jax.sharding import PartitionSpec as P

HEAD_DIM = 128
MAX_DOCUMENT = 768
QUERY_BLOCK = 256
WINDOW = MAX_DOCUMENT + QUERY_BLOCK
f32 = jnp.float32
bf16 = jnp.bfloat16


def add_low(a, b):
    return (a.astype(f32) + b.astype(f32)).astype(bf16)


def pick(value, index, dim):
    return lax.dynamic_index_in_dim(value, index, dim, keepdims=False)


def narrow_bit(bit):
    return (lax.axis_index("narrow") >> bit) & 1


def narrow_bits():
    return lax.axis_size("narrow").bit_length() - 1


def swap(value, bit):
    count = lax.axis_size("narrow")
    return lax.ppermute(value, "narrow", [(i, i ^ (1 << bit)) for i in range(count)])


def bit_orders():
    later = list(range(1, narrow_bits()))
    return later, later[::-1]


def row_block():
    bits = narrow_bits()
    return sum(narrow_bit(b) << (bits - 1 - b) for b in range(bits))


def reduce_rows(value):
    bits = narrow_bits()
    rows, width = value.shape
    half_rows = rows >> (bits + 1)
    value = value.reshape(2, rows // 2, width)
    mine = narrow_bit(0)
    value = add_low(pick(value, mine, 0), swap(pick(value, 1 - mine, 0), 0))
    value = value.reshape((2,) * (bits - 1) + (2, half_rows, width))
    parts = []
    for half, order in enumerate(bit_orders()):
        piece = lax.index_in_dim(value, half, bits - 1, keepdims=False)
        left = list(range(1, bits))
        for b in order:
            at = left.index(b)
            mine = narrow_bit(b)
            piece = add_low(pick(piece, mine, at), swap(pick(piece, 1 - mine, at), b))
            left.pop(at)
        parts.append(piece)
    return jnp.concatenate(parts, axis=0)


def pair(value, other, bit, dim):
    return jnp.where(
        narrow_bit(bit) == 0, jnp.stack([value, other], axis=dim), jnp.stack([other, value], axis=dim)
    )


def gather_rows(block):
    bits = narrow_bits()
    rows, width = block.shape
    parts = []
    for half, order in enumerate(bit_orders()):
        piece = block[half * (rows // 2) : (half + 1) * (rows // 2)]
        have = []
        for b in order[::-1]:
            piece = pair(piece, swap(piece, b), b, sum(1 for x in have if x < b))
            have.append(b)
        parts.append(piece)
    value = jnp.stack(parts, axis=bits - 1)
    value = pair(value, swap(value, 0), 0, 0)
    return value.reshape(rows << bits, width)


def narrow_total(value):
    for b in range(narrow_bits()):
        value = value + swap(value, b)
    return value


class Line:
    def __init__(self):
        self.count = lax.axis_size("wide")
        self.half = self.count // 2
        self.at = lax.axis_index("wide")
        self.stages = self.count - 1

    def step(self, stage, value):
        n, half = self.count, self.half
        if stage < half - 1:
            moves = [(stage, stage + 1), (n - 1 - stage, n - 2 - stage)]
        elif stage == half - 1:
            moves = [(half - 1, half), (half, half - 1)]
        else:
            a = n - 1 - stage
            moves = [(a, a - 1), (n - 1 - a, n - a)]
        got = lax.ppermute(value, "wide", moves)
        if stage < half:
            return (value.astype(f32) + got.astype(f32)).astype(value.dtype)
        a = n - 1 - stage
        return jnp.where((self.at == a - 1) | (self.at == n - a), got, value)

    def whole(self, value):
        for stage in range(self.stages):
            value = self.step(stage, value)
        return value

    def pipeline(self, chunks):
        state = list(chunks)
        for tick in range(len(chunks) + self.stages - 1):
            live = [
                (tick - stage, stage)
                for stage in range(self.stages)
                if 0 <= tick - stage < len(chunks)
            ]
            held = lax.optimization_barrier(tuple(state[k] for k, _ in live))
            for (k, stage), value in zip(live, held):
                state[k] = self.step(stage, value)
        return state


def norm_stats(values):
    center = values - jnp.mean(values, axis=-1, keepdims=True)
    spread = jnp.mean(center * center, axis=-1, keepdims=True)
    inverse = lax.rsqrt(spread + 1e-05)
    return (center * inverse, inverse)


def norm_back(grad_out, normed_raw, inverse, gain):
    scaled = grad_out * gain
    grad_in = inverse * (
        scaled
        - jnp.mean(scaled, axis=-1, keepdims=True)
        - normed_raw * jnp.mean(scaled * normed_raw, axis=-1, keepdims=True)
    )
    return (grad_in, jnp.sum(grad_out * normed_raw, axis=0), jnp.sum(grad_out, axis=0))


def dot(a, b, dims):
    return lax.dot_general(a, b, (dims, ((), ())), preferred_element_type=f32)


def window_probs(query, keys, pos, valid):
    scores = dot(query, keys, ((1,), (1,))) * HEAD_DIM**-0.5
    own = lax.broadcasted_iota(jnp.int32, scores.shape, 0) + MAX_DOCUMENT
    key = lax.broadcasted_iota(jnp.int32, scores.shape, 1)
    back = own - key
    allowed = ((back >= 0) & (back <= pos) & (valid == 1)) | (back == 0)
    scores = jnp.where(allowed, scores, -1e30)
    exps = jnp.exp(scores - jnp.max(scores, axis=-1, keepdims=True))
    return exps * (1.0 / jnp.sum(exps, axis=-1, keepdims=True))


def attend_kernel(q_ref, k_ref, v_ref, pos_ref, valid_ref, out_ref):
    start = pl.multiple_of(pl.program_id(1) * QUERY_BLOCK, QUERY_BLOCK)
    window = pl.ds(start, WINDOW)
    probs = window_probs(q_ref[...], k_ref[window, :], pos_ref[...], valid_ref[0])
    out_ref[...] = dot(probs.astype(bf16), v_ref[window, :], ((1,), (0,))).astype(bf16)


def attend_back_kernel(q_ref, k_ref, v_ref, do_ref, pos_ref, valid_ref, dq_ref, dk_ref, dv_ref):
    start = pl.multiple_of(pl.program_id(1) * QUERY_BLOCK, QUERY_BLOCK)
    window = pl.ds(start, WINDOW)

    @pl.when(pl.program_id(1) == 0)
    def _():
        dk_ref[...] = jnp.zeros_like(dk_ref)
        dv_ref[...] = jnp.zeros_like(dv_ref)

    query, keys, out = q_ref[...], k_ref[window, :], do_ref[...]
    probs = window_probs(query, keys, pos_ref[...], valid_ref[0])
    dprob = dot(out, v_ref[window, :], ((1,), (1,)))
    dscore = probs * (dprob - jnp.sum(probs * dprob, axis=-1, keepdims=True))
    dscore = dscore.astype(bf16)
    dq_ref[...] = (dot(dscore, keys, ((1,), (0,))) * HEAD_DIM**-0.5).astype(bf16)
    dk_ref[window, :] += dot(dscore, query, ((0,), (0,))) * HEAD_DIM**-0.5
    dv_ref[window, :] += dot(probs.astype(bf16), out, ((0,), (0,)))


def attend_specs(rows):
    block = pl.BlockSpec((QUERY_BLOCK, HEAD_DIM), lambda h, i: (i, h))
    joined = pl.BlockSpec((rows + MAX_DOCUMENT, HEAD_DIM), lambda h, i: (0, h))
    pos = pl.BlockSpec((QUERY_BLOCK, 1), lambda h, i: (i, 0))
    valid = pl.BlockSpec((1, 1, WINDOW), lambda h, i: (i, 0, 0))
    return block, joined, pos, valid


def attend(query, keys, vals, pos, valid):
    rows, width = query.shape
    block, joined, pos_spec, valid_spec = attend_specs(rows)
    return pl.pallas_call(
        attend_kernel,
        grid=(width // HEAD_DIM, rows // QUERY_BLOCK),
        in_specs=[block, joined, joined, pos_spec, valid_spec],
        out_specs=block,
        out_shape=jax.ShapeDtypeStruct((rows, width), bf16),
        name="attend",
    )(query, keys, vals, pos, valid)


def attend_back(query, keys, vals, out, pos, valid):
    rows, width = query.shape
    block, joined, pos_spec, valid_spec = attend_specs(rows)
    wide_shape = jax.ShapeDtypeStruct((rows + MAX_DOCUMENT, width), f32)
    return pl.pallas_call(
        attend_back_kernel,
        grid=(width // HEAD_DIM, rows // QUERY_BLOCK),
        in_specs=[block, joined, joined, block, pos_spec, valid_spec],
        out_specs=[block, joined, joined],
        out_shape=[jax.ShapeDtypeStruct((rows, width), bf16), wide_shape, wide_shape],
        name="attend_back",
    )(query, keys, vals, out, pos, valid)


def on_device(
    layer_entry_input,
    ln1_gain,
    ln1_bias,
    w_qkv,
    b_qv,
    w_out,
    b_out,
    ln2_gain,
    ln2_bias,
    w_up,
    b_up,
    w_down,
    b_down,
    document_index,
    positions,
    valid,
    cotangent,
):
    rows, width = layer_entry_input.shape
    local_width = w_qkv.shape[2]
    hidden = w_up.shape[1]
    line = Line()
    start = line.at * rows
    ahead = [(i, i + 1) for i in range(line.count - 1)]
    behind = [(i + 1, i) for i in range(line.count - 1)]
    block_rows = rows // lax.axis_size("narrow")
    block_start = row_block() * block_rows

    def rows_of(value):
        return lax.dynamic_slice_in_dim(value, block_start, block_rows, 0)

    pos = lax.dynamic_slice_in_dim(positions, start, rows, 0).reshape(rows, 1)
    padded_valid = jnp.concatenate([jnp.zeros((MAX_DOCUMENT,), jnp.int32), valid])
    valid_near = lax.dynamic_slice_in_dim(padded_valid, start, rows + MAX_DOCUMENT, 0)
    valid_windows = jnp.stack(
        [valid_near[i : i + WINDOW] for i in range(0, rows, QUERY_BLOCK)]
    ).reshape(rows // QUERY_BLOCK, 1, WINDOW)

    inputs = layer_entry_input.astype(f32)
    raw_one, _ = norm_stats(inputs)
    normed_one = (raw_one * ln1_gain + ln1_bias).astype(bf16)
    w_flat = w_qkv.reshape(width, 3 * local_width)
    mixed = dot(normed_one, w_flat[:, local_width:], ((1,), (0,)))
    keys = mixed[:, :local_width].astype(bf16)
    vals = (mixed[:, local_width:] + b_qv[1]).astype(bf16)
    halo_keys = lax.ppermute(keys[rows - MAX_DOCUMENT :], "wide", ahead)
    halo_vals = lax.ppermute(vals[rows - MAX_DOCUMENT :], "wide", ahead)
    query = (dot(normed_one, w_flat[:, :local_width], ((1,), (0,))) + b_qv[0]).astype(bf16)
    keys = jnp.concatenate([halo_keys, keys])
    vals = jnp.concatenate([halo_vals, vals])
    attended = attend(query, keys, vals, pos, valid_windows)
    attn_part = dot(attended, w_out, ((1,), (0,))).astype(bf16)
    attn_total = reduce_rows(attn_part).astype(f32)
    inputs_rows = rows_of(layer_entry_input).astype(f32)
    after_attn = inputs_rows + b_out + attn_total
    raw_two, inv_two = norm_stats(after_attn)
    normed_two = gather_rows((raw_two * ln2_gain + ln2_bias).astype(bf16))

    upper = dot(normed_two, w_up, ((1,), (0,))) + b_up
    active, gelu_pull = jax.vjp(jax.nn.gelu, upper)
    active = active.astype(bf16)
    step = hidden // 4
    chunks_down = [
        dot(active[:, i * step : (i + 1) * step], cotangent, ((0,), (0,))).astype(bf16)
        for i in range(4)
    ]
    grad_active = dot(cotangent, w_down, ((1,), (1,)))
    grad_upper = gelu_pull(grad_active)[0].astype(bf16)
    step = width // 4
    chunks_up = [
        dot(normed_two[:, i * step : (i + 1) * step], grad_upper, ((0,), (0,))).astype(bf16)
        for i in range(4)
    ]
    grad_b_up = jnp.sum(grad_upper.astype(f32), axis=0)
    back_part = dot(grad_upper, w_up, ((1,), (1,))).astype(bf16)
    grad_norm_two = reduce_rows(back_part).astype(f32)
    grad_resid, grad_ln2_gain, grad_ln2_bias = norm_back(grad_norm_two, raw_two, inv_two, ln2_gain)
    grad_out_rows = rows_of(cotangent).astype(f32)
    grad_mid = grad_out_rows + grad_resid
    grad_mid_low = gather_rows(grad_mid.astype(bf16))

    chunk_out = dot(attended, grad_mid_low, ((0,), (0,))).astype(bf16)
    grad_attended = dot(grad_mid_low, w_out, ((1,), (1,))).astype(bf16)
    grad_query, grad_keys, grad_vals = attend_back(
        query, keys, vals, grad_attended, pos, valid_windows
    )

    def carry(value):
        got = lax.ppermute(value[:MAX_DOCUMENT].astype(bf16), "wide", behind)
        low = rows - MAX_DOCUMENT
        own = value[MAX_DOCUMENT:]
        return jnp.concatenate([own[:low], own[low:] + got.astype(f32)]).astype(bf16)

    grad_mixed = [grad_query, carry(grad_keys), carry(grad_vals)]
    chunks_qkv = [dot(normed_one, part, ((0,), (0,))).astype(bf16) for part in grad_mixed]
    grad_b_qv = [jnp.sum(grad_mixed[i].astype(f32), axis=0) for i in (0, 2)]
    back_part = dot(jnp.concatenate(grad_mixed, axis=1), w_flat, ((1,), (1,))).astype(bf16)
    grad_norm_one = reduce_rows(back_part).astype(f32)
    raw_rows, inv_rows = norm_stats(inputs_rows)
    grad_resid, grad_ln1_gain, grad_ln1_bias = norm_back(
        grad_norm_one, raw_rows, inv_rows, ln1_gain
    )
    grad_input = gather_rows((grad_mid + grad_resid).astype(bf16))

    mlp_part = dot(active, w_down, ((1,), (0,))).astype(bf16)
    mlp_total = reduce_rows(mlp_part).astype(f32)
    output = gather_rows((after_attn + b_down + mlp_total).astype(bf16))

    early = narrow_total(
        jnp.stack(
            [
                grad_ln2_gain,
                grad_ln2_bias,
                jnp.sum(grad_mid, axis=0),
                jnp.sum(grad_out_rows, axis=0),
            ]
        )
    )
    late = narrow_total(jnp.stack([grad_ln1_gain, grad_ln1_bias]))
    early = line.whole(jnp.concatenate([early.reshape(-1), grad_b_up]).reshape(-1, 128))
    late = line.whole(jnp.concatenate([late.reshape(-1)] + grad_b_qv).reshape(-1, 128))
    early, late = early.reshape(-1), late.reshape(-1)
    grad_ln2_gain, grad_ln2_bias, grad_b_out, grad_b_down = early[: 4 * width].reshape(4, width)
    grad_b_up = early[4 * width :]
    grad_ln1_gain, grad_ln1_bias = late[: 2 * width].reshape(2, width)
    grad_b_qv = late[2 * width :].reshape(2, local_width)

    chunks = chunks_down + chunks_up + [chunk_out] + chunks_qkv
    done = [None] * len(chunks)
    for chain in range(2):
        done[chain::2] = line.pipeline(chunks[chain::2])
    done = [value.astype(f32) for value in done]
    grad_w_down = jnp.concatenate(done[:4])
    grad_w_up = jnp.concatenate(done[4:8])
    grad_w_out = done[8]
    grad_w_qkv = jnp.stack(done[9:12], axis=1)
    return (
        output,
        grad_input,
        grad_ln1_gain,
        grad_ln1_bias,
        grad_w_qkv,
        grad_b_qv,
        grad_w_out,
        grad_b_out,
        grad_ln2_gain,
        grad_ln2_bias,
        grad_w_up,
        grad_b_up,
        grad_w_down,
        grad_b_down,
    )


def solution(mesh):
    return jax.shard_map(
        on_device,
        mesh=mesh,
        in_specs=(
            P("wide", None),
            P(),
            P(),
            P(None, None, "narrow"),
            P(None, "narrow"),
            P("narrow", None),
            P(),
            P(),
            P(),
            P(None, "narrow"),
            P("narrow"),
            P("narrow", None),
            P(),
            P(),
            P(),
            P(),
            P("wide", None),
        ),
        out_specs=(
            P("wide", None),
            P("wide", None),
            P(),
            P(),
            P(None, None, "narrow"),
            P(None, "narrow"),
            P("narrow", None),
            P(),
            P(),
            P(),
            P(None, "narrow"),
            P("narrow"),
            P("narrow", None),
            P(),
        ),
        check_vma=False,
    )
```

```python
import jax
import jax.numpy as jnp
from jax import lax
from jax.experimental import pallas as pl
from jax.experimental.pallas import tpu as pltpu
from jax.sharding import PartitionSpec as P

HEAD_DIM = 128
MAX_DOCUMENT = 768
QUERY_BLOCK = 256
WINDOW = MAX_DOCUMENT + QUERY_BLOCK
f32 = jnp.float32
bf16 = jnp.bfloat16


def add_low(a, b):
    return (a.astype(f32) + b.astype(f32)).astype(a.dtype)


def pick(value, index, dim):
    return lax.dynamic_index_in_dim(value, index, dim, keepdims=False)


def narrow_bit(bit):
    return (lax.axis_index("narrow") >> bit) & 1


def narrow_bits():
    return lax.axis_size("narrow").bit_length() - 1


def swap(value, bit):
    count = lax.axis_size("narrow")
    return lax.ppermute(value, "narrow", [(i, i ^ (1 << bit)) for i in range(count)])


def bit_orders():
    later = list(range(1, narrow_bits()))
    return later, later[::-1]


def row_block():
    bits = narrow_bits()
    return sum(narrow_bit(b) << (bits - 1 - b) for b in range(bits))


def as_is(*values):
    return values


def at_calls(sync, *which):
    count = iter(range(99))
    return lambda *values: sync(*values) if next(count) in which else values


def reduce_rows(value, sync=as_is):
    bits = narrow_bits()
    rows, width = value.shape
    half_rows = rows >> (bits + 1)
    value = value.reshape(2, rows // 2, width)
    mine = narrow_bit(0)
    value = add_low(pick(value, mine, 0), swap(pick(value, 1 - mine, 0), 0))
    (value,) = sync(value)
    value = value.reshape((2,) * (bits - 1) + (2, half_rows, width))
    orders = bit_orders()
    parts = [lax.index_in_dim(value, half, bits - 1, keepdims=False) for half in range(2)]
    left = [list(range(1, bits)) for _ in orders]
    for step in range(bits - 1):
        for half, order in enumerate(orders):
            b = order[step]
            at = left[half].index(b)
            mine = narrow_bit(b)
            piece = parts[half]
            parts[half] = add_low(pick(piece, mine, at), swap(pick(piece, 1 - mine, at), b))
            left[half].pop(at)
        parts = list(sync(*parts))
    return jnp.concatenate(parts, axis=0)


def pair(value, other, bit, dim):
    return jnp.where(
        narrow_bit(bit) == 0, jnp.stack([value, other], axis=dim), jnp.stack([other, value], axis=dim)
    )


def gather_rows(block, sync=as_is):
    bits = narrow_bits()
    rows, width = block.shape
    orders = [order[::-1] for order in bit_orders()]
    parts = [block[half * (rows // 2) : (half + 1) * (rows // 2)] for half in range(2)]
    for step in range(bits - 1):
        for half, order in enumerate(orders):
            b = order[step]
            at = sum(1 for x in order[:step] if x < b)
            parts[half] = pair(parts[half], swap(parts[half], b), b, at)
        parts = list(sync(*parts))
    value = jnp.stack(parts, axis=bits - 1)
    value = pair(value, swap(value, 0), 0, 0)
    return value.reshape(rows << bits, width)


def narrow_total(value):
    for b in range(narrow_bits()):
        value = value + swap(value, b)
    return value


class Line:
    def __init__(self):
        self.count = lax.axis_size("wide")
        self.half = self.count // 2
        self.at = lax.axis_index("wide")
        self.depth = jnp.minimum(self.at, self.count - 1 - self.at)

    def exchange(self, value, kind):
        moves = {i: i for i in range(self.count)}
        for i in range(kind, self.count - 1, 2):
            moves[i], moves[i + 1] = i + 1, i
        return lax.ppermute(value, "wide", list(moves.items()))

    def swaps(self, kind, tick, count):
        n, half = self.count, self.half
        plan = []
        for e in range(half):
            if e % 2 == kind:
                sent = tick - e
                got, add = (sent, True) if e == half - 1 else (tick - (n - 2 - e), False)
            elif e:
                sent, got, add = tick - (n - 1 - e), tick - (e - 1), True
            else:
                continue
            sent = sent if 0 <= sent < count else None
            got = got if 0 <= got < count else None
            plan.append((e, sent, got, add))
        return plan

    def whole(self, value):
        lane = Lane(self)
        lane.chunks.append(value)
        while lane.live():
            lane.start()
            lane.take(lane.waiting())
        return lane.chunks[0]


class Lane:
    def __init__(self, line):
        self.line = line
        self.chunks = []
        self.count = None
        self.tick = 0
        self.flying = []

    def total(self):
        return self.count or len(self.chunks)

    def live(self):
        return self.tick < self.total() + self.line.count - 2

    def start(self):
        self.flying = []
        for kind in range(2):
            plan = self.line.swaps(kind, self.tick, self.total())
            sends = [(e, sent) for e, sent, _, _ in plan if sent is not None]
            if not sends:
                continue
            value = self.chunks[sends[0][1]]
            for e, sent in sends[1:]:
                value = jnp.where(self.line.depth == e, self.chunks[sent], value)
            got = self.line.exchange(value, kind)
            self.flying.append((got, plan))

    def waiting(self):
        return tuple(got for got, _ in self.flying)

    def take(self, values):
        short = self.line.half == 2
        for got, (_, plan) in zip(values, self.flying):
            for e, _, k, add in plan:
                if k is None:
                    continue
                held = self.chunks[k]
                new = add_low(held, got) if add else got
                if not (add and short):
                    new = jnp.where(self.line.depth == e, new, held)
                self.chunks[k] = new
        self.tick += 1


class Bulk:
    def __init__(self, line, counts):
        self.lanes = [Lane(line) for _ in counts]
        for lane, count in zip(self.lanes, counts):
            lane.count = count
        self.turn = 0

    def feed(self, at, chunk):
        self.lanes[at].chunks.append(chunk)

    def sync(self, *values):
        lane = self.lanes[self.turn]
        self.turn = (self.turn + 1) % len(self.lanes)
        if not lane.live():
            return values
        got = lane.waiting()
        held = lax.optimization_barrier(got + tuple(values))
        lane.take(held[: len(got)])
        if lane.live():
            lane.start()
        return held[len(got) :]

    def finish(self):
        while any(lane.live() for lane in self.lanes):
            self.sync()


def norm_stats(values):
    center = values - jnp.mean(values, axis=-1, keepdims=True)
    spread = jnp.mean(center * center, axis=-1, keepdims=True)
    inverse = lax.rsqrt(spread + 1e-05)
    return (center * inverse, inverse)


def norm_back(grad_out, normed_raw, inverse, gain):
    scaled = grad_out * gain
    grad_in = inverse * (
        scaled
        - jnp.mean(scaled, axis=-1, keepdims=True)
        - normed_raw * jnp.mean(scaled * normed_raw, axis=-1, keepdims=True)
    )
    return (grad_in, jnp.sum(grad_out * normed_raw, axis=0), jnp.sum(grad_out, axis=0))


def dot(a, b, dims):
    return lax.dot_general(a, b, (dims, ((), ())), preferred_element_type=f32)


def window_probs(query, keys, pos, valid):
    scores = dot(query, keys, ((1,), (1,))) * HEAD_DIM**-0.5
    own = lax.broadcasted_iota(jnp.int32, scores.shape, 0) + MAX_DOCUMENT
    key = lax.broadcasted_iota(jnp.int32, scores.shape, 1)
    back = own - key
    allowed = ((back >= 0) & (back <= pos) & (valid == 1)) | (back == 0)
    scores = jnp.where(allowed, scores, -1e30)
    exps = jnp.exp(scores - jnp.max(scores, axis=-1, keepdims=True))
    return exps * (1.0 / jnp.sum(exps, axis=-1, keepdims=True))


def attend_kernel(q_ref, k_ref, v_ref, pos_ref, valid_ref, out_ref):
    start = pl.multiple_of(pl.program_id(1) * QUERY_BLOCK, QUERY_BLOCK)
    window = pl.ds(start, WINDOW)
    probs = window_probs(q_ref[...], k_ref[window, :], pos_ref[...], valid_ref[0])
    out_ref[...] = dot(probs.astype(bf16), v_ref[window, :], ((1,), (0,))).astype(bf16)


def attend_back_kernel(q_ref, k_ref, v_ref, do_ref, pos_ref, valid_ref, dq_ref, dk_ref, dv_ref):
    start = pl.multiple_of(pl.program_id(1) * QUERY_BLOCK, QUERY_BLOCK)
    window = pl.ds(start, WINDOW)

    @pl.when(pl.program_id(1) == 0)
    def _():
        dk_ref[...] = jnp.zeros_like(dk_ref)
        dv_ref[...] = jnp.zeros_like(dv_ref)

    query, keys, out = q_ref[...], k_ref[window, :], do_ref[...]
    probs = window_probs(query, keys, pos_ref[...], valid_ref[0])
    dprob = dot(out, v_ref[window, :], ((1,), (1,)))
    dscore = probs * (dprob - jnp.sum(probs * dprob, axis=-1, keepdims=True))
    dscore = dscore.astype(bf16)
    dq_ref[...] = (dot(dscore, keys, ((1,), (0,))) * HEAD_DIM**-0.5).astype(bf16)
    dk_ref[window, :] += dot(dscore, query, ((0,), (0,))) * HEAD_DIM**-0.5
    dv_ref[window, :] += dot(probs.astype(bf16), out, ((0,), (0,)))


def attend_specs(rows, heads):
    block = pl.BlockSpec((QUERY_BLOCK, HEAD_DIM), lambda h, i: (i, h))
    keys = pl.BlockSpec((rows + MAX_DOCUMENT, HEAD_DIM), lambda h, i: (0, h))
    vals = pl.BlockSpec((rows + MAX_DOCUMENT, HEAD_DIM), lambda h, i: (0, h + heads))
    pos = pl.BlockSpec((QUERY_BLOCK, 1), lambda h, i: (i, 0))
    valid = pl.BlockSpec((1, 1, WINDOW), lambda h, i: (i, 0, 0))
    return block, keys, vals, pos, valid


def attend(query, keys_vals, pos, valid):
    rows, width = query.shape
    heads = width // HEAD_DIM
    block, keys_spec, vals_spec, pos_spec, valid_spec = attend_specs(rows, heads)
    return pl.pallas_call(
        attend_kernel,
        grid=(heads, rows // QUERY_BLOCK),
        in_specs=[block, keys_spec, vals_spec, pos_spec, valid_spec],
        out_specs=block,
        out_shape=jax.ShapeDtypeStruct((rows, width), bf16),
        name="attend",
    )(query, keys_vals, keys_vals, pos, valid)


def attend_back(query, keys_vals, out, pos, valid):
    rows, width = query.shape
    heads = width // HEAD_DIM
    block, keys_spec, vals_spec, pos_spec, valid_spec = attend_specs(rows, heads)
    wide_shape = jax.ShapeDtypeStruct((rows + MAX_DOCUMENT, width), f32)
    return pl.pallas_call(
        attend_back_kernel,
        grid=(heads, rows // QUERY_BLOCK),
        in_specs=[block, keys_spec, vals_spec, block, pos_spec, valid_spec],
        out_specs=[block, keys_spec, keys_spec],
        out_shape=[jax.ShapeDtypeStruct((rows, width), bf16), wide_shape, wide_shape],
        name="attend_back",
    )(query, keys_vals, keys_vals, out, pos, valid)


def on_device(
    layer_entry_input,
    ln1_gain,
    ln1_bias,
    w_qkv,
    b_qv,
    w_out,
    b_out,
    ln2_gain,
    ln2_bias,
    w_up,
    b_up,
    w_down,
    b_down,
    document_index,
    positions,
    valid,
    cotangent,
):
    rows, width = layer_entry_input.shape
    local_width = w_qkv.shape[2]
    hidden = w_up.shape[1]
    line = Line()
    start = line.at * rows
    ahead = [(i, i + 1) for i in range(line.count - 1)]
    behind = [(i + 1, i) for i in range(line.count - 1)]
    block_rows = rows // lax.axis_size("narrow")
    block_start = row_block() * block_rows

    def rows_of(value):
        return lax.dynamic_slice_in_dim(value, block_start, block_rows, 0)

    pos = lax.dynamic_slice_in_dim(positions, start, rows, 0).reshape(rows, 1)
    padded_valid = jnp.concatenate([jnp.zeros((MAX_DOCUMENT,), jnp.int32), valid])
    valid_near = lax.dynamic_slice_in_dim(padded_valid, start, rows + MAX_DOCUMENT, 0)
    valid_windows = jnp.stack(
        [valid_near[i : i + WINDOW] for i in range(0, rows, QUERY_BLOCK)]
    ).reshape(rows // QUERY_BLOCK, 1, WINDOW)

    inputs = layer_entry_input.astype(f32)
    raw_one, _ = norm_stats(inputs)
    normed_one = (raw_one * ln1_gain + ln1_bias).astype(bf16)
    w_flat = w_qkv.reshape(width, 3 * local_width)
    mixed = dot(normed_one, w_flat[:, local_width:], ((1,), (0,)))
    bias = jnp.concatenate([jnp.zeros_like(b_qv[1]), b_qv[1]])
    keys_vals = (mixed + bias).astype(bf16)
    halo = lax.ppermute(keys_vals[rows - MAX_DOCUMENT :], "wide", ahead)
    query = (dot(normed_one, w_flat[:, :local_width], ((1,), (0,))) + b_qv[0]).astype(bf16)
    grad_active = dot(cotangent, w_down, ((1,), (1,))).astype(bf16)
    halo, query, grad_active = lax.optimization_barrier((halo, query, grad_active))
    keys_vals = jnp.concatenate([halo, keys_vals])
    attended = attend(query, keys_vals, pos, valid_windows)
    attn_part = dot(attended, w_out, ((1,), (0,))).astype(bf16)
    attn_total = reduce_rows(attn_part).astype(f32)
    inputs_rows = rows_of(layer_entry_input).astype(f32)
    after_attn = inputs_rows + b_out + attn_total
    raw_two, inv_two = norm_stats(after_attn)
    normed_two = gather_rows((raw_two * ln2_gain + ln2_bias).astype(bf16))

    upper = dot(normed_two, w_up, ((1,), (0,))) + b_up
    active, gelu_pull = jax.vjp(jax.nn.gelu, upper)
    active = active.astype(bf16)
    grad_upper = gelu_pull(grad_active.astype(f32))[0].astype(bf16)

    bulk = Bulk(line, (6, 6))
    step = width // 4
    places = [(i, j) for i in range(0, hidden, step) for j in range(0, width, hidden)]
    for at, (i, j) in enumerate(places):
        bulk.feed(
            at % 2,
            dot(active[:, i : i + step], cotangent[:, j : j + hidden], ((0,), (0,))).astype(bf16),
        )
    for lane in bulk.lanes:
        lane.start()
    for i in range(4):
        bulk.feed(
            i % 2,
            dot(normed_two[:, i * step : (i + 1) * step], grad_upper, ((0,), (0,))).astype(bf16),
        )
    grad_b_up = jnp.sum(grad_upper.astype(f32), axis=0)
    back_part = dot(grad_upper, w_up, ((1,), (1,))).astype(bf16)
    grad_norm_two = reduce_rows(back_part, at_calls(bulk.sync, 0, 1, 2)).astype(f32)
    grad_resid, grad_ln2_gain, grad_ln2_bias = norm_back(grad_norm_two, raw_two, inv_two, ln2_gain)
    grad_out_rows = rows_of(cotangent).astype(f32)
    grad_mid = grad_out_rows + grad_resid
    grad_mid_low = gather_rows(grad_mid.astype(bf16), at_calls(bulk.sync, 1))
    grad_attended = dot(grad_mid_low, w_out, ((1,), (1,))).astype(bf16)
    bulk.feed(
        0,
        jnp.concatenate(
            [
                dot(attended, grad_mid_low[:, j : j + hidden], ((0,), (0,))).astype(bf16)
                for j in range(0, width, hidden)
            ]
        ),
    )
    (grad_attended,) = bulk.sync(grad_attended)
    grad_query, grad_keys, grad_vals = attend_back(
        query, keys_vals, grad_attended, pos, valid_windows
    )
    grad_kv = jnp.concatenate([grad_keys, grad_vals], axis=1)
    got = lax.ppermute(grad_kv[:MAX_DOCUMENT].astype(bf16), "wide", behind)
    own = grad_kv[MAX_DOCUMENT:]
    mlp_part = dot(active, w_down, ((1,), (0,))).astype(bf16)
    own, mlp_part = bulk.sync(own, mlp_part)
    mlp_total = reduce_rows(mlp_part, at_calls(bulk.sync, 0)).astype(f32)
    low = rows - MAX_DOCUMENT
    grad_kv = jnp.concatenate([own[:low], own[low:] + got.astype(f32)]).astype(bf16)
    grad_mixed = jnp.concatenate([grad_query, grad_kv], axis=1)
    parts = [
        dot(normed_one[:, i * step : (i + 1) * step], grad_mixed, ((0,), (0,))).astype(bf16)
        for i in range(3)
    ]
    rest = dot(normed_one[:, 3 * step :], grad_mixed, ((0,), (0,))).astype(bf16)
    for i, lane in enumerate((1, 0, 1)):
        extra = rest[:, i * local_width : (i + 1) * local_width]
        bulk.feed(lane, jnp.concatenate([parts[i], extra], axis=1))
    grad_mixed, mlp_total = bulk.sync(grad_mixed, mlp_total)
    grad_b_qv = jnp.sum(grad_mixed.astype(f32), axis=0)
    grad_b_qv = [grad_b_qv[i * local_width : (i + 1) * local_width] for i in (0, 2)]
    back_part = dot(grad_mixed, w_flat, ((1,), (1,))).astype(bf16)
    output = gather_rows((after_attn + b_down + mlp_total).astype(bf16))
    grad_norm_one = reduce_rows(back_part, at_calls(bulk.sync, 0, 1, 2)).astype(f32)
    raw_rows, inv_rows = norm_stats(inputs_rows)
    grad_resid, grad_ln1_gain, grad_ln1_bias = norm_back(
        grad_norm_one, raw_rows, inv_rows, ln1_gain
    )
    grad_input = gather_rows((grad_mid + grad_resid).astype(bf16))

    sums = narrow_total(
        jnp.stack(
            [
                grad_ln2_gain,
                grad_ln2_bias,
                jnp.sum(grad_mid, axis=0),
                jnp.sum(grad_out_rows, axis=0),
                grad_ln1_gain,
                grad_ln1_bias,
            ]
        )
    )
    sums = jnp.concatenate([sums.reshape(-1), grad_b_up] + grad_b_qv)
    sums = line.whole(sums.reshape(-1, 128)).reshape(-1)
    bulk.finish()
    grad_ln2_gain, grad_ln2_bias, grad_b_out, grad_b_down, grad_ln1_gain, grad_ln1_bias = sums[
        : 6 * width
    ].reshape(6, width)
    grad_b_up = sums[6 * width : 6 * width + hidden]
    grad_b_qv = sums[6 * width + hidden :].reshape(2, local_width)

    done = [[value.astype(f32) for value in lane.chunks] for lane in bulk.lanes]
    per_row = width // hidden
    down = [done[at % 2][at // 2] for at in range(4)]
    grad_w_down = jnp.concatenate(
        [jnp.concatenate(down[i : i + per_row], axis=1) for i in range(0, 4, per_row)]
    )
    grad_w_up = jnp.concatenate([done[i % 2][2 + i // 2] for i in range(4)])
    grad_w_out = jnp.concatenate(
        [done[0][4][i * local_width : (i + 1) * local_width] for i in range(per_row)], axis=1
    )
    mixed_done = [done[1][4], done[0][5], done[1][5]]
    grad_w_qkv = jnp.stack(
        [
            jnp.concatenate(
                [value[:, c * local_width : (c + 1) * local_width] for value in mixed_done]
                + [mixed_done[c][:, 3 * local_width :]]
            )
            for c in range(3)
        ],
        axis=1,
    )
    return (
        output,
        grad_input,
        grad_ln1_gain,
        grad_ln1_bias,
        grad_w_qkv,
        grad_b_qv,
        grad_w_out,
        grad_b_out,
        grad_ln2_gain,
        grad_ln2_bias,
        grad_w_up,
        grad_b_up,
        grad_w_down,
        grad_b_down,
    )


def solution(mesh):
    return jax.shard_map(
        on_device,
        mesh=mesh,
        in_specs=(
            P("wide", None),
            P(),
            P(),
            P(None, None, "narrow"),
            P(None, "narrow"),
            P("narrow", None),
            P(),
            P(),
            P(),
            P(None, "narrow"),
            P("narrow"),
            P("narrow", None),
            P(),
            P(),
            P(),
            P(),
            P("wide", None),
        ),
        out_specs=(
            P("wide", None),
            P("wide", None),
            P(),
            P(),
            P(None, None, "narrow"),
            P(None, "narrow"),
            P("narrow", None),
            P(),
            P(),
            P(),
            P(None, "narrow"),
            P("narrow"),
            P("narrow", None),
            P(),
        ),
        check_vma=False,
    )
```

```python
import jax
import jax.numpy as jnp
from jax import lax
from jax.experimental import pallas as pl
from jax.sharding import PartitionSpec as P


HEAD_DIM = 128
MAX_DOCUMENT = 768
QUERY_BLOCK = 256
WINDOW = MAX_DOCUMENT + QUERY_BLOCK
LAG = 3
f32 = jnp.float32
bf16 = jnp.bfloat16


def add_low(a, b):
    return (a.astype(f32) + b.astype(f32)).astype(a.dtype)


def pick(value, index, dim):
    return lax.dynamic_index_in_dim(value, index, dim, keepdims=False)


def narrow_bit(bit):
    return (lax.axis_index("narrow") >> bit) & 1


def narrow_bits():
    return lax.axis_size("narrow").bit_length() - 1


def swap(value, bit):
    count = lax.axis_size("narrow")
    return lax.ppermute(value, "narrow", [(i, i ^ (1 << bit)) for i in range(count)])


def bit_orders():
    later = list(range(1, narrow_bits()))
    return later, later[::-1]


def row_block():
    bits = narrow_bits()
    return sum(narrow_bit(b) << (bits - 1 - b) for b in range(bits))


def as_is(*values):
    return values


def at_calls(sync, *which):
    count = iter(range(99))
    return lambda *values: sync(*values) if next(count) in which else values


def reduce_rows(value, sync=as_is):
    bits = narrow_bits()
    rows, width = value.shape
    half_rows = rows >> (bits + 1)
    value = value.reshape(2, rows // 2, width)
    mine = narrow_bit(0)
    got = swap(pick(value, 1 - mine, 0), 0)
    value = add_low(pick(value, mine, 0), got)
    (value,) = sync(value)
    value = value.reshape((2,) * (bits - 1) + (2, half_rows, width))
    orders = bit_orders()
    parts = [lax.index_in_dim(value, half, bits - 1, keepdims=False) for half in range(2)]
    left = [list(range(1, bits)) for _ in orders]
    for step in range(bits - 1):
        for half, order in enumerate(orders):
            b = order[step]
            at = left[half].index(b)
            mine = narrow_bit(b)
            piece = parts[half]
            got = swap(pick(piece, 1 - mine, at), b)
            parts[half] = add_low(pick(piece, mine, at), got)
            left[half].pop(at)
        parts = list(sync(*parts))
    return jnp.concatenate(parts, axis=0)


def pair(value, other, bit, dim):
    return jnp.where(
        narrow_bit(bit) == 0, jnp.stack([value, other], axis=dim), jnp.stack([other, value], axis=dim)
    )


def gather_rows(block, sync=as_is):
    bits = narrow_bits()
    rows, width = block.shape
    orders = [order[::-1] for order in bit_orders()]
    parts = [block[half * (rows // 2) : (half + 1) * (rows // 2)] for half in range(2)]
    for step in range(bits - 1):
        for half, order in enumerate(orders):
            b = order[step]
            at = sum(1 for x in order[:step] if x < b)
            got = swap(parts[half], b)
            parts[half] = pair(parts[half], got, b, at)
        parts = list(sync(*parts))
    value = jnp.stack(parts, axis=bits - 1)
    value = pair(value, swap(value, 0), 0, 0)
    return value.reshape(rows << bits, width)


def narrow_total(value):
    for b in range(narrow_bits()):
        value = value + swap(value, b)
    return value


class Line:
    def __init__(self):
        self.count = lax.axis_size("wide")
        self.half = self.count // 2
        self.at = lax.axis_index("wide")
        self.depth = jnp.minimum(self.at, self.count - 1 - self.at)

    def exchange(self, value, kind):
        moves = {i: i for i in range(self.count)}
        for i in range(kind, self.count - 1, 2):
            moves[i], moves[i + 1] = i + 1, i
        return lax.ppermute(value, "wide", list(moves.items()))

    def swaps(self, kind, slot, count):
        n, half = self.count, self.half
        plan = []
        for e in range(half):
            if e % 2 == kind:
                sent = slot - LAG * (e // 2)
                add = e == half - 1
                got = sent if add else slot - LAG * ((n - 2 - e) // 2)
            elif e:
                sent, got, add = slot - LAG * ((n - 1 - e) // 2), slot - LAG * ((e - 1) // 2), True
            else:
                continue
            sent = sent if 0 <= sent < count else None
            got = got if 0 <= got < count else None
            plan.append((e, sent, got, add))
        return plan

    def whole(self, value):
        stream = Stream(self, 1)
        stream.feed(value)
        for slot in range(stream.slots()):
            for kind in range(2):
                stream.start(kind, slot)
                stream.take(kind, slot, stream.waiting(kind, slot))
        return stream.chunks[0]


class Stream:
    def __init__(self, line, count):
        self.line = line
        self.count = count
        self.chunks = []
        self.flying = {}
        self.turn = 0

    def slots(self):
        return self.count + LAG * ((self.line.count - 2) // 2)

    def feed(self, chunk):
        self.chunks.append(chunk)

    def start(self, kind, slot):
        plan = self.line.swaps(kind, slot, self.count)
        sends = [(e, sent) for e, sent, _, _ in plan if sent is not None]
        if not sends:
            return
        value = self.chunks[sends[0][1]]
        for e, sent in sends[1:]:
            value = jnp.where(self.line.depth == e, self.chunks[sent], value)
        got = self.line.exchange(value, kind)
        self.flying[kind, slot] = got, plan

    def waiting(self, kind, slot):
        flight = self.flying.get((kind, slot))
        return () if flight is None else flight[:1]

    def take(self, kind, slot, values):
        short = self.line.half == 2
        for got in values:
            for e, _, k, add in self.flying[kind, slot][1]:
                if k is None:
                    continue
                held = self.chunks[k]
                new = add_low(held, got) if add else got
                if not (add and short):
                    new = jnp.where(self.line.depth == e, new, held)
                self.chunks[k] = new

    def begin(self):
        self.start(0, 0)
        self.start(0, 1)

    def sync(self, *values):
        n = self.turn
        self.turn += 1
        outer, inner = self.waiting(0, n), self.waiting(1, n - 1)
        held = lax.optimization_barrier(outer + inner + tuple(values))
        self.take(0, n, held[: len(outer)])
        self.take(1, n - 1, held[len(outer) : len(outer) + len(inner)])
        self.start(1, n)
        self.start(0, n + 2)
        return held[len(outer) + len(inner) :]

    def finish(self):
        while self.turn < self.slots():
            self.sync()


def norm_stats(values):
    center = values - jnp.mean(values, axis=-1, keepdims=True)
    spread = jnp.mean(center * center, axis=-1, keepdims=True)
    inverse = lax.rsqrt(spread + 1e-05)
    return (center * inverse, inverse)


def norm_back(grad_out, normed_raw, inverse, gain):
    scaled = grad_out * gain
    grad_in = inverse * (
        scaled
        - jnp.mean(scaled, axis=-1, keepdims=True)
        - normed_raw * jnp.mean(scaled * normed_raw, axis=-1, keepdims=True)
    )
    return (grad_in, jnp.sum(grad_out * normed_raw, axis=0), jnp.sum(grad_out, axis=0))


def dot(a, b, dims):
    return lax.dot_general(a, b, (dims, ((), ())), preferred_element_type=f32)


def window_probs(query, keys, pos, valid):
    scores = dot(query, keys, ((1,), (1,))) * HEAD_DIM**-0.5
    own = lax.broadcasted_iota(jnp.int32, scores.shape, 0) + MAX_DOCUMENT
    key = lax.broadcasted_iota(jnp.int32, scores.shape, 1)
    back = own - key
    allowed = ((back >= 0) & (back <= pos) & (valid == 1)) | (back == 0)
    scores = jnp.where(allowed, scores, -1e30)
    exps = jnp.exp(scores - jnp.max(scores, axis=-1, keepdims=True))
    return exps * (1.0 / jnp.sum(exps, axis=-1, keepdims=True))


def attend_kernel(q_ref, k_ref, v_ref, pos_ref, valid_ref, out_ref):
    start = pl.multiple_of(pl.program_id(1) * QUERY_BLOCK, QUERY_BLOCK)
    window = pl.ds(start, WINDOW)
    probs = window_probs(q_ref[...], k_ref[window, :], pos_ref[...], valid_ref[0])
    out_ref[...] = dot(probs.astype(bf16), v_ref[window, :], ((1,), (0,))).astype(bf16)


def attend_back_kernel(q_ref, k_ref, v_ref, do_ref, pos_ref, valid_ref, dq_ref, dk_ref, dv_ref):
    start = pl.multiple_of(pl.program_id(1) * QUERY_BLOCK, QUERY_BLOCK)
    window = pl.ds(start, WINDOW)

    @pl.when(pl.program_id(1) == 0)
    def _():
        dk_ref[...] = jnp.zeros_like(dk_ref)
        dv_ref[...] = jnp.zeros_like(dv_ref)

    query, keys, out = q_ref[...], k_ref[window, :], do_ref[...]
    probs = window_probs(query, keys, pos_ref[...], valid_ref[0])
    dprob = dot(out, v_ref[window, :], ((1,), (1,)))
    dscore = probs * (dprob - jnp.sum(probs * dprob, axis=-1, keepdims=True))
    dscore = dscore.astype(bf16)
    dq_ref[...] = (dot(dscore, keys, ((1,), (0,))) * HEAD_DIM**-0.5).astype(bf16)
    dk_ref[window, :] += dot(dscore, query, ((0,), (0,))) * HEAD_DIM**-0.5
    dv_ref[window, :] += dot(probs.astype(bf16), out, ((0,), (0,)))


def attend_specs(rows, heads):
    block = pl.BlockSpec((QUERY_BLOCK, HEAD_DIM), lambda h, i: (i, h))
    keys = pl.BlockSpec((rows + MAX_DOCUMENT, HEAD_DIM), lambda h, i: (0, h))
    vals = pl.BlockSpec((rows + MAX_DOCUMENT, HEAD_DIM), lambda h, i: (0, h + heads))
    pos = pl.BlockSpec((QUERY_BLOCK, 1), lambda h, i: (i, 0))
    valid = pl.BlockSpec((1, 1, WINDOW), lambda h, i: (i, 0, 0))
    return block, keys, vals, pos, valid


def attend(query, keys_vals, pos, valid):
    rows, width = query.shape
    heads = width // HEAD_DIM
    block, keys_spec, vals_spec, pos_spec, valid_spec = attend_specs(rows, heads)
    return pl.pallas_call(
        attend_kernel,
        grid=(heads, rows // QUERY_BLOCK),
        in_specs=[block, keys_spec, vals_spec, pos_spec, valid_spec],
        out_specs=block,
        out_shape=jax.ShapeDtypeStruct((rows, width), bf16),
        name="attend",
    )(query, keys_vals, keys_vals, pos, valid)


def attend_back(query, keys_vals, out, pos, valid):
    rows, width = query.shape
    heads = width // HEAD_DIM
    block, keys_spec, vals_spec, pos_spec, valid_spec = attend_specs(rows, heads)
    wide_shape = jax.ShapeDtypeStruct((rows + MAX_DOCUMENT, width), f32)
    return pl.pallas_call(
        attend_back_kernel,
        grid=(heads, rows // QUERY_BLOCK),
        in_specs=[block, keys_spec, vals_spec, block, pos_spec, valid_spec],
        out_specs=[block, keys_spec, keys_spec],
        out_shape=[jax.ShapeDtypeStruct((rows, width), bf16), wide_shape, wide_shape],
        name="attend_back",
    )(query, keys_vals, keys_vals, out, pos, valid)


def on_device(
    layer_entry_input,
    ln1_gain,
    ln1_bias,
    w_qkv,
    b_qv,
    w_out,
    b_out,
    ln2_gain,
    ln2_bias,
    w_up,
    b_up,
    w_down,
    b_down,
    document_index,
    positions,
    valid,
    cotangent,
):
    rows, width = layer_entry_input.shape
    local_width = w_qkv.shape[2]
    hidden = w_up.shape[1]
    line = Line()
    start = line.at * rows
    ahead = [(i, i + 1) for i in range(line.count - 1)]
    behind = [(i + 1, i) for i in range(line.count - 1)]
    block_rows = rows // lax.axis_size("narrow")
    block_start = row_block() * block_rows

    def rows_of(value):
        return lax.dynamic_slice_in_dim(value, block_start, block_rows, 0)

    pos = lax.dynamic_slice_in_dim(positions, start, rows, 0).reshape(rows, 1)
    padded_valid = jnp.concatenate([jnp.zeros((MAX_DOCUMENT,), jnp.int32), valid])
    valid_near = lax.dynamic_slice_in_dim(padded_valid, start, rows + MAX_DOCUMENT, 0)
    valid_windows = jnp.stack(
        [valid_near[i : i + WINDOW] for i in range(0, rows, QUERY_BLOCK)]
    ).reshape(rows // QUERY_BLOCK, 1, WINDOW)

    inputs = layer_entry_input.astype(f32)
    raw_one, _ = norm_stats(inputs)
    normed_one = (raw_one * ln1_gain + ln1_bias).astype(bf16)
    w_flat = w_qkv.reshape(width, 3 * local_width)
    mixed = dot(normed_one, w_flat[:, local_width:], ((1,), (0,)))
    bias = jnp.concatenate([jnp.zeros_like(b_qv[1]), b_qv[1]])
    keys_vals = (mixed + bias).astype(bf16)
    halo = lax.ppermute(keys_vals[rows - MAX_DOCUMENT :], "wide", ahead)
    query = (dot(normed_one, w_flat[:, :local_width], ((1,), (0,))) + b_qv[0]).astype(bf16)
    grad_active = dot(cotangent, w_down, ((1,), (1,))).astype(bf16)
    halo, query, grad_active = lax.optimization_barrier((halo, query, grad_active))
    keys_vals = jnp.concatenate([halo, keys_vals])
    attended = attend(query, keys_vals, pos, valid_windows)
    attn_part = dot(attended, w_out, ((1,), (0,))).astype(bf16)
    attn_total = reduce_rows(attn_part).astype(f32)
    inputs_rows = rows_of(layer_entry_input).astype(f32)
    after_attn = inputs_rows + b_out + attn_total
    raw_two, inv_two = norm_stats(after_attn)
    normed_two = gather_rows((raw_two * ln2_gain + ln2_bias).astype(bf16))

    upper = dot(normed_two, w_up, ((1,), (0,))) + b_up
    active, gelu_pull = jax.vjp(jax.nn.gelu, upper)
    active = active.astype(bf16)
    grad_upper = gelu_pull(grad_active.astype(f32))[0].astype(bf16)

    bulk = Stream(line, 12)
    step = width // 4
    places = [(i, j) for i in range(0, hidden, step) for j in range(0, width, hidden)]
    for i, j in places:
        bulk.feed(
            dot(active[:, i : i + step], cotangent[:, j : j + hidden], ((0,), (0,))).astype(bf16)
        )
    bulk.begin()
    for i in range(4):
        bulk.feed(
            dot(normed_two[:, i * step : (i + 1) * step], grad_upper, ((0,), (0,))).astype(bf16)
        )
    grad_b_up = jnp.sum(grad_upper.astype(f32), axis=0)
    back_part = dot(grad_upper, w_up, ((1,), (1,))).astype(bf16)
    grad_norm_two = reduce_rows(back_part, at_calls(bulk.sync, 1)).astype(f32)
    grad_resid, grad_ln2_gain, grad_ln2_bias = norm_back(grad_norm_two, raw_two, inv_two, ln2_gain)
    grad_out_rows = rows_of(cotangent).astype(f32)
    grad_mid = grad_out_rows + grad_resid
    grad_mid_low = gather_rows(grad_mid.astype(bf16), at_calls(bulk.sync, 0))
    grad_attended = dot(grad_mid_low, w_out, ((1,), (1,))).astype(bf16)
    bulk.feed(
        jnp.concatenate(
            [
                dot(attended, grad_mid_low[:, j : j + hidden], ((0,), (0,))).astype(bf16)
                for j in range(0, width, hidden)
            ]
        ),
    )
    (grad_attended,) = bulk.sync(grad_attended)
    grad_query, grad_keys, grad_vals = attend_back(
        query, keys_vals, grad_attended, pos, valid_windows
    )
    grad_kv = jnp.concatenate([grad_keys, grad_vals], axis=1)
    got = lax.ppermute(grad_kv[:MAX_DOCUMENT].astype(bf16), "wide", behind)
    own = grad_kv[MAX_DOCUMENT:]
    mlp_part = dot(active, w_down, ((1,), (0,))).astype(bf16)
    own, mlp_part = bulk.sync(own, mlp_part)
    held = [own]

    def sync_own(*values):
        *values, held[0] = bulk.sync(*values, held[0])
        return values

    mlp_total = reduce_rows(mlp_part, at_calls(sync_own, 1)).astype(f32)
    own = held[0]
    low = rows - MAX_DOCUMENT
    grad_kv = jnp.concatenate([own[:low], own[low:] + got.astype(f32)]).astype(bf16)
    grad_mixed = jnp.concatenate([grad_query, grad_kv], axis=1)
    parts = [
        dot(normed_one[:, i * step : (i + 1) * step], grad_mixed, ((0,), (0,))).astype(bf16)
        for i in range(3)
    ]
    rest = dot(normed_one[:, 3 * step :], grad_mixed, ((0,), (0,))).astype(bf16)
    for i in range(3):
        extra = rest[:, i * local_width : (i + 1) * local_width]
        bulk.feed(jnp.concatenate([parts[i], extra], axis=1))
    grad_mixed, mlp_total = bulk.sync(grad_mixed, mlp_total)
    grad_b_qv = jnp.sum(grad_mixed.astype(f32), axis=0)
    grad_b_qv = [grad_b_qv[i * local_width : (i + 1) * local_width] for i in (0, 2)]
    back_part = dot(grad_mixed, w_flat, ((1,), (1,))).astype(bf16)
    output = gather_rows((after_attn + b_down + mlp_total).astype(bf16))
    grad_norm_one = reduce_rows(back_part, at_calls(bulk.sync, 1)).astype(f32)
    raw_rows, inv_rows = norm_stats(inputs_rows)
    grad_resid, grad_ln1_gain, grad_ln1_bias = norm_back(
        grad_norm_one, raw_rows, inv_rows, ln1_gain
    )
    grad_input = gather_rows((grad_mid + grad_resid).astype(bf16), at_calls(bulk.sync, 0))

    sums = narrow_total(
        jnp.stack(
            [
                grad_ln2_gain,
                grad_ln2_bias,
                jnp.sum(grad_mid, axis=0),
                jnp.sum(grad_out_rows, axis=0),
                grad_ln1_gain,
                grad_ln1_bias,
            ]
        )
    )
    sums = jnp.concatenate([sums.reshape(-1), grad_b_up] + grad_b_qv)
    sums = line.whole(sums.reshape(-1, 128)).reshape(-1)
    bulk.finish()
    grad_ln2_gain, grad_ln2_bias, grad_b_out, grad_b_down, grad_ln1_gain, grad_ln1_bias = sums[
        : 6 * width
    ].reshape(6, width)
    grad_b_up = sums[6 * width : 6 * width + hidden]
    grad_b_qv = sums[6 * width + hidden :].reshape(2, local_width)

    done = [value.astype(f32) for value in bulk.chunks]
    per_row = width // hidden
    grad_w_down = jnp.concatenate(
        [jnp.concatenate(done[i : i + per_row], axis=1) for i in range(0, 4, per_row)]
    )
    grad_w_up = jnp.concatenate(done[4:8])
    grad_w_out = jnp.concatenate(
        [done[8][i * local_width : (i + 1) * local_width] for i in range(per_row)], axis=1
    )
    mixed_done = done[9:12]
    grad_w_qkv = jnp.stack(
        [
            jnp.concatenate(
                [value[:, c * local_width : (c + 1) * local_width] for value in mixed_done]
                + [mixed_done[c][:, 3 * local_width :]]
            )
            for c in range(3)
        ],
        axis=1,
    )
    return (
        output,
        grad_input,
        grad_ln1_gain,
        grad_ln1_bias,
        grad_w_qkv,
        grad_b_qv,
        grad_w_out,
        grad_b_out,
        grad_ln2_gain,
        grad_ln2_bias,
        grad_w_up,
        grad_b_up,
        grad_w_down,
        grad_b_down,
    )


def solution(mesh):
    return jax.shard_map(
        on_device,
        mesh=mesh,
        in_specs=(
            P("wide", None),
            P(),
            P(),
            P(None, None, "narrow"),
            P(None, "narrow"),
            P("narrow", None),
            P(),
            P(),
            P(),
            P(None, "narrow"),
            P("narrow"),
            P("narrow", None),
            P(),
            P(),
            P(),
            P(),
            P("wide", None),
        ),
        out_specs=(
            P("wide", None),
            P("wide", None),
            P(),
            P(),
            P(None, None, "narrow"),
            P(None, "narrow"),
            P("narrow", None),
            P(),
            P(),
            P(),
            P(None, "narrow"),
            P("narrow"),
            P("narrow", None),
            P(),
        ),
        check_vma=False,
    )
```

```python
import jax
import jax.numpy as jnp
from jax import lax
from jax.experimental import pallas as pl
from jax.sharding import PartitionSpec as P


HEAD_DIM = 128
MAX_DOCUMENT = 768
QUERY_BLOCK = 256
WINDOW = MAX_DOCUMENT + QUERY_BLOCK
LAG = 3
f32 = jnp.float32
bf16 = jnp.bfloat16


def add_low(a, b):
    return (a.astype(f32) + b.astype(f32)).astype(a.dtype)


def pick(value, index, dim):
    return lax.dynamic_index_in_dim(value, index, dim, keepdims=False)


def narrow_bit(bit):
    return (lax.axis_index("narrow") >> bit) & 1


def narrow_bits():
    return lax.axis_size("narrow").bit_length() - 1


def swap(value, bit):
    count = lax.axis_size("narrow")
    return lax.ppermute(value, "narrow", [(i, i ^ (1 << bit)) for i in range(count)])


def bit_orders():
    later = list(range(1, narrow_bits()))
    return later, later[::-1]


def row_block():
    bits = narrow_bits()
    return sum(narrow_bit(b) << (bits - 1 - b) for b in range(bits))


def as_is(*values):
    return values


def at_calls(sync, *which):
    count = iter(range(99))
    return lambda *values: sync(*values) if next(count) in which else values


def reduce_rows(value, sync=as_is):
    bits = narrow_bits()
    rows, width = value.shape
    half_rows = rows >> (bits + 1)
    value = value.reshape(2, rows // 2, width)
    mine = narrow_bit(0)
    got = swap(pick(value, 1 - mine, 0), 0)
    value = add_low(pick(value, mine, 0), got)
    (value,) = sync(value)
    value = value.reshape((2,) * (bits - 1) + (2, half_rows, width))
    orders = bit_orders()
    parts = [lax.index_in_dim(value, half, bits - 1, keepdims=False) for half in range(2)]
    left = [list(range(1, bits)) for _ in orders]
    for step in range(bits - 1):
        for half, order in enumerate(orders):
            b = order[step]
            at = left[half].index(b)
            mine = narrow_bit(b)
            piece = parts[half]
            got = swap(pick(piece, 1 - mine, at), b)
            parts[half] = add_low(pick(piece, mine, at), got)
            left[half].pop(at)
        parts = list(sync(*parts))
    return jnp.concatenate(parts, axis=0)


def pair(value, other, bit, dim):
    return jnp.where(
        narrow_bit(bit) == 0, jnp.stack([value, other], axis=dim), jnp.stack([other, value], axis=dim)
    )


def gather_rows(block, sync=as_is):
    bits = narrow_bits()
    rows, width = block.shape
    orders = [order[::-1] for order in bit_orders()]
    parts = [block[half * (rows // 2) : (half + 1) * (rows // 2)] for half in range(2)]
    for step in range(bits - 1):
        for half, order in enumerate(orders):
            b = order[step]
            at = sum(1 for x in order[:step] if x < b)
            got = swap(parts[half], b)
            parts[half] = pair(parts[half], got, b, at)
        parts = list(sync(*parts))
    value = jnp.stack(parts, axis=bits - 1)
    got = swap(value, 0)
    value = pair(value, got, 0, 0)
    return value.reshape(rows << bits, width)


def narrow_total(value):
    for b in range(narrow_bits()):
        value = value + swap(value, b)
    return value


class Line:
    def __init__(self):
        self.count = lax.axis_size("wide")
        self.half = self.count // 2
        self.at = lax.axis_index("wide")
        self.depth = jnp.minimum(self.at, self.count - 1 - self.at)

    def exchange(self, value, kind):
        moves = {i: i for i in range(self.count)}
        for i in range(kind, self.count - 1, 2):
            moves[i], moves[i + 1] = i + 1, i
        return lax.ppermute(value, "wide", list(moves.items()))

    def swaps(self, kind, slot, count):
        n, half = self.count, self.half
        plan = []
        for e in range(half):
            if e % 2 == kind:
                sent = slot - LAG * (e // 2)
                add = e == half - 1
                got = sent if add else slot - LAG * ((n - 2 - e) // 2)
            elif e:
                sent, got, add = slot - LAG * ((n - 1 - e) // 2), slot - LAG * ((e - 1) // 2), True
            else:
                continue
            sent = sent if 0 <= sent < count else None
            got = got if 0 <= got < count else None
            plan.append((e, sent, got, add))
        return plan

    def whole(self, value, sync):
        stream = Stream(self, 1)
        stream.feed(value)
        for slot in range(stream.slots()):
            for kind in range(2):
                stream.start(kind, slot)
                got = stream.waiting(kind, slot)
                if got:
                    stream.take(kind, slot, sync(*got))
        return stream.chunks[0]


class Stream:
    def __init__(self, line, count):
        self.line = line
        self.count = count
        self.chunks = []
        self.flying = {}
        self.turn = 0

    def slots(self):
        return self.count + LAG * ((self.line.count - 2) // 2)

    def feed(self, chunk):
        self.chunks.append(chunk)

    def start(self, kind, slot):
        plan = self.line.swaps(kind, slot, self.count)
        sends = [(e, sent) for e, sent, _, _ in plan if sent is not None]
        if not sends:
            return
        value = self.chunks[sends[0][1]]
        for e, sent in sends[1:]:
            value = jnp.where(self.line.depth == e, self.chunks[sent], value)
        got = self.line.exchange(value, kind)
        self.flying[kind, slot] = got, plan

    def waiting(self, kind, slot):
        flight = self.flying.get((kind, slot))
        return () if flight is None else flight[:1]

    def take(self, kind, slot, values):
        short = self.line.half == 2
        for got in values:
            for e, _, k, add in self.flying[kind, slot][1]:
                if k is None:
                    continue
                held = self.chunks[k]
                new = add_low(held, got) if add else got
                if not (add and short):
                    new = jnp.where(self.line.depth == e, new, held)
                self.chunks[k] = new

    def begin(self):
        self.start(0, 0)
        self.start(0, 1)

    def sync(self, *values):
        n = self.turn
        self.turn += 1
        outer = self.waiting(0, n)
        held = lax.optimization_barrier(outer + tuple(values))
        self.take(0, n, held[: len(outer)])
        self.start(1, n)
        self.take(1, n - 1, self.waiting(1, n - 1))
        self.start(0, n + 2)
        return held[len(outer) :]

    def finish(self):
        while self.turn < self.slots():
            self.sync()


def norm_stats(values):
    center = values - jnp.mean(values, axis=-1, keepdims=True)
    spread = jnp.mean(center * center, axis=-1, keepdims=True)
    inverse = lax.rsqrt(spread + 1e-05)
    return (center * inverse, inverse)


def norm_back(grad_out, normed_raw, inverse, gain):
    scaled = grad_out * gain
    grad_in = inverse * (
        scaled
        - jnp.mean(scaled, axis=-1, keepdims=True)
        - normed_raw * jnp.mean(scaled * normed_raw, axis=-1, keepdims=True)
    )
    return (grad_in, jnp.sum(grad_out * normed_raw, axis=0), jnp.sum(grad_out, axis=0))


def dot(a, b, dims):
    return lax.dot_general(a, b, (dims, ((), ())), preferred_element_type=f32)


def window_probs(query, keys, pos, valid):
    scores = dot(query, keys, ((1,), (1,))) * HEAD_DIM**-0.5
    own = lax.broadcasted_iota(jnp.int32, scores.shape, 0) + MAX_DOCUMENT
    key = lax.broadcasted_iota(jnp.int32, scores.shape, 1)
    back = own - key
    allowed = ((back >= 0) & (back <= pos) & (valid == 1)) | (back == 0)
    scores = jnp.where(allowed, scores, -1e30)
    exps = jnp.exp(scores - jnp.max(scores, axis=-1, keepdims=True))
    return exps * (1.0 / jnp.sum(exps, axis=-1, keepdims=True))


def attend_kernel(q_ref, k_ref, v_ref, pos_ref, valid_ref, out_ref):
    start = pl.multiple_of(pl.program_id(1) * QUERY_BLOCK, QUERY_BLOCK)
    window = pl.ds(start, WINDOW)
    probs = window_probs(q_ref[...], k_ref[window, :], pos_ref[...], valid_ref[0])
    out_ref[...] = dot(probs.astype(bf16), v_ref[window, :], ((1,), (0,))).astype(bf16)


def attend_back_kernel(q_ref, k_ref, v_ref, do_ref, pos_ref, valid_ref, dq_ref, dk_ref, dv_ref):
    start = pl.multiple_of(pl.program_id(1) * QUERY_BLOCK, QUERY_BLOCK)
    window = pl.ds(start, WINDOW)

    @pl.when(pl.program_id(1) == 0)
    def _():
        dk_ref[...] = jnp.zeros_like(dk_ref)
        dv_ref[...] = jnp.zeros_like(dv_ref)

    query, keys, out = q_ref[...], k_ref[window, :], do_ref[...]
    probs = window_probs(query, keys, pos_ref[...], valid_ref[0])
    dprob = dot(out, v_ref[window, :], ((1,), (1,)))
    dscore = probs * (dprob - jnp.sum(probs * dprob, axis=-1, keepdims=True))
    dscore = dscore.astype(bf16)
    dq_ref[...] = (dot(dscore, keys, ((1,), (0,))) * HEAD_DIM**-0.5).astype(bf16)
    dk_ref[window, :] += dot(dscore, query, ((0,), (0,))) * HEAD_DIM**-0.5
    dv_ref[window, :] += dot(probs.astype(bf16), out, ((0,), (0,)))


def attend_specs(rows, heads):
    block = pl.BlockSpec((QUERY_BLOCK, HEAD_DIM), lambda h, i: (i, h))
    keys = pl.BlockSpec((rows + MAX_DOCUMENT, HEAD_DIM), lambda h, i: (0, h))
    vals = pl.BlockSpec((rows + MAX_DOCUMENT, HEAD_DIM), lambda h, i: (0, h + heads))
    pos = pl.BlockSpec((QUERY_BLOCK, 1), lambda h, i: (i, 0))
    valid = pl.BlockSpec((1, 1, WINDOW), lambda h, i: (i, 0, 0))
    return block, keys, vals, pos, valid


def attend(query, keys_vals, pos, valid):
    rows, width = query.shape
    heads = width // HEAD_DIM
    block, keys_spec, vals_spec, pos_spec, valid_spec = attend_specs(rows, heads)
    return pl.pallas_call(
        attend_kernel,
        grid=(heads, rows // QUERY_BLOCK),
        in_specs=[block, keys_spec, vals_spec, pos_spec, valid_spec],
        out_specs=block,
        out_shape=jax.ShapeDtypeStruct((rows, width), bf16),
        name="attend",
    )(query, keys_vals, keys_vals, pos, valid)


def attend_back(query, keys_vals, out, pos, valid):
    rows, width = query.shape
    heads = width // HEAD_DIM
    block, keys_spec, vals_spec, pos_spec, valid_spec = attend_specs(rows, heads)
    wide_shape = jax.ShapeDtypeStruct((rows + MAX_DOCUMENT, width), f32)
    return pl.pallas_call(
        attend_back_kernel,
        grid=(heads, rows // QUERY_BLOCK),
        in_specs=[block, keys_spec, vals_spec, block, pos_spec, valid_spec],
        out_specs=[block, keys_spec, keys_spec],
        out_shape=[jax.ShapeDtypeStruct((rows, width), bf16), wide_shape, wide_shape],
        name="attend_back",
    )(query, keys_vals, keys_vals, out, pos, valid)


def tile_kernel(*refs):
    *parts, out_ref = refs
    for at, part in enumerate(parts):

        @pl.when(pl.program_id(0) == at)
        def _():
            out_ref[...] = part[...].astype(f32)


def tiled(parts, per_row):
    rows, cols = parts[0].shape
    return pl.pallas_call(
        tile_kernel,
        grid=(len(parts),),
        in_specs=[pl.BlockSpec((rows, cols), lambda i: (0, 0)) for _ in parts],
        out_specs=pl.BlockSpec((rows, cols), lambda i: (i // per_row, i % per_row)),
        out_shape=jax.ShapeDtypeStruct((len(parts) // per_row * rows, per_row * cols), f32),
        name="tiled",
    )(*parts)


def on_device(
    layer_entry_input,
    ln1_gain,
    ln1_bias,
    w_qkv,
    b_qv,
    w_out,
    b_out,
    ln2_gain,
    ln2_bias,
    w_up,
    b_up,
    w_down,
    b_down,
    document_index,
    positions,
    valid,
    cotangent,
):
    rows, width = layer_entry_input.shape
    local_width = w_qkv.shape[2]
    hidden = w_up.shape[1]
    line = Line()
    start = line.at * rows
    ahead = [(i, i + 1) for i in range(line.count - 1)]
    behind = [(i + 1, i) for i in range(line.count - 1)]
    block_rows = rows // lax.axis_size("narrow")
    block_start = row_block() * block_rows

    def rows_of(value):
        return lax.dynamic_slice_in_dim(value, block_start, block_rows, 0)

    pos = lax.dynamic_slice_in_dim(positions, start, rows, 0).reshape(rows, 1)
    padded_valid = jnp.concatenate([jnp.zeros((MAX_DOCUMENT,), jnp.int32), valid])
    valid_near = lax.dynamic_slice_in_dim(padded_valid, start, rows + MAX_DOCUMENT, 0)
    valid_windows = jnp.stack(
        [valid_near[i : i + WINDOW] for i in range(0, rows, QUERY_BLOCK)]
    ).reshape(rows // QUERY_BLOCK, 1, WINDOW)

    inputs = layer_entry_input.astype(f32)
    raw_one, _ = norm_stats(inputs)
    normed_one = (raw_one * ln1_gain + ln1_bias).astype(bf16)
    w_flat = w_qkv.reshape(width, 3 * local_width)
    mixed = dot(normed_one, w_flat[:, local_width:], ((1,), (0,)))
    bias = jnp.concatenate([jnp.zeros_like(b_qv[1]), b_qv[1]])
    keys_vals = (mixed + bias).astype(bf16)
    halo = lax.ppermute(keys_vals[rows - MAX_DOCUMENT :], "wide", ahead)
    query = (dot(normed_one, w_flat[:, :local_width], ((1,), (0,))) + b_qv[0]).astype(bf16)
    grad_active = dot(cotangent, w_down, ((1,), (1,))).astype(bf16)
    halo, query, grad_active = lax.optimization_barrier((halo, query, grad_active))
    keys_vals = jnp.concatenate([halo, keys_vals])
    attended = attend(query, keys_vals, pos, valid_windows)
    attn_part = dot(attended, w_out, ((1,), (0,))).astype(bf16)
    attn_total = reduce_rows(attn_part).astype(f32)
    inputs_rows = rows_of(layer_entry_input).astype(f32)
    after_attn = inputs_rows + b_out + attn_total
    raw_two, inv_two = norm_stats(after_attn)
    normed_two = gather_rows((raw_two * ln2_gain + ln2_bias).astype(bf16))

    upper = dot(normed_two, w_up, ((1,), (0,))) + b_up
    active, gelu_pull = jax.vjp(jax.nn.gelu, upper)
    active = active.astype(bf16)
    grad_upper = gelu_pull(grad_active.astype(f32))[0].astype(bf16)

    bulk = Stream(line, 12)
    step = width // 4
    places = [(i, j) for i in range(0, hidden, step) for j in range(0, width, hidden)]
    for i, j in places:
        bulk.feed(
            dot(active[:, i : i + step], cotangent[:, j : j + hidden], ((0,), (0,))).astype(bf16)
        )
    bulk.begin()
    for i in range(4):
        bulk.feed(
            dot(normed_two[:, i * step : (i + 1) * step], grad_upper, ((0,), (0,))).astype(bf16)
        )
    grad_b_up = jnp.sum(grad_upper.astype(f32), axis=0)
    back_part = dot(grad_upper, w_up, ((1,), (1,))).astype(bf16)
    grad_norm_two = reduce_rows(back_part, at_calls(bulk.sync, 1)).astype(f32)
    grad_resid, grad_ln2_gain, grad_ln2_bias = norm_back(grad_norm_two, raw_two, inv_two, ln2_gain)
    grad_out_rows = rows_of(cotangent).astype(f32)
    grad_mid = grad_out_rows + grad_resid
    grad_mid_low = gather_rows(grad_mid.astype(bf16), at_calls(bulk.sync, 0))
    grad_attended = dot(grad_mid_low, w_out, ((1,), (1,))).astype(bf16)
    bulk.feed(
        jnp.concatenate(
            [
                dot(attended, grad_mid_low[:, j : j + hidden], ((0,), (0,))).astype(bf16)
                for j in range(0, width, hidden)
            ]
        ),
    )
    (grad_attended,) = bulk.sync(grad_attended)
    grad_query, grad_keys, grad_vals = attend_back(
        query, keys_vals, grad_attended, pos, valid_windows
    )
    grad_kv = jnp.concatenate([grad_keys, grad_vals], axis=1)
    got = lax.ppermute(grad_kv[:MAX_DOCUMENT].astype(bf16), "wide", behind)
    own = grad_kv[MAX_DOCUMENT:]
    own, active = bulk.sync(own, active)
    mlp_part = dot(active, w_down, ((1,), (0,))).astype(bf16)
    held = [own]

    def sync_own(*values):
        *values, held[0] = bulk.sync(*values, held[0])
        return values

    mlp_total = reduce_rows(mlp_part, at_calls(sync_own, 1)).astype(f32)
    own = held[0]
    low = rows - MAX_DOCUMENT
    grad_kv = jnp.concatenate([own[:low], own[low:] + got.astype(f32)]).astype(bf16)
    grad_mixed = jnp.concatenate([grad_query, grad_kv], axis=1)
    parts = [
        dot(normed_one[:, i * step : (i + 1) * step], grad_mixed, ((0,), (0,))).astype(bf16)
        for i in range(3)
    ]
    rest = dot(normed_one[:, 3 * step :], grad_mixed, ((0,), (0,))).astype(bf16)
    for i in range(3):
        extra = rest[:, i * local_width : (i + 1) * local_width]
        bulk.feed(jnp.concatenate([parts[i], extra], axis=1))
    grad_mixed, mlp_total = bulk.sync(grad_mixed, mlp_total)
    grad_b_qv = jnp.sum(grad_mixed.astype(f32), axis=0)
    grad_b_qv = [grad_b_qv[i * local_width : (i + 1) * local_width] for i in (0, 2)]
    back_part = dot(grad_mixed, w_flat, ((1,), (1,))).astype(bf16)
    output = gather_rows((after_attn + b_down + mlp_total).astype(bf16))
    grad_norm_one = reduce_rows(back_part, at_calls(bulk.sync, 0, 2)).astype(f32)
    raw_rows, inv_rows = norm_stats(inputs_rows)
    grad_resid, grad_ln1_gain, grad_ln1_bias = norm_back(
        grad_norm_one, raw_rows, inv_rows, ln1_gain
    )
    grad_input = gather_rows((grad_mid + grad_resid).astype(bf16), at_calls(bulk.sync, 0, 1))

    sums = narrow_total(
        jnp.stack(
            [
                grad_ln2_gain,
                grad_ln2_bias,
                jnp.sum(grad_mid, axis=0),
                jnp.sum(grad_out_rows, axis=0),
                grad_ln1_gain,
                grad_ln1_bias,
            ]
        )
    )
    sums = jnp.concatenate([sums.reshape(-1), grad_b_up] + grad_b_qv)
    sums = line.whole(sums.reshape(-1, 128), bulk.sync).reshape(-1)
    bulk.finish()
    grad_ln2_gain, grad_ln2_bias, grad_b_out, grad_b_down, grad_ln1_gain, grad_ln1_bias = sums[
        : 6 * width
    ].reshape(6, width)
    grad_b_up = sums[6 * width : 6 * width + hidden]
    grad_b_qv = sums[6 * width + hidden :].reshape(2, local_width)

    done = [value.astype(f32) for value in bulk.chunks]
    per_row = width // hidden
    grad_w_down = tiled(bulk.chunks[:4], per_row)
    grad_w_up = tiled(bulk.chunks[4:8], 1)
    grad_w_out = jnp.concatenate(
        [done[8][i * local_width : (i + 1) * local_width] for i in range(per_row)], axis=1
    )
    mixed_done = done[9:12]
    grad_w_qkv = jnp.stack(
        [
            jnp.concatenate(
                [value[:, c * local_width : (c + 1) * local_width] for value in mixed_done]
                + [mixed_done[c][:, 3 * local_width :]]
            )
            for c in range(3)
        ],
        axis=1,
    )
    return (
        output,
        grad_input,
        grad_ln1_gain,
        grad_ln1_bias,
        grad_w_qkv,
        grad_b_qv,
        grad_w_out,
        grad_b_out,
        grad_ln2_gain,
        grad_ln2_bias,
        grad_w_up,
        grad_b_up,
        grad_w_down,
        grad_b_down,
    )


def solution(mesh):
    return jax.shard_map(
        on_device,
        mesh=mesh,
        in_specs=(
            P("wide", None),
            P(),
            P(),
            P(None, None, "narrow"),
            P(None, "narrow"),
            P("narrow", None),
            P(),
            P(),
            P(),
            P(None, "narrow"),
            P("narrow"),
            P("narrow", None),
            P(),
            P(),
            P(),
            P(),
            P("wide", None),
        ),
        out_specs=(
            P("wide", None),
            P("wide", None),
            P(),
            P(),
            P(None, None, "narrow"),
            P(None, "narrow"),
            P("narrow", None),
            P(),
            P(),
            P(),
            P(None, "narrow"),
            P("narrow"),
            P("narrow", None),
            P(),
        ),
        check_vma=False,
    )
```

```python
import jax
import jax.numpy as jnp
from jax import lax
from jax.experimental import pallas as pl
from jax.experimental.pallas import tpu as pltpu
from jax.sharding import PartitionSpec as P


HEAD_DIM = 128
MAX_DOCUMENT = 768
QUERY_BLOCK = 256
WINDOW = MAX_DOCUMENT + QUERY_BLOCK
LAG = 3
f32 = jnp.float32
bf16 = jnp.bfloat16


def add_low(a, b):
    return (a.astype(f32) + b.astype(f32)).astype(a.dtype)


def pick(value, index, dim):
    return lax.dynamic_index_in_dim(value, index, dim, keepdims=False)


def narrow_bit(bit):
    return (lax.axis_index("narrow") >> bit) & 1


def narrow_bits():
    return lax.axis_size("narrow").bit_length() - 1


def swap(value, bit):
    count = lax.axis_size("narrow")
    return lax.ppermute(value, "narrow", [(i, i ^ (1 << bit)) for i in range(count)])


def bit_orders():
    later = list(range(1, narrow_bits()))
    return later, later[::-1]


def row_block():
    bits = narrow_bits()
    return sum(narrow_bit(b) << (bits - 1 - b) for b in range(bits))


def as_is(*values):
    return values


def at_calls(sync, *which):
    count = iter(range(99))
    return lambda *values: sync(*values) if next(count) in which else values


def reduce_rows(value, sync=as_is):
    bits = narrow_bits()
    rows, width = value.shape
    half_rows = rows >> (bits + 1)
    value = value.reshape(2, rows // 2, width)
    mine = narrow_bit(0)
    got = swap(pick(value, 1 - mine, 0), 0)
    value = add_low(pick(value, mine, 0), got)
    (value,) = sync(value)
    value = value.reshape((2,) * (bits - 1) + (2, half_rows, width))
    orders = bit_orders()
    parts = [lax.index_in_dim(value, half, bits - 1, keepdims=False) for half in range(2)]
    left = [list(range(1, bits)) for _ in orders]
    for step in range(bits - 1):
        for half, order in enumerate(orders):
            b = order[step]
            at = left[half].index(b)
            mine = narrow_bit(b)
            piece = parts[half]
            got = swap(pick(piece, 1 - mine, at), b)
            parts[half] = add_low(pick(piece, mine, at), got)
            left[half].pop(at)
        parts = list(sync(*parts))
    return jnp.concatenate(parts, axis=0)


def pair(value, other, bit, dim):
    return jnp.where(
        narrow_bit(bit) == 0, jnp.stack([value, other], axis=dim), jnp.stack([other, value], axis=dim)
    )


def gather_rows(block, sync=as_is):
    bits = narrow_bits()
    rows, width = block.shape
    orders = [order[::-1] for order in bit_orders()]
    parts = [block[half * (rows // 2) : (half + 1) * (rows // 2)] for half in range(2)]
    for step in range(bits - 1):
        for half, order in enumerate(orders):
            b = order[step]
            at = sum(1 for x in order[:step] if x < b)
            got = swap(parts[half], b)
            parts[half] = pair(parts[half], got, b, at)
        parts = list(sync(*parts))
    value = jnp.stack(parts, axis=bits - 1)
    got = swap(value, 0)
    value = pair(value, got, 0, 0)
    return value.reshape(rows << bits, width)


def narrow_total(value):
    for b in range(narrow_bits()):
        value = value + swap(value, b)
    return value


class Line:
    def __init__(self):
        self.count = lax.axis_size("wide")
        self.half = self.count // 2
        self.at = lax.axis_index("wide")
        self.depth = jnp.minimum(self.at, self.count - 1 - self.at)

    def exchange(self, value, kind):
        pairs = [(i, i + 1) for i in range(kind, self.count - 1, 2)]
        return lax.ppermute(value, "wide", pairs + [(b, a) for a, b in pairs])

    def swaps(self, kind, slot, count):
        n, half = self.count, self.half
        plan = []
        for e in range(half):
            if e % 2 == kind:
                sent = slot - LAG * (e // 2)
                add = e == half - 1
                got = sent if add else slot - LAG * ((n - 2 - e) // 2)
            elif e:
                sent, got, add = slot - LAG * ((n - 1 - e) // 2), slot - LAG * ((e - 1) // 2), True
            else:
                continue
            sent = sent if 0 <= sent < count else None
            got = got if 0 <= got < count else None
            plan.append((e, sent, got, add))
        return plan

    def whole(self, value, sync):
        stream = Stream(self, 1)
        stream.feed(value)
        for slot in range(stream.slots()):
            for kind in range(2):
                stream.start(kind, slot)
                got = stream.waiting(kind, slot)
                if got:
                    stream.take(kind, slot, sync(*got))
        return stream.result(0)


class Stream:
    def __init__(self, line, count):
        self.line = line
        self.count = count
        self.chunks = []
        self.final = {}
        self.flying = {}
        self.turn = 0

    def slots(self):
        return self.count + LAG * ((self.line.count - 2) // 2)

    def feed(self, chunk):
        self.chunks.append(chunk)

    def edge(self):
        return (self.line.depth == 0).astype(jnp.int32).reshape(1)

    def pair(self, k):
        return self.chunks[k], self.final.get(k, self.chunks[k])

    def result(self, k):
        held, got = self.pair(k)
        return held if held is got else jnp.where(self.line.depth == 0, got, held)

    def tiles(self, start, stop, per_row):
        held, got = zip(*[self.pair(k) for k in range(start, stop)])
        return tiled(self.edge(), held, got, per_row)

    def start(self, kind, slot):
        plan = self.line.swaps(kind, slot, self.count)
        sends = [(e, sent) for e, sent, _, _ in plan if sent is not None]
        if not sends:
            return
        value = self.chunks[sends[0][1]]
        for e, sent in sends[1:]:
            value = jnp.where(self.line.depth == e, self.chunks[sent], value)
        got = self.line.exchange(value, kind)
        self.flying[kind, slot] = got, plan

    def waiting(self, kind, slot):
        flight = self.flying.get((kind, slot))
        return () if flight is None else flight[:1]

    def take(self, kind, slot, values):
        short = self.line.half == 2
        for got in values:
            for e, _, k, add in self.flying[kind, slot][1]:
                if k is None:
                    continue
                held = self.chunks[k]
                if not add and short:
                    self.final[k] = got
                    continue
                new = add_low(held, got) if add else got
                if not short:
                    new = jnp.where(self.line.depth == e, new, held)
                self.chunks[k] = new

    def begin(self):
        self.start(0, 0)
        self.start(0, 1)

    def sync(self, *values):
        n = self.turn
        self.turn += 1
        outer = self.waiting(0, n)
        held = lax.optimization_barrier(outer + tuple(values))
        self.take(0, n, held[: len(outer)])
        self.start(1, n)
        self.take(1, n - 1, self.waiting(1, n - 1))
        self.start(0, n + 2)
        return held[len(outer) :]

    def finish(self):
        while self.turn < self.slots():
            self.sync()


def norm_stats(values):
    center = values - jnp.mean(values, axis=-1, keepdims=True)
    spread = jnp.mean(center * center, axis=-1, keepdims=True)
    inverse = lax.rsqrt(spread + 1e-05)
    return (center * inverse, inverse)


def norm_back(grad_out, normed_raw, inverse, gain):
    scaled = grad_out * gain
    grad_in = inverse * (
        scaled
        - jnp.mean(scaled, axis=-1, keepdims=True)
        - normed_raw * jnp.mean(scaled * normed_raw, axis=-1, keepdims=True)
    )
    return (grad_in, jnp.sum(grad_out * normed_raw, axis=0), jnp.sum(grad_out, axis=0))


def dot(a, b, dims):
    return lax.dot_general(a, b, (dims, ((), ())), preferred_element_type=f32)


def window_probs(query, keys, pos, valid):
    scores = dot(query, keys, ((1,), (1,))) * HEAD_DIM**-0.5
    own = lax.broadcasted_iota(jnp.int32, scores.shape, 0) + MAX_DOCUMENT
    key = lax.broadcasted_iota(jnp.int32, scores.shape, 1)
    back = own - key
    allowed = ((back >= 0) & (back <= pos) & (valid == 1)) | (back == 0)
    scores = jnp.where(allowed, scores, -1e30)
    exps = jnp.exp(scores - jnp.max(scores, axis=-1, keepdims=True))
    return exps * (1.0 / jnp.sum(exps, axis=-1, keepdims=True))


def attend_kernel(q_ref, k_ref, v_ref, pos_ref, valid_ref, out_ref):
    start = pl.multiple_of(pl.program_id(1) * QUERY_BLOCK, QUERY_BLOCK)
    window = pl.ds(start, WINDOW)
    probs = window_probs(q_ref[...], k_ref[window, :], pos_ref[...], valid_ref[0])
    out_ref[...] = dot(probs.astype(bf16), v_ref[window, :], ((1,), (0,))).astype(bf16)


def attend_back_kernel(q_ref, k_ref, v_ref, do_ref, pos_ref, valid_ref, dq_ref, dk_ref, dv_ref):
    start = pl.multiple_of(pl.program_id(1) * QUERY_BLOCK, QUERY_BLOCK)
    window = pl.ds(start, WINDOW)

    @pl.when(pl.program_id(1) == 0)
    def _():
        dk_ref[...] = jnp.zeros_like(dk_ref)
        dv_ref[...] = jnp.zeros_like(dv_ref)

    query, keys, out = q_ref[...], k_ref[window, :], do_ref[...]
    probs = window_probs(query, keys, pos_ref[...], valid_ref[0])
    dprob = dot(out, v_ref[window, :], ((1,), (1,)))
    dscore = probs * (dprob - jnp.sum(probs * dprob, axis=-1, keepdims=True))
    dscore = dscore.astype(bf16)
    dq_ref[...] = (dot(dscore, keys, ((1,), (0,))) * HEAD_DIM**-0.5).astype(bf16)
    dk_ref[window, :] += dot(dscore, query, ((0,), (0,))) * HEAD_DIM**-0.5
    dv_ref[window, :] += dot(probs.astype(bf16), out, ((0,), (0,)))


def attend_specs(rows, heads):
    block = pl.BlockSpec((QUERY_BLOCK, HEAD_DIM), lambda h, i: (i, h))
    keys = pl.BlockSpec((rows + MAX_DOCUMENT, HEAD_DIM), lambda h, i: (0, h))
    vals = pl.BlockSpec((rows + MAX_DOCUMENT, HEAD_DIM), lambda h, i: (0, h + heads))
    pos = pl.BlockSpec((QUERY_BLOCK, 1), lambda h, i: (i, 0))
    valid = pl.BlockSpec((1, 1, WINDOW), lambda h, i: (i, 0, 0))
    return block, keys, vals, pos, valid


def attend(query, keys_vals, pos, valid):
    rows, width = query.shape
    heads = width // HEAD_DIM
    block, keys_spec, vals_spec, pos_spec, valid_spec = attend_specs(rows, heads)
    return pl.pallas_call(
        attend_kernel,
        grid=(heads, rows // QUERY_BLOCK),
        in_specs=[block, keys_spec, vals_spec, pos_spec, valid_spec],
        out_specs=block,
        out_shape=jax.ShapeDtypeStruct((rows, width), bf16),
        compiler_params=pltpu.CompilerParams(vmem_limit_bytes=16 << 20),
        name="attend",
    )(query, keys_vals, keys_vals, pos, valid)


def attend_back(query, keys_vals, out, pos, valid):
    rows, width = query.shape
    heads = width // HEAD_DIM
    block, keys_spec, vals_spec, pos_spec, valid_spec = attend_specs(rows, heads)
    wide_shape = jax.ShapeDtypeStruct((rows + MAX_DOCUMENT, width), f32)
    return pl.pallas_call(
        attend_back_kernel,
        grid=(heads, rows // QUERY_BLOCK),
        in_specs=[block, keys_spec, vals_spec, block, pos_spec, valid_spec],
        out_specs=[block, keys_spec, keys_spec],
        out_shape=[jax.ShapeDtypeStruct((rows, width), bf16), wide_shape, wide_shape],
        compiler_params=pltpu.CompilerParams(vmem_limit_bytes=24 << 20),
        name="attend_back",
    )(query, keys_vals, keys_vals, out, pos, valid)


def tile_kernel(edge_ref, *refs):
    *parts, out_ref = refs
    half = len(parts) // 2
    for at in range(half):
        for edge, part in enumerate((parts[at], parts[at + half])):

            @pl.when((pl.program_id(0) == at) & (edge_ref[0] == edge))
            def _(part=part):
                out_ref[...] = part[...].astype(f32)


def tiled(edge, held, got, per_row):
    rows, cols = held[0].shape
    parts = list(held) + list(got)
    whole = pl.BlockSpec((rows, cols), lambda i: (0, 0), pipeline_mode=pl.Buffered(1))
    return pl.pallas_call(
        tile_kernel,
        grid=(len(held),),
        in_specs=[pl.BlockSpec(memory_space=pltpu.SMEM)] + [whole for _ in parts],
        out_specs=pl.BlockSpec((rows, cols), lambda i: (i // per_row, i % per_row)),
        out_shape=jax.ShapeDtypeStruct((len(held) // per_row * rows, per_row * cols), f32),
        compiler_params=pltpu.CompilerParams(vmem_limit_bytes=16 << 20),
        name="tiled",
    )(edge, *parts)


def on_device(
    layer_entry_input,
    ln1_gain,
    ln1_bias,
    w_qkv,
    b_qv,
    w_out,
    b_out,
    ln2_gain,
    ln2_bias,
    w_up,
    b_up,
    w_down,
    b_down,
    document_index,
    positions,
    valid,
    cotangent,
):
    rows, width = layer_entry_input.shape
    local_width = w_qkv.shape[2]
    hidden = w_up.shape[1]
    line = Line()
    start = line.at * rows
    ahead = [(i, i + 1) for i in range(line.count - 1)]
    behind = [(i + 1, i) for i in range(line.count - 1)]
    block_rows = rows // lax.axis_size("narrow")
    block_start = row_block() * block_rows

    def rows_of(value):
        return lax.dynamic_slice_in_dim(value, block_start, block_rows, 0)

    pos = lax.dynamic_slice_in_dim(positions, start, rows, 0).reshape(rows, 1)
    padded_valid = jnp.concatenate([jnp.zeros((MAX_DOCUMENT,), jnp.int32), valid])
    valid_near = lax.dynamic_slice_in_dim(padded_valid, start, rows + MAX_DOCUMENT, 0)
    valid_windows = jnp.stack(
        [valid_near[i : i + WINDOW] for i in range(0, rows, QUERY_BLOCK)]
    ).reshape(rows // QUERY_BLOCK, 1, WINDOW)

    inputs = layer_entry_input.astype(f32)
    raw_one, _ = norm_stats(inputs)
    normed_one = (raw_one * ln1_gain + ln1_bias).astype(bf16)
    w_flat = w_qkv.reshape(width, 3 * local_width)
    mixed = dot(normed_one, w_flat[:, local_width:], ((1,), (0,)))
    bias = jnp.concatenate([jnp.zeros_like(b_qv[1]), b_qv[1]])
    keys_vals = (mixed + bias).astype(bf16)
    halo = lax.ppermute(keys_vals[rows - MAX_DOCUMENT :], "wide", ahead)
    query = (dot(normed_one, w_flat[:, :local_width], ((1,), (0,))) + b_qv[0]).astype(bf16)
    grad_active = dot(cotangent, w_down, ((1,), (1,))).astype(bf16)
    halo, query, grad_active = lax.optimization_barrier((halo, query, grad_active))
    keys_vals = jnp.concatenate([halo, keys_vals])
    attended = attend(query, keys_vals, pos, valid_windows)
    attn_part = dot(attended, w_out, ((1,), (0,))).astype(bf16)
    attn_total = reduce_rows(attn_part).astype(f32)
    inputs_rows = rows_of(layer_entry_input).astype(f32)
    after_attn = inputs_rows + b_out + attn_total
    raw_two, inv_two = norm_stats(after_attn)
    normed_two = gather_rows((raw_two * ln2_gain + ln2_bias).astype(bf16))

    upper = dot(normed_two, w_up, ((1,), (0,))) + b_up
    active, gelu_pull = jax.vjp(jax.nn.gelu, upper)
    active = active.astype(bf16)
    grad_upper = gelu_pull(grad_active.astype(f32))[0].astype(bf16)

    bulk = Stream(line, 12)
    step = width // 4
    places = [(i, j) for i in range(0, hidden, step) for j in range(0, width, hidden)]
    for i, j in places:
        bulk.feed(
            dot(active[:, i : i + step], cotangent[:, j : j + hidden], ((0,), (0,))).astype(bf16)
        )
    bulk.begin()
    for i in range(4):
        bulk.feed(
            dot(normed_two[:, i * step : (i + 1) * step], grad_upper, ((0,), (0,))).astype(bf16)
        )
    grad_b_up = jnp.sum(grad_upper.astype(f32), axis=0)
    back_part = dot(grad_upper, w_up, ((1,), (1,))).astype(bf16)
    grad_norm_two = reduce_rows(back_part, at_calls(bulk.sync, 1)).astype(f32)
    grad_resid, grad_ln2_gain, grad_ln2_bias = norm_back(grad_norm_two, raw_two, inv_two, ln2_gain)
    grad_out_rows = rows_of(cotangent).astype(f32)
    grad_mid = grad_out_rows + grad_resid
    grad_mid_low = gather_rows(grad_mid.astype(bf16), at_calls(bulk.sync, 0))
    grad_attended = dot(grad_mid_low, w_out, ((1,), (1,))).astype(bf16)
    bulk.feed(
        jnp.concatenate(
            [
                dot(attended, grad_mid_low[:, j : j + hidden], ((0,), (0,))).astype(bf16)
                for j in range(0, width, hidden)
            ]
        ),
    )
    (grad_attended,) = bulk.sync(grad_attended)
    grad_query, grad_keys, grad_vals = attend_back(
        query, keys_vals, grad_attended, pos, valid_windows
    )
    grad_kv = jnp.concatenate([grad_keys, grad_vals], axis=1)
    got = lax.ppermute(grad_kv[:MAX_DOCUMENT].astype(bf16), "wide", behind)
    own = grad_kv[MAX_DOCUMENT:]
    own, active = bulk.sync(own, active)
    mlp_part = dot(active, w_down, ((1,), (0,))).astype(bf16)
    held = [own]

    def sync_own(*values):
        *values, held[0] = bulk.sync(*values, held[0])
        return values

    mlp_total = reduce_rows(mlp_part, at_calls(sync_own, 1)).astype(f32)
    own = held[0]
    low = rows - MAX_DOCUMENT
    grad_kv = jnp.concatenate([own[:low], own[low:] + got.astype(f32)]).astype(bf16)
    grad_mixed = jnp.concatenate([grad_query, grad_kv], axis=1)
    parts = [
        dot(normed_one[:, i * step : (i + 1) * step], grad_mixed, ((0,), (0,))).astype(bf16)
        for i in range(3)
    ]
    rest = dot(normed_one[:, 3 * step :], grad_mixed, ((0,), (0,))).astype(bf16)
    for i in range(3):
        extra = rest[:, i * local_width : (i + 1) * local_width]
        bulk.feed(jnp.concatenate([parts[i], extra], axis=1))
    grad_mixed, mlp_total = bulk.sync(grad_mixed, mlp_total)
    grad_b_qv = jnp.sum(grad_mixed.astype(f32), axis=0)
    grad_b_qv = [grad_b_qv[i * local_width : (i + 1) * local_width] for i in (0, 2)]
    back_part = dot(grad_mixed, w_flat, ((1,), (1,))).astype(bf16)
    output = gather_rows((after_attn + b_down + mlp_total).astype(bf16))
    grad_norm_one = reduce_rows(back_part, at_calls(bulk.sync, 0, 2)).astype(f32)
    raw_rows, inv_rows = norm_stats(inputs_rows)
    grad_resid, grad_ln1_gain, grad_ln1_bias = norm_back(
        grad_norm_one, raw_rows, inv_rows, ln1_gain
    )
    grad_input = gather_rows((grad_mid + grad_resid).astype(bf16), at_calls(bulk.sync, 0, 1))

    sums = narrow_total(
        jnp.stack(
            [
                grad_ln2_gain,
                grad_ln2_bias,
                jnp.sum(grad_mid, axis=0),
                jnp.sum(grad_out_rows, axis=0),
                grad_ln1_gain,
                grad_ln1_bias,
            ]
        )
    )
    sums = jnp.concatenate([sums.reshape(-1), grad_b_up] + grad_b_qv)
    sums = line.whole(sums.reshape(-1, 128), bulk.sync).reshape(-1)
    bulk.finish()
    grad_ln2_gain, grad_ln2_bias, grad_b_out, grad_b_down, grad_ln1_gain, grad_ln1_bias = sums[
        : 6 * width
    ].reshape(6, width)
    grad_b_up = sums[6 * width : 6 * width + hidden]
    grad_b_qv = sums[6 * width + hidden :].reshape(2, local_width)

    done = [None] * 8 + [bulk.result(k).astype(f32) for k in range(8, 12)]
    per_row = width // hidden
    grad_w_down = bulk.tiles(0, 4, per_row)
    grad_w_up = bulk.tiles(4, 8, 1)
    grad_w_out = jnp.concatenate(
        [done[8][i * local_width : (i + 1) * local_width] for i in range(per_row)], axis=1
    )
    mixed_done = done[9:12]
    grad_w_qkv = jnp.stack(
        [
            jnp.concatenate(
                [value[:, c * local_width : (c + 1) * local_width] for value in mixed_done]
                + [mixed_done[c][:, 3 * local_width :]]
            )
            for c in range(3)
        ],
        axis=1,
    )
    return (
        output,
        grad_input,
        grad_ln1_gain,
        grad_ln1_bias,
        grad_w_qkv,
        grad_b_qv,
        grad_w_out,
        grad_b_out,
        grad_ln2_gain,
        grad_ln2_bias,
        grad_w_up,
        grad_b_up,
        grad_w_down,
        grad_b_down,
    )


def solution(mesh):
    return jax.shard_map(
        on_device,
        mesh=mesh,
        in_specs=(
            P("wide", None),
            P(),
            P(),
            P(None, None, "narrow"),
            P(None, "narrow"),
            P("narrow", None),
            P(),
            P(),
            P(),
            P(None, "narrow"),
            P("narrow"),
            P("narrow", None),
            P(),
            P(),
            P(),
            P(),
            P("wide", None),
        ),
        out_specs=(
            P("wide", None),
            P("wide", None),
            P(),
            P(),
            P(None, None, "narrow"),
            P(None, "narrow"),
            P("narrow", None),
            P(),
            P(),
            P(),
            P(None, "narrow"),
            P("narrow"),
            P("narrow", None),
            P(),
        ),
        check_vma=False,
    )
```

```python
import jax
import jax.numpy as jnp
from jax import lax
from jax.experimental import pallas as pl
from jax.experimental.pallas import tpu as pltpu
from jax.sharding import PartitionSpec as P


HEAD_DIM = 128
MAX_DOCUMENT = 768
QUERY_BLOCK = 256
WINDOW = MAX_DOCUMENT + QUERY_BLOCK
LAG = 3
f32 = jnp.float32
bf16 = jnp.bfloat16


def add_low(a, b):
    return (a.astype(f32) + b.astype(f32)).astype(a.dtype)


def pick(value, index, dim):
    return lax.dynamic_index_in_dim(value, index, dim, keepdims=False)


def narrow_bit(bit):
    return (lax.axis_index("narrow") >> bit) & 1


def narrow_bits():
    return lax.axis_size("narrow").bit_length() - 1


def swap(value, bit):
    count = lax.axis_size("narrow")
    return lax.ppermute(value, "narrow", [(i, i ^ (1 << bit)) for i in range(count)])


def bit_orders():
    later = list(range(1, narrow_bits()))
    return later, later[::-1]


def row_block():
    bits = narrow_bits()
    return sum(narrow_bit(b) << (bits - 1 - b) for b in range(bits))


def as_is(*values):
    return values


def at_calls(sync, *which):
    count = iter(range(99))
    return lambda *values: sync(*values) if next(count) in which else values


def reduce_rows(value, sync=as_is):
    bits = narrow_bits()
    rows, width = value.shape
    half_rows = rows >> (bits + 1)
    value = value.reshape(2, rows // 2, width)
    mine = narrow_bit(0)
    got = swap(pick(value, 1 - mine, 0), 0)
    value = add_low(pick(value, mine, 0), got)
    (value,) = sync(value)
    value = value.reshape((2,) * (bits - 1) + (2, half_rows, width))
    orders = bit_orders()
    parts = [lax.index_in_dim(value, half, bits - 1, keepdims=False) for half in range(2)]
    left = [list(range(1, bits)) for _ in orders]
    for step in range(bits - 1):
        for half, order in enumerate(orders):
            b = order[step]
            at = left[half].index(b)
            mine = narrow_bit(b)
            piece = parts[half]
            got = swap(pick(piece, 1 - mine, at), b)
            parts[half] = add_low(pick(piece, mine, at), got)
            left[half].pop(at)
        parts = list(sync(*parts))
    return jnp.concatenate(parts, axis=0)


def pair(value, other, bit, dim):
    return jnp.where(
        narrow_bit(bit) == 0, jnp.stack([value, other], axis=dim), jnp.stack([other, value], axis=dim)
    )


def gather_rows(block, sync=as_is):
    bits = narrow_bits()
    rows, width = block.shape
    orders = [order[::-1] for order in bit_orders()]
    parts = [block[half * (rows // 2) : (half + 1) * (rows // 2)] for half in range(2)]
    for step in range(bits - 1):
        for half, order in enumerate(orders):
            b = order[step]
            at = sum(1 for x in order[:step] if x < b)
            got = swap(parts[half], b)
            parts[half] = pair(parts[half], got, b, at)
        parts = list(sync(*parts))
    value = jnp.stack(parts, axis=bits - 1)
    got = swap(value, 0)
    value = pair(value, got, 0, 0)
    return value.reshape(rows << bits, width)


def narrow_total(value):
    for b in range(narrow_bits()):
        value = value + swap(value, b)
    return value


class Line:
    def __init__(self):
        self.count = lax.axis_size("wide")
        self.half = self.count // 2
        self.at = lax.axis_index("wide")
        self.depth = jnp.minimum(self.at, self.count - 1 - self.at)

    def exchange(self, value, kind):
        pairs = [(i, i + 1) for i in range(kind, self.count - 1, 2)]
        return lax.ppermute(value, "wide", pairs + [(b, a) for a, b in pairs])

    def swaps(self, kind, slot, count):
        n, half = self.count, self.half
        plan = []
        for e in range(half):
            if e % 2 == kind:
                sent = slot - LAG * (e // 2)
                add = e == half - 1
                got = sent if add else slot - LAG * ((n - 2 - e) // 2)
            elif e:
                sent, got, add = slot - LAG * ((n - 1 - e) // 2), slot - LAG * ((e - 1) // 2), True
            else:
                continue
            sent = sent if 0 <= sent < count else None
            got = got if 0 <= got < count else None
            plan.append((e, sent, got, add))
        return plan

    def whole(self, value, sync):
        stream = Stream(self, 1)
        stream.feed(value)
        for slot in range(stream.slots()):
            for kind in range(2):
                stream.start(kind, slot)
                got = stream.waiting(kind, slot)
                if got:
                    stream.take(kind, slot, sync(*got))
        return stream.result(0)


class Stream:
    def __init__(self, line, count):
        self.line = line
        self.count = count
        self.chunks = []
        self.final = {}
        self.flying = {}
        self.turn = 0

    def slots(self):
        return self.count + LAG * ((self.line.count - 2) // 2)

    def feed(self, chunk):
        self.chunks.append(chunk)

    def edge(self):
        return (self.line.depth == 0).astype(jnp.int32).reshape(1)

    def pair(self, k):
        return self.chunks[k], self.final.get(k, self.chunks[k])

    def result(self, k):
        held, got = self.pair(k)
        return held if held is got else jnp.where(self.line.depth == 0, got, held)

    def tiles(self, start, stop, per_row):
        held, got = zip(*[self.pair(k) for k in range(start, stop)])
        return tiled(self.edge(), held, got, per_row)

    def start(self, kind, slot):
        plan = self.line.swaps(kind, slot, self.count)
        sends = [(e, sent) for e, sent, _, _ in plan if sent is not None]
        if not sends:
            return
        value = self.chunks[sends[0][1]]
        for e, sent in sends[1:]:
            value = jnp.where(self.line.depth == e, self.chunks[sent], value)
        got = self.line.exchange(value, kind)
        self.flying[kind, slot] = got, plan

    def waiting(self, kind, slot):
        flight = self.flying.get((kind, slot))
        return () if flight is None else flight[:1]

    def take(self, kind, slot, values):
        short = self.line.half == 2
        for got in values:
            for e, _, k, add in self.flying[kind, slot][1]:
                if k is None:
                    continue
                held = self.chunks[k]
                if not add and short:
                    self.final[k] = got
                    continue
                new = add_low(held, got) if add else got
                if not short:
                    new = jnp.where(self.line.depth == e, new, held)
                self.chunks[k] = new

    def begin(self):
        self.start(0, 0)
        self.start(0, 1)

    def sync(self, *values):
        n = self.turn
        self.turn += 1
        outer = self.waiting(0, n)
        held = lax.optimization_barrier(outer + tuple(values))
        self.take(0, n, held[: len(outer)])
        self.start(1, n)
        self.take(1, n - 1, self.waiting(1, n - 1))
        self.start(0, n + 2)
        return held[len(outer) :]

    def finish(self):
        while self.turn < self.slots():
            self.sync()


def norm_stats(values):
    center = values - jnp.mean(values, axis=-1, keepdims=True)
    spread = jnp.mean(center * center, axis=-1, keepdims=True)
    inverse = lax.rsqrt(spread + 1e-05)
    return (center * inverse, inverse)


def norm_back(grad_out, normed_raw, inverse, gain):
    scaled = grad_out * gain
    grad_in = inverse * (
        scaled
        - jnp.mean(scaled, axis=-1, keepdims=True)
        - normed_raw * jnp.mean(scaled * normed_raw, axis=-1, keepdims=True)
    )
    return (grad_in, jnp.sum(grad_out * normed_raw, axis=0), jnp.sum(grad_out, axis=0))


def dot(a, b, dims):
    return lax.dot_general(a, b, (dims, ((), ())), preferred_element_type=f32)


def window_probs(query, keys, pos, valid):
    scores = dot(query, keys, ((1,), (1,))) * HEAD_DIM**-0.5
    own = lax.broadcasted_iota(jnp.int32, scores.shape, 0) + MAX_DOCUMENT
    key = lax.broadcasted_iota(jnp.int32, scores.shape, 1)
    back = own - key
    allowed = ((back >= 0) & (back <= pos) & (valid == 1)) | (back == 0)
    scores = jnp.where(allowed, scores, -1e30)
    exps = jnp.exp(scores - jnp.max(scores, axis=-1, keepdims=True))
    return exps * (1.0 / jnp.sum(exps, axis=-1, keepdims=True))


def attend_kernel(q_ref, k_ref, v_ref, pos_ref, valid_ref, out_ref):
    start = pl.multiple_of(pl.program_id(1) * QUERY_BLOCK, QUERY_BLOCK)
    window = pl.ds(start, WINDOW)
    probs = window_probs(q_ref[...], k_ref[window, :], pos_ref[...], valid_ref[0])
    out_ref[...] = dot(probs.astype(bf16), v_ref[window, :], ((1,), (0,))).astype(bf16)


def attend_back_kernel(q_ref, k_ref, v_ref, do_ref, pos_ref, valid_ref, dq_ref, dk_ref, dv_ref):
    start = pl.multiple_of(pl.program_id(1) * QUERY_BLOCK, QUERY_BLOCK)
    window = pl.ds(start, WINDOW)

    @pl.when(pl.program_id(1) == 0)
    def _():
        dk_ref[...] = jnp.zeros_like(dk_ref)
        dv_ref[...] = jnp.zeros_like(dv_ref)

    query, keys, out = q_ref[...], k_ref[window, :], do_ref[...]
    probs = window_probs(query, keys, pos_ref[...], valid_ref[0])
    dprob = dot(out, v_ref[window, :], ((1,), (1,)))
    dscore = probs * (dprob - jnp.sum(probs * dprob, axis=-1, keepdims=True))
    dscore = dscore.astype(bf16)
    dq_ref[...] = (dot(dscore, keys, ((1,), (0,))) * HEAD_DIM**-0.5).astype(bf16)
    dk_ref[window, :] += dot(dscore, query, ((0,), (0,))) * HEAD_DIM**-0.5
    dv_ref[window, :] += dot(probs.astype(bf16), out, ((0,), (0,)))


def attend_specs(rows, heads):
    block = pl.BlockSpec((QUERY_BLOCK, HEAD_DIM), lambda h, i: (i, h))
    keys = pl.BlockSpec((rows + MAX_DOCUMENT, HEAD_DIM), lambda h, i: (0, h))
    vals = pl.BlockSpec((rows + MAX_DOCUMENT, HEAD_DIM), lambda h, i: (0, h + heads))
    pos = pl.BlockSpec((QUERY_BLOCK, 1), lambda h, i: (i, 0))
    valid = pl.BlockSpec((1, 1, WINDOW), lambda h, i: (i, 0, 0))
    return block, keys, vals, pos, valid


def attend(query, keys_vals, pos, valid):
    rows, width = query.shape
    heads = width // HEAD_DIM
    block, keys_spec, vals_spec, pos_spec, valid_spec = attend_specs(rows, heads)
    return pl.pallas_call(
        attend_kernel,
        grid=(heads, rows // QUERY_BLOCK),
        in_specs=[block, keys_spec, vals_spec, pos_spec, valid_spec],
        out_specs=block,
        out_shape=jax.ShapeDtypeStruct((rows, width), bf16),
        compiler_params=pltpu.CompilerParams(vmem_limit_bytes=16 << 20),
        name="attend",
    )(query, keys_vals, keys_vals, pos, valid)


def attend_back(query, keys_vals, out, pos, valid):
    rows, width = query.shape
    heads = width // HEAD_DIM
    block, keys_spec, vals_spec, pos_spec, valid_spec = attend_specs(rows, heads)
    wide_shape = jax.ShapeDtypeStruct((rows + MAX_DOCUMENT, width), f32)
    return pl.pallas_call(
        attend_back_kernel,
        grid=(heads, rows // QUERY_BLOCK),
        in_specs=[block, keys_spec, vals_spec, block, pos_spec, valid_spec],
        out_specs=[block, keys_spec, keys_spec],
        out_shape=[jax.ShapeDtypeStruct((rows, width), bf16), wide_shape, wide_shape],
        compiler_params=pltpu.CompilerParams(vmem_limit_bytes=24 << 20),
        name="attend_back",
    )(query, keys_vals, keys_vals, out, pos, valid)


def tile_kernel(edge_ref, *refs):
    *parts, out_ref = refs
    half = len(parts) // 2
    for at in range(half):
        for edge, part in enumerate((parts[at], parts[at + half])):

            @pl.when((pl.program_id(0) == at) & (edge_ref[0] == edge))
            def _(part=part):
                out_ref[...] = part[...].astype(f32)


def tiled(edge, held, got, per_row):
    rows, cols = held[0].shape
    parts = list(held) + list(got)
    whole = pl.BlockSpec((rows, cols), lambda i: (0, 0), pipeline_mode=pl.Buffered(1))
    return pl.pallas_call(
        tile_kernel,
        grid=(len(held),),
        in_specs=[pl.BlockSpec(memory_space=pltpu.SMEM)] + [whole for _ in parts],
        out_specs=pl.BlockSpec((rows, cols), lambda i: (i // per_row, i % per_row)),
        out_shape=jax.ShapeDtypeStruct((len(held) // per_row * rows, per_row * cols), f32),
        compiler_params=pltpu.CompilerParams(vmem_limit_bytes=16 << 20),
        name="tiled",
    )(edge, *parts)


def on_device(
    layer_entry_input,
    ln1_gain,
    ln1_bias,
    w_qkv,
    b_qv,
    w_out,
    b_out,
    ln2_gain,
    ln2_bias,
    w_up,
    b_up,
    w_down,
    b_down,
    document_index,
    positions,
    valid,
    cotangent,
):
    rows, width = layer_entry_input.shape
    local_width = w_qkv.shape[2]
    hidden = w_up.shape[1]
    line = Line()
    start = line.at * rows
    ahead = [(i, i + 1) for i in range(line.count - 1)]
    behind = [(i + 1, i) for i in range(line.count - 1)]
    block_rows = rows // lax.axis_size("narrow")
    block_start = row_block() * block_rows

    def rows_of(value):
        return lax.dynamic_slice_in_dim(value, block_start, block_rows, 0)

    pos = lax.dynamic_slice_in_dim(positions, start, rows, 0).reshape(rows, 1)
    padded_valid = jnp.concatenate([jnp.zeros((MAX_DOCUMENT,), jnp.int32), valid])
    valid_near = lax.dynamic_slice_in_dim(padded_valid, start, rows + MAX_DOCUMENT, 0)
    valid_windows = jnp.stack(
        [valid_near[i : i + WINDOW] for i in range(0, rows, QUERY_BLOCK)]
    ).reshape(rows // QUERY_BLOCK, 1, WINDOW)

    inputs = layer_entry_input.astype(f32)
    raw_one, _ = norm_stats(inputs)
    normed_one = (raw_one * ln1_gain + ln1_bias).astype(bf16)
    w_flat = w_qkv.reshape(width, 3 * local_width)
    mixed = dot(normed_one, w_flat[:, local_width:], ((1,), (0,)))
    bias = jnp.concatenate([jnp.zeros_like(b_qv[1]), b_qv[1]])
    keys_vals = (mixed + bias).astype(bf16)
    halo = lax.ppermute(keys_vals[rows - MAX_DOCUMENT :], "wide", ahead)
    query = (dot(normed_one, w_flat[:, :local_width], ((1,), (0,))) + b_qv[0]).astype(bf16)
    grad_active = dot(cotangent, w_down, ((1,), (1,))).astype(bf16)
    halo, query, grad_active = lax.optimization_barrier((halo, query, grad_active))
    keys_vals = jnp.concatenate([halo, keys_vals])
    attended = attend(query, keys_vals, pos, valid_windows)
    attn_part = dot(attended, w_out, ((1,), (0,))).astype(bf16)
    attn_total = reduce_rows(attn_part).astype(f32)
    inputs_rows = rows_of(layer_entry_input).astype(f32)
    after_attn = inputs_rows + b_out + attn_total
    raw_two, inv_two = norm_stats(after_attn)
    normed_two = gather_rows((raw_two * ln2_gain + ln2_bias).astype(bf16))

    upper = dot(normed_two, w_up, ((1,), (0,))) + b_up
    active, gelu_pull = jax.vjp(jax.nn.gelu, upper)
    active = active.astype(bf16)
    grad_upper = gelu_pull(grad_active.astype(f32))[0].astype(bf16)

    bulk = Stream(line, 12)
    step = width // 4
    places = [(i, j) for i in range(0, hidden, step) for j in range(0, width, hidden)]
    for i, j in places:
        part = dot(active[:, i : i + step], cotangent[:, j : j + hidden], ((0,), (0,)))
        bulk.feed(part.astype(bf16))
    bulk.begin()
    for i in range(4):
        bulk.feed(
            dot(normed_two[:, i * step : (i + 1) * step], grad_upper, ((0,), (0,))).astype(bf16)
        )
    grad_b_up = jnp.sum(grad_upper.astype(f32), axis=0)
    back_part = dot(grad_upper, w_up, ((1,), (1,))).astype(bf16)
    grad_norm_two = reduce_rows(back_part, at_calls(bulk.sync, 1)).astype(f32)
    grad_resid, grad_ln2_gain, grad_ln2_bias = norm_back(grad_norm_two, raw_two, inv_two, ln2_gain)
    grad_out_rows = rows_of(cotangent).astype(f32)
    grad_mid = grad_out_rows + grad_resid
    grad_mid_low = gather_rows(grad_mid.astype(bf16), at_calls(bulk.sync, 0))
    grad_attended = dot(grad_mid_low, w_out, ((1,), (1,))).astype(bf16)
    bulk.feed(
        jnp.concatenate(
            [
                dot(attended, grad_mid_low[:, j : j + hidden], ((0,), (0,))).astype(bf16)
                for j in range(0, width, hidden)
            ]
        ),
    )
    (grad_attended,) = bulk.sync(grad_attended)
    grad_query, grad_keys, grad_vals = attend_back(
        query, keys_vals, grad_attended, pos, valid_windows
    )
    grad_kv = jnp.concatenate([grad_keys, grad_vals], axis=1)
    got = lax.ppermute(grad_kv[:MAX_DOCUMENT].astype(bf16), "wide", behind)
    own = grad_kv[MAX_DOCUMENT:]
    own, active = bulk.sync(own, active)
    mlp_part = dot(active, w_down, ((1,), (0,))).astype(bf16)
    mlp_total = reduce_rows(mlp_part, at_calls(bulk.sync, 1)).astype(f32)
    own, got, mlp_total = bulk.sync(own, got, mlp_total)
    low = rows - MAX_DOCUMENT
    grad_kv = jnp.concatenate([own[:low], own[low:] + got.astype(f32)]).astype(bf16)
    grad_mixed = jnp.concatenate([grad_query, grad_kv], axis=1)
    parts = [
        dot(normed_one[:, i * step : (i + 1) * step], grad_mixed, ((0,), (0,))).astype(bf16)
        for i in range(3)
    ]
    rest = dot(normed_one[:, 3 * step :], grad_mixed, ((0,), (0,))).astype(bf16)
    for i in range(3):
        extra = rest[:, i * local_width : (i + 1) * local_width]
        bulk.feed(jnp.concatenate([parts[i], extra], axis=1))
    grad_b_qv = jnp.sum(grad_mixed.astype(f32), axis=0)
    grad_b_qv = [grad_b_qv[i * local_width : (i + 1) * local_width] for i in (0, 2)]
    back_part = dot(grad_mixed, w_flat, ((1,), (1,))).astype(bf16)
    output = gather_rows((after_attn + b_down + mlp_total).astype(bf16))
    grad_norm_one = reduce_rows(back_part, at_calls(bulk.sync, 0, 2)).astype(f32)
    raw_rows, inv_rows = norm_stats(inputs_rows)
    grad_resid, grad_ln1_gain, grad_ln1_bias = norm_back(
        grad_norm_one, raw_rows, inv_rows, ln1_gain
    )
    grad_input = gather_rows((grad_mid + grad_resid).astype(bf16), at_calls(bulk.sync, 0, 1))

    sums = narrow_total(
        jnp.stack(
            [
                grad_ln2_gain,
                grad_ln2_bias,
                jnp.sum(grad_mid, axis=0),
                jnp.sum(grad_out_rows, axis=0),
                grad_ln1_gain,
                grad_ln1_bias,
            ]
        )
    )
    sums = jnp.concatenate([sums.reshape(-1), grad_b_up] + grad_b_qv)
    sums = line.whole(sums.reshape(-1, 128), bulk.sync).reshape(-1)
    bulk.finish()
    grad_ln2_gain, grad_ln2_bias, grad_b_out, grad_b_down, grad_ln1_gain, grad_ln1_bias = sums[
        : 6 * width
    ].reshape(6, width)
    grad_b_up = sums[6 * width : 6 * width + hidden]
    grad_b_qv = sums[6 * width + hidden :].reshape(2, local_width)

    done = [None] * 8 + [bulk.result(k).astype(f32) for k in range(8, 12)]
    per_row = width // hidden
    grad_w_down = bulk.tiles(0, 4, per_row)
    grad_w_up = bulk.tiles(4, 8, 1)
    grad_w_out = jnp.concatenate(
        [done[8][i * local_width : (i + 1) * local_width] for i in range(per_row)], axis=1
    )
    mixed_done = done[9:12]
    grad_w_qkv = jnp.stack(
        [
            jnp.concatenate(
                [value[:, c * local_width : (c + 1) * local_width] for value in mixed_done]
                + [mixed_done[c][:, 3 * local_width :]]
            )
            for c in range(3)
        ],
        axis=1,
    )
    return (
        output,
        grad_input,
        grad_ln1_gain,
        grad_ln1_bias,
        grad_w_qkv,
        grad_b_qv,
        grad_w_out,
        grad_b_out,
        grad_ln2_gain,
        grad_ln2_bias,
        grad_w_up,
        grad_b_up,
        grad_w_down,
        grad_b_down,
    )


def solution(mesh):
    return jax.shard_map(
        on_device,
        mesh=mesh,
        in_specs=(
            P("wide", None),
            P(),
            P(),
            P(None, None, "narrow"),
            P(None, "narrow"),
            P("narrow", None),
            P(),
            P(),
            P(),
            P(None, "narrow"),
            P("narrow"),
            P("narrow", None),
            P(),
            P(),
            P(),
            P(),
            P("wide", None),
        ),
        out_specs=(
            P("wide", None),
            P("wide", None),
            P(),
            P(),
            P(None, None, "narrow"),
            P(None, "narrow"),
            P("narrow", None),
            P(),
            P(),
            P(),
            P(None, "narrow"),
            P("narrow"),
            P("narrow", None),
            P(),
        ),
        check_vma=False,
    )
```

```python
import jax
import jax.numpy as jnp
from jax import lax
from jax.experimental import pallas as pl
from jax.experimental.pallas import tpu as pltpu
from jax.sharding import PartitionSpec as P


HEAD_DIM = 128
MAX_DOCUMENT = 768
QUERY_BLOCK = 256
WINDOW = MAX_DOCUMENT + QUERY_BLOCK
LAG = 3
f32 = jnp.float32
bf16 = jnp.bfloat16


def add_low(a, b):
    return (a.astype(f32) + b.astype(f32)).astype(a.dtype)


def pick(value, index, dim):
    return lax.dynamic_index_in_dim(value, index, dim, keepdims=False)


def narrow_bit(bit):
    return (lax.axis_index("narrow") >> bit) & 1


def narrow_bits():
    return lax.axis_size("narrow").bit_length() - 1


def swap(value, bit):
    count = lax.axis_size("narrow")
    return lax.ppermute(value, "narrow", [(i, i ^ (1 << bit)) for i in range(count)])


def bit_orders():
    later = list(range(1, narrow_bits()))
    return later, later[::-1]


def row_block():
    bits = narrow_bits()
    return sum(narrow_bit(b) << (bits - 1 - b) for b in range(bits))


def as_is(*values):
    return values


def at_calls(sync, *which):
    count = iter(range(99))
    return lambda *values: sync(*values) if next(count) in which else values


def reduce_rows(value, sync=as_is):
    bits = narrow_bits()
    rows, width = value.shape
    half_rows = rows >> (bits + 1)
    value = value.reshape(2, rows // 2, width)
    mine = narrow_bit(0)
    got = swap(pick(value, 1 - mine, 0), 0)
    value = add_low(pick(value, mine, 0), got)
    (value,) = sync(value)
    value = value.reshape((2,) * (bits - 1) + (2, half_rows, width))
    orders = bit_orders()
    parts = [lax.index_in_dim(value, half, bits - 1, keepdims=False) for half in range(2)]
    left = [list(range(1, bits)) for _ in orders]
    for step in range(bits - 1):
        for half, order in enumerate(orders):
            b = order[step]
            at = left[half].index(b)
            mine = narrow_bit(b)
            piece = parts[half]
            got = swap(pick(piece, 1 - mine, at), b)
            parts[half] = add_low(pick(piece, mine, at), got)
            left[half].pop(at)
        parts = list(sync(*parts))
    return jnp.concatenate(parts, axis=0)


def pair(value, other, bit, dim):
    return jnp.where(
        narrow_bit(bit) == 0, jnp.stack([value, other], axis=dim), jnp.stack([other, value], axis=dim)
    )


def gather_rows(block, sync=as_is):
    bits = narrow_bits()
    rows, width = block.shape
    orders = [order[::-1] for order in bit_orders()]
    parts = [block[half * (rows // 2) : (half + 1) * (rows // 2)] for half in range(2)]
    for step in range(bits - 1):
        for half, order in enumerate(orders):
            b = order[step]
            at = sum(1 for x in order[:step] if x < b)
            got = swap(parts[half], b)
            parts[half] = pair(parts[half], got, b, at)
        parts = list(sync(*parts))
    value = jnp.stack(parts, axis=bits - 1)
    got = swap(value, 0)
    value = pair(value, got, 0, 0)
    return value.reshape(rows << bits, width)


def narrow_total(value):
    for b in range(narrow_bits()):
        value = value + swap(value, b)
    return value


class Line:
    def __init__(self):
        self.count = lax.axis_size("wide")
        self.half = self.count // 2
        self.at = lax.axis_index("wide")
        self.depth = jnp.minimum(self.at, self.count - 1 - self.at)

    def exchange(self, value, kind):
        pairs = [(i, i + 1) for i in range(kind, self.count - 1, 2)]
        return lax.ppermute(value, "wide", pairs + [(b, a) for a, b in pairs])

    def swaps(self, kind, slot, count):
        n, half = self.count, self.half
        plan = []
        for e in range(half):
            if e % 2 == kind:
                sent = slot - LAG * (e // 2)
                add = e == half - 1
                got = sent if add else slot - LAG * ((n - 2 - e) // 2)
            elif e:
                sent, got, add = slot - LAG * ((n - 1 - e) // 2), slot - LAG * ((e - 1) // 2), True
            else:
                continue
            sent = sent if 0 <= sent < count else None
            got = got if 0 <= got < count else None
            plan.append((e, sent, got, add))
        return plan

    def whole(self, value, sync):
        stream = Stream(self, 1)
        stream.feed(value)
        for slot in range(stream.slots()):
            for kind in range(2):
                stream.start(kind, slot)
                got = stream.waiting(kind, slot)
                if got:
                    stream.take(kind, slot, sync(*got))
        return stream.result(0)


class Stream:
    def __init__(self, line, count):
        self.line = line
        self.count = count
        self.chunks = []
        self.final = {}
        self.flying = {}
        self.turn = 0

    def slots(self):
        return self.count + LAG * ((self.line.count - 2) // 2)

    def feed(self, chunk):
        self.chunks.append(chunk)

    def edge(self):
        return (self.line.depth == 0).astype(jnp.int32).reshape(1)

    def pair(self, k):
        return self.chunks[k], self.final.get(k, self.chunks[k])

    def result(self, k):
        held, got = self.pair(k)
        return held if held is got else jnp.where(self.line.depth == 0, got, held)

    def tiles(self, which, count, per_row):
        held, got = zip(*[self.pair(k) for k in which])
        return tiled(self.edge(), held, got, count, per_row)

    def last_tile(self, k, others):
        return tiled(self.edge(), *[[value] for value in self.pair(k)], 4, 1, others)

    def start(self, kind, slot):
        plan = self.line.swaps(kind, slot, self.count)
        sends = [(e, sent) for e, sent, _, _ in plan if sent is not None]
        if not sends:
            return
        value = self.chunks[sends[0][1]]
        for e, sent in sends[1:]:
            value = jnp.where(self.line.depth == e, self.chunks[sent], value)
        got = self.line.exchange(value, kind)
        self.flying[kind, slot] = got, plan

    def waiting(self, kind, slot):
        flight = self.flying.get((kind, slot))
        return () if flight is None else flight[:1]

    def take(self, kind, slot, values):
        short = self.line.half == 2
        for got in values:
            for e, _, k, add in self.flying[kind, slot][1]:
                if k is None:
                    continue
                held = self.chunks[k]
                if not add and short:
                    self.final[k] = got
                    continue
                new = add_low(held, got) if add else got
                if not short:
                    new = jnp.where(self.line.depth == e, new, held)
                self.chunks[k] = new

    def begin(self):
        self.start(0, 0)
        self.start(0, 1)

    def sync(self, *values):
        n = self.turn
        self.turn += 1
        outer = self.waiting(0, n)
        held = lax.optimization_barrier(outer + tuple(values))
        self.take(0, n, held[: len(outer)])
        self.start(1, n)
        self.take(1, n - 1, self.waiting(1, n - 1))
        self.start(0, n + 2)
        return held[len(outer) :]

    def finish(self):
        while self.turn < self.slots():
            self.sync()


def norm_stats(values):
    center = values - jnp.mean(values, axis=-1, keepdims=True)
    spread = jnp.mean(center * center, axis=-1, keepdims=True)
    inverse = lax.rsqrt(spread + 1e-05)
    return (center * inverse, inverse)


def norm_back(grad_out, normed_raw, inverse, gain):
    scaled = grad_out * gain
    grad_in = inverse * (
        scaled
        - jnp.mean(scaled, axis=-1, keepdims=True)
        - normed_raw * jnp.mean(scaled * normed_raw, axis=-1, keepdims=True)
    )
    return (grad_in, jnp.sum(grad_out * normed_raw, axis=0), jnp.sum(grad_out, axis=0))


def dot(a, b, dims):
    return lax.dot_general(a, b, (dims, ((), ())), preferred_element_type=f32)


def window_probs(query, keys, pos, valid):
    scores = dot(query, keys, ((1,), (1,))) * HEAD_DIM**-0.5
    own = lax.broadcasted_iota(jnp.int32, scores.shape, 0) + MAX_DOCUMENT
    key = lax.broadcasted_iota(jnp.int32, scores.shape, 1)
    back = own - key
    allowed = ((back >= 0) & (back <= pos) & (valid == 1)) | (back == 0)
    scores = jnp.where(allowed, scores, -1e30)
    exps = jnp.exp(scores - jnp.max(scores, axis=-1, keepdims=True))
    return exps * (1.0 / jnp.sum(exps, axis=-1, keepdims=True))


def attend_kernel(q_ref, k_ref, v_ref, pos_ref, valid_ref, out_ref):
    start = pl.multiple_of(pl.program_id(1) * QUERY_BLOCK, QUERY_BLOCK)
    window = pl.ds(start, WINDOW)
    probs = window_probs(q_ref[...], k_ref[window, :], pos_ref[...], valid_ref[0])
    out_ref[...] = dot(probs.astype(bf16), v_ref[window, :], ((1,), (0,))).astype(bf16)


def attend_back_kernel(q_ref, k_ref, v_ref, do_ref, pos_ref, valid_ref, dq_ref, dk_ref, dv_ref):
    start = pl.multiple_of(pl.program_id(1) * QUERY_BLOCK, QUERY_BLOCK)
    window = pl.ds(start, WINDOW)

    @pl.when(pl.program_id(1) == 0)
    def _():
        dk_ref[...] = jnp.zeros_like(dk_ref)
        dv_ref[...] = jnp.zeros_like(dv_ref)

    query, keys, out = q_ref[...], k_ref[window, :], do_ref[...]
    probs = window_probs(query, keys, pos_ref[...], valid_ref[0])
    dprob = dot(out, v_ref[window, :], ((1,), (1,)))
    dscore = probs * (dprob - jnp.sum(probs * dprob, axis=-1, keepdims=True))
    dscore = dscore.astype(bf16)
    dq_ref[...] = (dot(dscore, keys, ((1,), (0,))) * HEAD_DIM**-0.5).astype(bf16)
    dk_ref[window, :] += dot(dscore, query, ((0,), (0,))) * HEAD_DIM**-0.5
    dv_ref[window, :] += dot(probs.astype(bf16), out, ((0,), (0,)))


def attend_specs(rows, heads):
    block = pl.BlockSpec((QUERY_BLOCK, HEAD_DIM), lambda h, i: (i, h))
    keys = pl.BlockSpec((rows + MAX_DOCUMENT, HEAD_DIM), lambda h, i: (0, h))
    vals = pl.BlockSpec((rows + MAX_DOCUMENT, HEAD_DIM), lambda h, i: (0, h + heads))
    pos = pl.BlockSpec((QUERY_BLOCK, 1), lambda h, i: (i, 0))
    valid = pl.BlockSpec((1, 1, WINDOW), lambda h, i: (i, 0, 0))
    return block, keys, vals, pos, valid


def attend(query, keys_vals, pos, valid):
    rows, width = query.shape
    heads = width // HEAD_DIM
    block, keys_spec, vals_spec, pos_spec, valid_spec = attend_specs(rows, heads)
    return pl.pallas_call(
        attend_kernel,
        grid=(heads, rows // QUERY_BLOCK),
        in_specs=[block, keys_spec, vals_spec, pos_spec, valid_spec],
        out_specs=block,
        out_shape=jax.ShapeDtypeStruct((rows, width), bf16),
        compiler_params=pltpu.CompilerParams(vmem_limit_bytes=16 << 20),
        name="attend",
    )(query, keys_vals, keys_vals, pos, valid)


def attend_back(query, keys_vals, out, pos, valid):
    rows, width = query.shape
    heads = width // HEAD_DIM
    block, keys_spec, vals_spec, pos_spec, valid_spec = attend_specs(rows, heads)
    wide_shape = jax.ShapeDtypeStruct((rows + MAX_DOCUMENT, width), f32)
    return pl.pallas_call(
        attend_back_kernel,
        grid=(heads, rows // QUERY_BLOCK),
        in_specs=[block, keys_spec, vals_spec, block, pos_spec, valid_spec],
        out_specs=[block, keys_spec, keys_spec],
        out_shape=[jax.ShapeDtypeStruct((rows, width), bf16), wide_shape, wide_shape],
        compiler_params=pltpu.CompilerParams(vmem_limit_bytes=24 << 20),
        name="attend_back",
    )(query, keys_vals, keys_vals, out, pos, valid)


def tile_kernel(edge_ref, *refs):
    *parts, out_ref = refs
    half = len(parts) // 2
    for at in range(half):
        for edge, part in enumerate((parts[at], parts[at + half])):

            @pl.when((pl.program_id(0) == at) & (edge_ref[0] == edge))
            def _(part=part):
                out_ref[...] = part[...].astype(f32)


def tiled(edge, held, got, count, per_row, others=None):
    rows, cols = held[0].shape
    parts = list(held) + list(got)
    first = 0 if others is None else count - len(held)
    whole = pl.BlockSpec((rows, cols), lambda i: (0, 0), pipeline_mode=pl.Buffered(1))
    specs = [pl.BlockSpec(memory_space=pltpu.SMEM)] + [whole for _ in parts]
    args = [edge] + parts
    kernel = tile_kernel
    if others is not None:
        specs.append(pl.BlockSpec(memory_space=pl.ANY))
        args.append(others)

        def kernel(*refs):
            tile_kernel(*refs[:-2], refs[-1])

    return pl.pallas_call(
        kernel,
        grid=(len(held),),
        in_specs=specs,
        out_specs=pl.BlockSpec(
            (rows, cols), lambda i: ((i + first) // per_row, (i + first) % per_row)
        ),
        out_shape=jax.ShapeDtypeStruct((count // per_row * rows, per_row * cols), f32),
        input_output_aliases={} if others is None else {len(args) - 1: 0},
        compiler_params=pltpu.CompilerParams(vmem_limit_bytes=16 << 20),
        name="tiled",
    )(*args)


def on_device(
    layer_entry_input,
    ln1_gain,
    ln1_bias,
    w_qkv,
    b_qv,
    w_out,
    b_out,
    ln2_gain,
    ln2_bias,
    w_up,
    b_up,
    w_down,
    b_down,
    document_index,
    positions,
    valid,
    cotangent,
):
    rows, width = layer_entry_input.shape
    local_width = w_qkv.shape[2]
    hidden = w_up.shape[1]
    line = Line()
    start = line.at * rows
    ahead = [(i, i + 1) for i in range(line.count - 1)]
    behind = [(i + 1, i) for i in range(line.count - 1)]
    block_rows = rows // lax.axis_size("narrow")
    block_start = row_block() * block_rows

    def rows_of(value):
        return lax.dynamic_slice_in_dim(value, block_start, block_rows, 0)

    pos = lax.dynamic_slice_in_dim(positions, start, rows, 0).reshape(rows, 1)
    padded_valid = jnp.concatenate([jnp.zeros((MAX_DOCUMENT,), jnp.int32), valid])
    valid_near = lax.dynamic_slice_in_dim(padded_valid, start, rows + MAX_DOCUMENT, 0)
    valid_windows = jnp.stack(
        [valid_near[i : i + WINDOW] for i in range(0, rows, QUERY_BLOCK)]
    ).reshape(rows // QUERY_BLOCK, 1, WINDOW)

    inputs = layer_entry_input.astype(f32)
    raw_one, _ = norm_stats(inputs)
    normed_one = (raw_one * ln1_gain + ln1_bias).astype(bf16)
    w_flat = w_qkv.reshape(width, 3 * local_width)
    mixed = dot(normed_one, w_flat[:, local_width:], ((1,), (0,)))
    bias = jnp.concatenate([jnp.zeros_like(b_qv[1]), b_qv[1]])
    keys_vals = (mixed + bias).astype(bf16)
    halo = lax.ppermute(keys_vals[rows - MAX_DOCUMENT :], "wide", ahead)
    query = (dot(normed_one, w_flat[:, :local_width], ((1,), (0,))) + b_qv[0]).astype(bf16)
    grad_active = dot(cotangent, w_down, ((1,), (1,))).astype(bf16)
    halo, query, grad_active = lax.optimization_barrier((halo, query, grad_active))
    keys_vals = jnp.concatenate([halo, keys_vals])
    attended = attend(query, keys_vals, pos, valid_windows)
    attn_part = dot(attended, w_out, ((1,), (0,))).astype(bf16)
    attn_total = reduce_rows(attn_part).astype(f32)
    inputs_rows = rows_of(layer_entry_input).astype(f32)
    after_attn = inputs_rows + b_out + attn_total
    raw_two, inv_two = norm_stats(after_attn)
    normed_two = gather_rows((raw_two * ln2_gain + ln2_bias).astype(bf16))

    upper = dot(normed_two, w_up, ((1,), (0,))) + b_up
    active, gelu_pull = jax.vjp(jax.nn.gelu, upper)
    active = active.astype(bf16)
    grad_upper = gelu_pull(grad_active.astype(f32))[0].astype(bf16)

    bulk = Stream(line, 12)
    step = width // 4
    places = [(i, j) for i in range(0, hidden, step) for j in range(0, width, hidden)]
    for i, j in places:
        part = dot(active[:, i : i + step], cotangent[:, j : j + hidden], ((0,), (0,)))
        bulk.feed(part.astype(bf16))
    bulk.begin()
    ups = [
        dot(normed_two[:, i * step : (i + 1) * step], grad_upper, ((0,), (0,))).astype(bf16)
        for i in range(4)
    ]
    for part in ups[:3]:
        bulk.feed(part)
    grad_b_up = jnp.sum(grad_upper.astype(f32), axis=0)
    back_part = dot(grad_upper, w_up, ((1,), (1,))).astype(bf16)
    grad_norm_two = reduce_rows(back_part, at_calls(bulk.sync, 0, 2)).astype(f32)
    grad_resid, grad_ln2_gain, grad_ln2_bias = norm_back(grad_norm_two, raw_two, inv_two, ln2_gain)
    grad_out_rows = rows_of(cotangent).astype(f32)
    grad_mid = grad_out_rows + grad_resid
    grad_mid_low = gather_rows(grad_mid.astype(bf16), at_calls(bulk.sync, 1))
    grad_attended = dot(grad_mid_low, w_out, ((1,), (1,))).astype(bf16)
    bulk.feed(
        jnp.concatenate(
            [
                dot(attended, grad_mid_low[:, j : j + hidden], ((0,), (0,))).astype(bf16)
                for j in range(0, width, hidden)
            ]
        ),
    )
    grad_query, grad_keys, grad_vals = attend_back(
        query, keys_vals, grad_attended, pos, valid_windows
    )
    grad_kv = jnp.concatenate([grad_keys, grad_vals], axis=1)
    got = lax.ppermute(grad_kv[:MAX_DOCUMENT].astype(bf16), "wide", behind)
    own = grad_kv[MAX_DOCUMENT:]
    own, active = bulk.sync(own, active)
    mlp_part = dot(active, w_down, ((1,), (0,))).astype(bf16)
    mlp_total = reduce_rows(mlp_part, at_calls(bulk.sync, 0)).astype(f32)
    own, got, mlp_total = bulk.sync(own, got, mlp_total)
    low = rows - MAX_DOCUMENT
    grad_kv = jnp.concatenate([own[:low], own[low:] + got.astype(f32)]).astype(bf16)
    grad_mixed = jnp.concatenate([grad_query, grad_kv], axis=1)
    parts = [
        dot(normed_one[:, i * step : (i + 1) * step], grad_mixed, ((0,), (0,))).astype(bf16)
        for i in range(3)
    ]
    rest = dot(normed_one[:, 3 * step :], grad_mixed, ((0,), (0,))).astype(bf16)
    for i in range(3):
        extra = rest[:, i * local_width : (i + 1) * local_width]
        bulk.feed(jnp.concatenate([parts[i], extra], axis=1))
    bulk.feed(ups[3])
    grad_b_qv = jnp.sum(grad_mixed.astype(f32), axis=0)
    grad_b_qv = [grad_b_qv[i * local_width : (i + 1) * local_width] for i in (0, 2)]
    back_part = dot(grad_mixed, w_flat, ((1,), (1,))).astype(bf16)
    output = gather_rows((after_attn + b_down + mlp_total).astype(bf16))
    grad_norm_one = reduce_rows(back_part, at_calls(bulk.sync, 0, 2)).astype(f32)
    raw_rows, inv_rows = norm_stats(inputs_rows)
    grad_resid, grad_ln1_gain, grad_ln1_bias = norm_back(
        grad_norm_one, raw_rows, inv_rows, ln1_gain
    )
    grad_input = gather_rows((grad_mid + grad_resid).astype(bf16), at_calls(bulk.sync, 0, 1))

    sums = narrow_total(
        jnp.stack(
            [
                grad_ln2_gain,
                grad_ln2_bias,
                jnp.sum(grad_mid, axis=0),
                jnp.sum(grad_out_rows, axis=0),
                grad_ln1_gain,
                grad_ln1_bias,
            ]
        )
    )
    sums = jnp.concatenate([sums.reshape(-1), grad_b_up] + grad_b_qv)
    sums = line.whole(sums.reshape(-1, 128), bulk.sync).reshape(-1)
    bulk.finish()
    grad_ln2_gain, grad_ln2_bias, grad_b_out, grad_b_down, grad_ln1_gain, grad_ln1_bias = sums[
        : 6 * width
    ].reshape(6, width)
    grad_b_up = sums[6 * width : 6 * width + hidden]
    grad_b_qv = sums[6 * width + hidden :].reshape(2, local_width)

    done = [bulk.result(k).astype(f32) for k in range(7, 11)]
    per_row = width // hidden
    grad_w_down = bulk.tiles(range(4), 4, per_row)
    grad_w_up = bulk.last_tile(11, bulk.tiles(range(4, 7), 4, 1))
    grad_w_out = jnp.concatenate(
        [done[0][i * local_width : (i + 1) * local_width] for i in range(per_row)], axis=1
    )
    mixed_done = done[1:4]
    grad_w_qkv = jnp.stack(
        [
            jnp.concatenate(
                [value[:, c * local_width : (c + 1) * local_width] for value in mixed_done]
                + [mixed_done[c][:, 3 * local_width :]]
            )
            for c in range(3)
        ],
        axis=1,
    )
    return (
        output,
        grad_input,
        grad_ln1_gain,
        grad_ln1_bias,
        grad_w_qkv,
        grad_b_qv,
        grad_w_out,
        grad_b_out,
        grad_ln2_gain,
        grad_ln2_bias,
        grad_w_up,
        grad_b_up,
        grad_w_down,
        grad_b_down,
    )


def solution(mesh):
    return jax.shard_map(
        on_device,
        mesh=mesh,
        in_specs=(
            P("wide", None),
            P(),
            P(),
            P(None, None, "narrow"),
            P(None, "narrow"),
            P("narrow", None),
            P(),
            P(),
            P(),
            P(None, "narrow"),
            P("narrow"),
            P("narrow", None),
            P(),
            P(),
            P(),
            P(),
            P("wide", None),
        ),
        out_specs=(
            P("wide", None),
            P("wide", None),
            P(),
            P(),
            P(None, None, "narrow"),
            P(None, "narrow"),
            P("narrow", None),
            P(),
            P(),
            P(),
            P(None, "narrow"),
            P("narrow"),
            P("narrow", None),
            P(),
        ),
        check_vma=False,
    )
```

```python
import jax
import jax.numpy as jnp
from jax import lax
from jax.experimental import pallas as pl
from jax.experimental.pallas import tpu as pltpu
from jax.sharding import PartitionSpec as P


HEAD_DIM = 128
MAX_DOCUMENT = 768
QUERY_BLOCK = 256
WINDOW = MAX_DOCUMENT + QUERY_BLOCK
LAG = 3
f32 = jnp.float32
bf16 = jnp.bfloat16


def add_low(a, b):
    return (a.astype(f32) + b.astype(f32)).astype(a.dtype)


def pick(value, index, dim):
    return lax.dynamic_index_in_dim(value, index, dim, keepdims=False)


def narrow_bit(bit):
    return (lax.axis_index("narrow") >> bit) & 1


def narrow_bits():
    return lax.axis_size("narrow").bit_length() - 1


def swap(value, bit):
    count = lax.axis_size("narrow")
    return lax.ppermute(value, "narrow", [(i, i ^ (1 << bit)) for i in range(count)])


def bit_orders():
    later = list(range(1, narrow_bits()))
    return later, later[::-1]


def row_block():
    bits = narrow_bits()
    return sum(narrow_bit(b) << (bits - 1 - b) for b in range(bits))


def as_is(*values):
    return values


def at_calls(sync, *which):
    count = iter(range(99))
    return lambda *values: sync(*values) if next(count) in which else values


def reduce_rows(value, sync=as_is):
    bits = narrow_bits()
    rows, width = value.shape
    half_rows = rows >> (bits + 1)
    value = value.reshape(2, rows // 2, width)
    mine = narrow_bit(0)
    got = swap(pick(value, 1 - mine, 0), 0)
    value = add_low(pick(value, mine, 0), got)
    (value,) = sync(value)
    value = value.reshape((2,) * (bits - 1) + (2, half_rows, width))
    orders = bit_orders()
    parts = [lax.index_in_dim(value, half, bits - 1, keepdims=False) for half in range(2)]
    left = [list(range(1, bits)) for _ in orders]
    for step in range(bits - 1):
        for half, order in enumerate(orders):
            b = order[step]
            at = left[half].index(b)
            mine = narrow_bit(b)
            piece = parts[half]
            got = swap(pick(piece, 1 - mine, at), b)
            parts[half] = add_low(pick(piece, mine, at), got)
            left[half].pop(at)
        parts = list(sync(*parts))
    return jnp.concatenate(parts, axis=0)


def pair(value, other, bit, dim):
    return jnp.where(
        narrow_bit(bit) == 0, jnp.stack([value, other], axis=dim), jnp.stack([other, value], axis=dim)
    )


def gather_rows(block, sync=as_is):
    bits = narrow_bits()
    rows, width = block.shape
    orders = [order[::-1] for order in bit_orders()]
    parts = [block[half * (rows // 2) : (half + 1) * (rows // 2)] for half in range(2)]
    for step in range(bits - 1):
        for half, order in enumerate(orders):
            b = order[step]
            at = sum(1 for x in order[:step] if x < b)
            got = swap(parts[half], b)
            parts[half] = pair(parts[half], got, b, at)
        parts = list(sync(*parts))
    value = jnp.stack(parts, axis=bits - 1)
    got = swap(value, 0)
    value = pair(value, got, 0, 0)
    return value.reshape(rows << bits, width)


def narrow_total(value):
    for b in range(narrow_bits()):
        value = value + swap(value, b)
    return value


class Line:
    def __init__(self):
        self.count = lax.axis_size("wide")
        self.half = self.count // 2
        self.at = lax.axis_index("wide")
        self.depth = jnp.minimum(self.at, self.count - 1 - self.at)

    def exchange(self, value, kind):
        pairs = [(i, i + 1) for i in range(kind, self.count - 1, 2)]
        return lax.ppermute(value, "wide", pairs + [(b, a) for a, b in pairs])

    def swaps(self, kind, slot, count):
        n, half = self.count, self.half
        plan = []
        for e in range(half):
            if e % 2 == kind:
                sent = slot - LAG * (e // 2)
                add = e == half - 1
                got = sent if add else slot - LAG * ((n - 2 - e) // 2)
            elif e:
                sent, got, add = slot - LAG * ((n - 1 - e) // 2), slot - LAG * ((e - 1) // 2), True
            else:
                continue
            sent = sent if 0 <= sent < count else None
            got = got if 0 <= got < count else None
            plan.append((e, sent, got, add))
        return plan

    def whole(self, value, sync):
        stream = Stream(self, 1)
        stream.feed(value)
        for slot in range(stream.slots()):
            for kind in range(2):
                stream.start(kind, slot)
                got = stream.waiting(kind, slot)
                if got:
                    stream.take(kind, slot, sync(*got))
        return stream.result(0)


class Stream:
    def __init__(self, line, count):
        self.line = line
        self.count = count
        self.chunks = []
        self.final = {}
        self.flying = {}
        self.turn = 0

    def slots(self):
        return self.count + LAG * ((self.line.count - 2) // 2)

    def feed(self, chunk):
        self.chunks.append(chunk)

    def edge(self):
        return (self.line.depth == 0).astype(jnp.int32).reshape(1)

    def pair(self, k):
        return self.chunks[k], self.final.get(k, self.chunks[k])

    def result(self, k):
        held, got = self.pair(k)
        return held if held is got else jnp.where(self.line.depth == 0, got, held)

    def tiles(self, which, count, per_row):
        held, got = zip(*[self.pair(k) for k in which])
        return tiled(self.edge(), held, got, count, per_row)

    def last_tile(self, k, others):
        return tiled(self.edge(), *[[value] for value in self.pair(k)], 4, 1, others)

    def start(self, kind, slot):
        plan = self.line.swaps(kind, slot, self.count)
        sends = [(e, sent) for e, sent, _, _ in plan if sent is not None]
        if not sends:
            return
        value = self.chunks[sends[0][1]]
        for e, sent in sends[1:]:
            value = jnp.where(self.line.depth == e, self.chunks[sent], value)
        got = self.line.exchange(value, kind)
        self.flying[kind, slot] = got, plan

    def waiting(self, kind, slot):
        flight = self.flying.get((kind, slot))
        return () if flight is None else flight[:1]

    def take(self, kind, slot, values):
        short = self.line.half == 2
        for got in values:
            for e, _, k, add in self.flying[kind, slot][1]:
                if k is None:
                    continue
                held = self.chunks[k]
                if not add and short:
                    self.final[k] = got
                    continue
                new = add_low(held, got) if add else got
                if not short:
                    new = jnp.where(self.line.depth == e, new, held)
                self.chunks[k] = new

    def begin(self):
        self.start(0, 0)
        self.start(0, 1)

    def sync(self, *values):
        n = self.turn
        self.turn += 1
        outer = self.waiting(0, n)
        held = lax.optimization_barrier(outer + tuple(values))
        self.take(0, n, held[: len(outer)])
        self.start(1, n)
        self.take(1, n - 1, self.waiting(1, n - 1))
        self.start(0, n + 2)
        return held[len(outer) :]

    def finish(self):
        while self.turn < self.slots():
            self.sync()


def norm_stats(values):
    center = values - jnp.mean(values, axis=-1, keepdims=True)
    spread = jnp.mean(center * center, axis=-1, keepdims=True)
    inverse = lax.rsqrt(spread + 1e-05)
    return (center * inverse, inverse)


def norm_back(grad_out, normed_raw, inverse, gain):
    scaled = grad_out * gain
    grad_in = inverse * (
        scaled
        - jnp.mean(scaled, axis=-1, keepdims=True)
        - normed_raw * jnp.mean(scaled * normed_raw, axis=-1, keepdims=True)
    )
    return (grad_in, jnp.sum(grad_out * normed_raw, axis=0), jnp.sum(grad_out, axis=0))


def norm_kernel(x_ref, gain_ref, bias_ref, out_ref):
    normed, _ = norm_stats(x_ref[...].astype(f32))
    out_ref[...] = (normed * gain_ref[...] + bias_ref[...]).astype(bf16)


def norm_rows(values, gain, bias):
    rows, width = values.shape
    block = pl.BlockSpec((128, width), lambda i: (i, 0))
    param = pl.BlockSpec((1, width), lambda i: (0, 0))
    return pl.pallas_call(
        norm_kernel,
        grid=(rows // 128,),
        in_specs=[block, param, param],
        out_specs=block,
        out_shape=jax.ShapeDtypeStruct((rows, width), bf16),
        compiler_params=pltpu.CompilerParams(vmem_limit_bytes=16 << 20),
        name="norm_rows",
    )(values, gain.reshape(1, width), bias.reshape(1, width))


def dot(a, b, dims):
    return lax.dot_general(a, b, (dims, ((), ())), preferred_element_type=f32)


def window_probs(query, keys, pos, valid):
    scores = dot(query, keys, ((1,), (1,))) * HEAD_DIM**-0.5
    own = lax.broadcasted_iota(jnp.int32, scores.shape, 0) + MAX_DOCUMENT
    key = lax.broadcasted_iota(jnp.int32, scores.shape, 1)
    back = own - key
    allowed = ((back >= 0) & (back <= pos) & (valid == 1)) | (back == 0)
    scores = jnp.where(allowed, scores, -1e30)
    exps = jnp.exp(scores - jnp.max(scores, axis=-1, keepdims=True))
    return exps * (1.0 / jnp.sum(exps, axis=-1, keepdims=True))


def attend_kernel(q_ref, k_ref, v_ref, pos_ref, valid_ref, out_ref):
    start = pl.multiple_of(pl.program_id(1) * QUERY_BLOCK, QUERY_BLOCK)
    window = pl.ds(start, WINDOW)
    probs = window_probs(q_ref[...], k_ref[window, :], pos_ref[...], valid_ref[0])
    out_ref[...] = dot(probs.astype(bf16), v_ref[window, :], ((1,), (0,))).astype(bf16)


def attend_back_kernel(q_ref, k_ref, v_ref, do_ref, pos_ref, valid_ref, dq_ref, dk_ref, dv_ref):
    start = pl.multiple_of(pl.program_id(1) * QUERY_BLOCK, QUERY_BLOCK)
    window = pl.ds(start, WINDOW)

    @pl.when(pl.program_id(1) == 0)
    def _():
        dk_ref[...] = jnp.zeros_like(dk_ref)
        dv_ref[...] = jnp.zeros_like(dv_ref)

    query, keys, out = q_ref[...], k_ref[window, :], do_ref[...]
    probs = window_probs(query, keys, pos_ref[...], valid_ref[0])
    dprob = dot(out, v_ref[window, :], ((1,), (1,)))
    dscore = probs * (dprob - jnp.sum(probs * dprob, axis=-1, keepdims=True))
    dscore = dscore.astype(bf16)
    dq_ref[...] = (dot(dscore, keys, ((1,), (0,))) * HEAD_DIM**-0.5).astype(bf16)
    dk_ref[window, :] += dot(dscore, query, ((0,), (0,))) * HEAD_DIM**-0.5
    dv_ref[window, :] += dot(probs.astype(bf16), out, ((0,), (0,)))


def attend_specs(rows):
    block = pl.BlockSpec((QUERY_BLOCK, HEAD_DIM), lambda h, i: (i, h))
    joined = (None, rows + MAX_DOCUMENT, HEAD_DIM)
    keys = pl.BlockSpec(joined, lambda h, i: (0, 0, h))
    vals = pl.BlockSpec(joined, lambda h, i: (1, 0, h))
    pos = pl.BlockSpec((QUERY_BLOCK, 1), lambda h, i: (i, 0))
    valid = pl.BlockSpec((1, 1, WINDOW), lambda h, i: (i, 0, 0))
    return block, keys, vals, pos, valid


def attend(query, keys_vals, pos, valid):
    rows, width = query.shape
    heads = width // HEAD_DIM
    block, keys_spec, vals_spec, pos_spec, valid_spec = attend_specs(rows)
    return pl.pallas_call(
        attend_kernel,
        grid=(heads, rows // QUERY_BLOCK),
        in_specs=[block, keys_spec, vals_spec, pos_spec, valid_spec],
        out_specs=block,
        out_shape=jax.ShapeDtypeStruct((rows, width), bf16),
        compiler_params=pltpu.CompilerParams(vmem_limit_bytes=16 << 20),
        name="attend",
    )(query, keys_vals, keys_vals, pos, valid)


def attend_back(query, keys_vals, out, pos, valid):
    rows, width = query.shape
    heads = width // HEAD_DIM
    block, keys_spec, vals_spec, pos_spec, valid_spec = attend_specs(rows)
    wide_shape = jax.ShapeDtypeStruct((rows + MAX_DOCUMENT, width), f32)
    grad_spec = pl.BlockSpec((rows + MAX_DOCUMENT, HEAD_DIM), lambda h, i: (0, h))
    return pl.pallas_call(
        attend_back_kernel,
        grid=(heads, rows // QUERY_BLOCK),
        in_specs=[block, keys_spec, vals_spec, block, pos_spec, valid_spec],
        out_specs=[block, grad_spec, grad_spec],
        out_shape=[jax.ShapeDtypeStruct((rows, width), bf16), wide_shape, wide_shape],
        compiler_params=pltpu.CompilerParams(vmem_limit_bytes=24 << 20),
        name="attend_back",
    )(query, keys_vals, keys_vals, out, pos, valid)


def tile_kernel(edge_ref, *refs):
    *parts, out_ref = refs
    half = len(parts) // 2
    for at in range(half):
        for edge, part in enumerate((parts[at], parts[at + half])):

            @pl.when((pl.program_id(0) == at) & (edge_ref[0] == edge))
            def _(part=part):
                out_ref[...] = part[...].astype(f32)


def tiled(edge, held, got, count, per_row, others=None):
    rows, cols = held[0].shape
    parts = list(held) + list(got)
    first = 0 if others is None else count - len(held)
    whole = pl.BlockSpec((rows, cols), lambda i: (0, 0), pipeline_mode=pl.Buffered(1))
    specs = [pl.BlockSpec(memory_space=pltpu.SMEM)] + [whole for _ in parts]
    args = [edge] + parts
    kernel = tile_kernel
    if others is not None:
        specs.append(pl.BlockSpec(memory_space=pl.ANY))
        args.append(others)

        def kernel(*refs):
            tile_kernel(*refs[:-2], refs[-1])

    return pl.pallas_call(
        kernel,
        grid=(len(held),),
        in_specs=specs,
        out_specs=pl.BlockSpec(
            (rows, cols), lambda i: ((i + first) // per_row, (i + first) % per_row)
        ),
        out_shape=jax.ShapeDtypeStruct((count // per_row * rows, per_row * cols), f32),
        input_output_aliases={} if others is None else {len(args) - 1: 0},
        compiler_params=pltpu.CompilerParams(vmem_limit_bytes=16 << 20),
        name="tiled",
    )(*args)


def on_device(
    layer_entry_input,
    ln1_gain,
    ln1_bias,
    w_qkv,
    b_qv,
    w_out,
    b_out,
    ln2_gain,
    ln2_bias,
    w_up,
    b_up,
    w_down,
    b_down,
    document_index,
    positions,
    valid,
    cotangent,
):
    rows, width = layer_entry_input.shape
    local_width = w_qkv.shape[2]
    hidden = w_up.shape[1]
    line = Line()
    start = line.at * rows
    ahead = [(i, i + 1) for i in range(line.count - 1)]
    behind = [(i + 1, i) for i in range(line.count - 1)]
    block_rows = rows // lax.axis_size("narrow")
    block_start = row_block() * block_rows

    def rows_of(value):
        return lax.dynamic_slice_in_dim(value, block_start, block_rows, 0)

    pos = lax.dynamic_slice_in_dim(positions, start, rows, 0).reshape(rows, 1)
    padded_valid = jnp.concatenate([jnp.zeros((MAX_DOCUMENT,), jnp.int32), valid])
    valid_near = lax.dynamic_slice_in_dim(padded_valid, start, rows + MAX_DOCUMENT, 0)
    valid_windows = jnp.stack(
        [valid_near[i : i + WINDOW] for i in range(0, rows, QUERY_BLOCK)]
    ).reshape(rows // QUERY_BLOCK, 1, WINDOW)

    normed_one = norm_rows(layer_entry_input, ln1_gain, ln1_bias)
    mixed = dot(normed_one, w_qkv[:, 1:], ((1,), (0,))).transpose(1, 0, 2)
    bias = jnp.stack([jnp.zeros_like(b_qv[1]), b_qv[1]])
    keys_vals = (mixed + bias[:, None, :]).astype(bf16)
    halo = lax.ppermute(keys_vals[:, rows - MAX_DOCUMENT :], "wide", ahead)
    query = (dot(normed_one, w_qkv[:, 0], ((1,), (0,))) + b_qv[0]).astype(bf16)
    grad_active = dot(cotangent, w_down, ((1,), (1,))).astype(bf16)
    halo, query, grad_active = lax.optimization_barrier((halo, query, grad_active))
    keys_vals = jnp.concatenate([halo, keys_vals], axis=1)
    attended = attend(query, keys_vals, pos, valid_windows)
    attn_part = dot(attended, w_out, ((1,), (0,))).astype(bf16)
    attn_total = reduce_rows(attn_part).astype(f32)
    inputs_rows = rows_of(layer_entry_input).astype(f32)
    after_attn = inputs_rows + b_out + attn_total
    raw_two, inv_two = norm_stats(after_attn)
    normed_two = gather_rows((raw_two * ln2_gain + ln2_bias).astype(bf16))

    upper = dot(normed_two, w_up, ((1,), (0,))) + b_up
    active, gelu_pull = jax.vjp(jax.nn.gelu, upper)
    active = active.astype(bf16)
    grad_upper = gelu_pull(grad_active.astype(f32))[0].astype(bf16)

    bulk = Stream(line, 12)
    step = width // 4
    places = [(i, j) for i in range(0, hidden, step) for j in range(0, width, hidden)]
    for i, j in places:
        part = dot(active[:, i : i + step], cotangent[:, j : j + hidden], ((0,), (0,)))
        bulk.feed(part.astype(bf16))
    bulk.begin()
    ups = [
        dot(normed_two[:, i * step : (i + 1) * step], grad_upper, ((0,), (0,))).astype(bf16)
        for i in range(4)
    ]
    for part in ups[:3]:
        bulk.feed(part)
    grad_b_up = jnp.sum(grad_upper.astype(f32), axis=0)
    back_part = dot(grad_upper, w_up, ((1,), (1,))).astype(bf16)
    grad_norm_two = reduce_rows(back_part, at_calls(bulk.sync, 0, 2)).astype(f32)
    grad_resid, grad_ln2_gain, grad_ln2_bias = norm_back(grad_norm_two, raw_two, inv_two, ln2_gain)
    grad_out_rows = rows_of(cotangent).astype(f32)
    grad_mid = grad_out_rows + grad_resid
    grad_mid_low = gather_rows(grad_mid.astype(bf16), at_calls(bulk.sync, 1))
    grad_attended = dot(grad_mid_low, w_out, ((1,), (1,))).astype(bf16)
    bulk.feed(
        jnp.concatenate(
            [
                dot(attended, grad_mid_low[:, j : j + hidden], ((0,), (0,))).astype(bf16)
                for j in range(0, width, hidden)
            ]
        ),
    )
    grad_query, grad_keys, grad_vals = attend_back(
        query, keys_vals, grad_attended, pos, valid_windows
    )
    grad_kv = jnp.concatenate([grad_keys, grad_vals], axis=1)
    got = lax.ppermute(grad_kv[:MAX_DOCUMENT].astype(bf16), "wide", behind)
    own = grad_kv[MAX_DOCUMENT:]
    own, active = bulk.sync(own, active)
    mlp_part = dot(active, w_down, ((1,), (0,))).astype(bf16)
    mlp_total = reduce_rows(mlp_part, at_calls(bulk.sync, 0)).astype(f32)
    own, got, mlp_total = bulk.sync(own, got, mlp_total)
    low = rows - MAX_DOCUMENT
    grad_kv = jnp.concatenate([own[:low], own[low:] + got.astype(f32)]).astype(bf16)
    grad_mixed = jnp.concatenate([grad_query, grad_kv], axis=1)
    parts = [
        dot(normed_one[:, i * step : (i + 1) * step], grad_mixed, ((0,), (0,))).astype(bf16)
        for i in range(3)
    ]
    rest = dot(normed_one[:, 3 * step :], grad_mixed, ((0,), (0,))).astype(bf16)
    for i in range(3):
        extra = rest[:, i * local_width : (i + 1) * local_width]
        bulk.feed(jnp.concatenate([parts[i], extra], axis=1))
    bulk.feed(ups[3])
    grad_b_qv = jnp.sum(grad_mixed.astype(f32), axis=0)
    grad_b_qv = [grad_b_qv[i * local_width : (i + 1) * local_width] for i in (0, 2)]
    grad_three = grad_mixed.reshape(rows, 3, local_width)
    back_part = dot(grad_three, w_qkv, ((1, 2), (1, 2))).astype(bf16)
    output = gather_rows((after_attn + b_down + mlp_total).astype(bf16))
    grad_norm_one = reduce_rows(back_part, at_calls(bulk.sync, 0, 2)).astype(f32)
    raw_rows, inv_rows = norm_stats(inputs_rows)
    grad_resid, grad_ln1_gain, grad_ln1_bias = norm_back(
        grad_norm_one, raw_rows, inv_rows, ln1_gain
    )
    grad_input = gather_rows((grad_mid + grad_resid).astype(bf16), at_calls(bulk.sync, 0, 1))

    sums = narrow_total(
        jnp.stack(
            [
                grad_ln2_gain,
                grad_ln2_bias,
                jnp.sum(grad_mid, axis=0),
                jnp.sum(grad_out_rows, axis=0),
                grad_ln1_gain,
                grad_ln1_bias,
            ]
        )
    )
    sums = jnp.concatenate([sums.reshape(-1), grad_b_up] + grad_b_qv)
    sums = line.whole(sums.reshape(-1, 128), bulk.sync).reshape(-1)
    bulk.finish()
    grad_ln2_gain, grad_ln2_bias, grad_b_out, grad_b_down, grad_ln1_gain, grad_ln1_bias = sums[
        : 6 * width
    ].reshape(6, width)
    grad_b_up = sums[6 * width : 6 * width + hidden]
    grad_b_qv = sums[6 * width + hidden :].reshape(2, local_width)

    done = [bulk.result(k).astype(f32) for k in range(7, 11)]
    per_row = width // hidden
    grad_w_down = bulk.tiles(range(4), 4, per_row)
    grad_w_up = bulk.last_tile(11, bulk.tiles(range(4, 7), 4, 1))
    grad_w_out = jnp.concatenate(
        [done[0][i * local_width : (i + 1) * local_width] for i in range(per_row)], axis=1
    )
    mixed_done = done[1:4]
    grad_w_qkv = jnp.stack(
        [
            jnp.concatenate(
                [value[:, c * local_width : (c + 1) * local_width] for value in mixed_done]
                + [mixed_done[c][:, 3 * local_width :]]
            )
            for c in range(3)
        ],
        axis=1,
    )
    return (
        output,
        grad_input,
        grad_ln1_gain,
        grad_ln1_bias,
        grad_w_qkv,
        grad_b_qv,
        grad_w_out,
        grad_b_out,
        grad_ln2_gain,
        grad_ln2_bias,
        grad_w_up,
        grad_b_up,
        grad_w_down,
        grad_b_down,
    )


def solution(mesh):
    return jax.shard_map(
        on_device,
        mesh=mesh,
        in_specs=(
            P("wide", None),
            P(),
            P(),
            P(None, None, "narrow"),
            P(None, "narrow"),
            P("narrow", None),
            P(),
            P(),
            P(),
            P(None, "narrow"),
            P("narrow"),
            P("narrow", None),
            P(),
            P(),
            P(),
            P(),
            P("wide", None),
        ),
        out_specs=(
            P("wide", None),
            P("wide", None),
            P(),
            P(),
            P(None, None, "narrow"),
            P(None, "narrow"),
            P("narrow", None),
            P(),
            P(),
            P(),
            P(None, "narrow"),
            P("narrow"),
            P("narrow", None),
            P(),
        ),
        check_vma=False,
    )
```

```python
import jax
import jax.numpy as jnp
from jax import lax
from jax.experimental import pallas as pl
from jax.experimental.pallas import tpu as pltpu
from jax.sharding import PartitionSpec as P


HEAD_DIM = 128
MAX_DOCUMENT = 768
QUERY_BLOCK = 256
WINDOW = MAX_DOCUMENT + QUERY_BLOCK
LAG = 3
f32 = jnp.float32
bf16 = jnp.bfloat16


def add_low(a, b):
    return (a.astype(f32) + b.astype(f32)).astype(a.dtype)


def pick(value, index, dim):
    return lax.dynamic_index_in_dim(value, index, dim, keepdims=False)


def narrow_bit(bit):
    return (lax.axis_index("narrow") >> bit) & 1


def narrow_bits():
    return lax.axis_size("narrow").bit_length() - 1


def swap(value, bit):
    count = lax.axis_size("narrow")
    return lax.ppermute(value, "narrow", [(i, i ^ (1 << bit)) for i in range(count)])


def bit_orders():
    later = list(range(1, narrow_bits()))
    return later, later[::-1]


def row_block():
    bits = narrow_bits()
    return sum(narrow_bit(b) << (bits - 1 - b) for b in range(bits))


def as_is(*values):
    return values


def at_calls(sync, *which):
    count = iter(range(99))
    return lambda *values: sync(*values) if next(count) in which else values


def reduce_rows(value, sync=as_is):
    bits = narrow_bits()
    rows, width = value.shape
    half_rows = rows >> (bits + 1)
    value = value.reshape(2, rows // 2, width)
    mine = narrow_bit(0)
    got = swap(pick(value, 1 - mine, 0), 0)
    value = add_low(pick(value, mine, 0), got)
    (value,) = sync(value)
    value = value.reshape((2,) * (bits - 1) + (2, half_rows, width))
    orders = bit_orders()
    parts = [lax.index_in_dim(value, half, bits - 1, keepdims=False) for half in range(2)]
    left = [list(range(1, bits)) for _ in orders]
    for step in range(bits - 1):
        for half, order in enumerate(orders):
            b = order[step]
            at = left[half].index(b)
            mine = narrow_bit(b)
            piece = parts[half]
            got = swap(pick(piece, 1 - mine, at), b)
            parts[half] = add_low(pick(piece, mine, at), got)
            left[half].pop(at)
        parts = list(sync(*parts))
    return jnp.concatenate(parts, axis=0)


def pair(value, other, bit, dim):
    return jnp.where(
        narrow_bit(bit) == 0, jnp.stack([value, other], axis=dim), jnp.stack([other, value], axis=dim)
    )


def gather_rows(block, sync=as_is):
    bits = narrow_bits()
    rows, width = block.shape
    orders = [order[::-1] for order in bit_orders()]
    parts = [block[half * (rows // 2) : (half + 1) * (rows // 2)] for half in range(2)]
    for step in range(bits - 1):
        for half, order in enumerate(orders):
            b = order[step]
            at = sum(1 for x in order[:step] if x < b)
            got = swap(parts[half], b)
            parts[half] = pair(parts[half], got, b, at)
        parts = list(sync(*parts))
    value = jnp.stack(parts, axis=bits - 1)
    got = swap(value, 0)
    value = pair(value, got, 0, 0)
    return value.reshape(rows << bits, width)


def narrow_total(value):
    for b in range(narrow_bits()):
        value = value + swap(value, b)
    return value


class Line:
    def __init__(self):
        self.count = lax.axis_size("wide")
        self.half = self.count // 2
        self.at = lax.axis_index("wide")
        self.depth = jnp.minimum(self.at, self.count - 1 - self.at)

    def exchange(self, value, kind):
        pairs = [(i, i + 1) for i in range(kind, self.count - 1, 2)]
        return lax.ppermute(value, "wide", pairs + [(b, a) for a, b in pairs])

    def swaps(self, kind, slot, count):
        n, half = self.count, self.half
        plan = []
        for e in range(half):
            if e % 2 == kind:
                sent = slot - LAG * (e // 2)
                add = e == half - 1
                got = sent if add else slot - LAG * ((n - 2 - e) // 2)
            elif e:
                sent, got, add = slot - LAG * ((n - 1 - e) // 2), slot - LAG * ((e - 1) // 2), True
            else:
                continue
            sent = sent if 0 <= sent < count else None
            got = got if 0 <= got < count else None
            plan.append((e, sent, got, add))
        return plan

    def whole(self, value, sync):
        stream = Stream(self, 1)
        stream.feed(value)
        for slot in range(stream.slots()):
            for kind in range(2):
                stream.start(kind, slot)
                got = stream.waiting(kind, slot)
                if got:
                    stream.take(kind, slot, sync(*got))
        return stream.result(0)


class Stream:
    def __init__(self, line, count):
        self.line = line
        self.count = count
        self.chunks = []
        self.owed = None
        self.final = {}
        self.flying = {}
        self.turn = 0

    def slots(self):
        return self.count + LAG * ((self.line.count - 2) // 2)

    def feed(self, chunk):
        self.chunks.append(chunk)
        if self.owed == len(self.chunks) - 1:
            self.start(0, self.owed)

    def edge(self):
        return (self.line.depth == 0).astype(jnp.int32).reshape(1)

    def pair(self, k):
        return self.chunks[k], self.final.get(k, self.chunks[k])

    def result(self, k):
        held, got = self.pair(k)
        return held if held is got else jnp.where(self.line.depth == 0, got, held)

    def tiles(self, which, count, per_row):
        held, got = zip(*[self.pair(k) for k in which])
        return tiled(self.edge(), held, got, count, per_row)

    def last_tile(self, k, others):
        return tiled(self.edge(), *[[value] for value in self.pair(k)], 4, 1, others)

    def start(self, kind, slot):
        plan = self.line.swaps(kind, slot, self.count)
        sends = [(e, sent) for e, sent, _, _ in plan if sent is not None]
        if not sends:
            return
        value = self.chunks[sends[0][1]]
        for e, sent in sends[1:]:
            value = jnp.where(self.line.depth == e, self.chunks[sent], value)
        got = self.line.exchange(value, kind)
        self.flying[kind, slot] = got, plan

    def waiting(self, kind, slot):
        flight = self.flying.get((kind, slot))
        return () if flight is None else flight[:1]

    def take(self, kind, slot, values):
        short = self.line.half == 2
        for got in values:
            for e, _, k, add in self.flying[kind, slot][1]:
                if k is None:
                    continue
                held = self.chunks[k]
                if not add and short:
                    self.final[k] = got
                    continue
                new = add_low(held, got) if add else got
                if not short:
                    new = jnp.where(self.line.depth == e, new, held)
                self.chunks[k] = new

    def begin(self):
        self.start(0, 0)
        self.start(0, 1)

    def sync(self, *values):
        n = self.turn
        self.turn += 1
        outer = self.waiting(0, n)
        held = lax.optimization_barrier(outer + tuple(values))
        self.take(0, n, held[: len(outer)])
        self.start(1, n)
        self.take(1, n - 1, self.waiting(1, n - 1))
        if len(self.chunks) <= n + 2 < self.count:
            self.owed = n + 2
        else:
            self.start(0, n + 2)
        return held[len(outer) :]

    def finish(self):
        while self.turn < self.slots():
            self.sync()


def norm_stats(values):
    center = values - jnp.mean(values, axis=-1, keepdims=True)
    spread = jnp.mean(center * center, axis=-1, keepdims=True)
    inverse = lax.rsqrt(spread + 1e-05)
    return (center * inverse, inverse)


def norm_back(grad_out, normed_raw, inverse, gain):
    scaled = grad_out * gain
    grad_in = inverse * (
        scaled
        - jnp.mean(scaled, axis=-1, keepdims=True)
        - normed_raw * jnp.mean(scaled * normed_raw, axis=-1, keepdims=True)
    )
    return (grad_in, jnp.sum(grad_out * normed_raw, axis=0), jnp.sum(grad_out, axis=0))


def norm_kernel(x_ref, gain_ref, bias_ref, out_ref):
    normed, _ = norm_stats(x_ref[...].astype(f32))
    out_ref[...] = (normed * gain_ref[...] + bias_ref[...]).astype(bf16)


def norm_rows(values, gain, bias):
    rows, width = values.shape
    block = pl.BlockSpec((128, width), lambda i: (i, 0))
    param = pl.BlockSpec((1, width), lambda i: (0, 0))
    return pl.pallas_call(
        norm_kernel,
        grid=(rows // 128,),
        in_specs=[block, param, param],
        out_specs=block,
        out_shape=jax.ShapeDtypeStruct((rows, width), bf16),
        compiler_params=pltpu.CompilerParams(vmem_limit_bytes=16 << 20),
        name="norm_rows",
    )(values, gain.reshape(1, width), bias.reshape(1, width))


def dot(a, b, dims):
    return lax.dot_general(a, b, (dims, ((), ())), preferred_element_type=f32)


def window_probs(query, keys, pos, valid):
    scores = dot(query, keys, ((1,), (1,))) * HEAD_DIM**-0.5
    own = lax.broadcasted_iota(jnp.int32, scores.shape, 0) + MAX_DOCUMENT
    key = lax.broadcasted_iota(jnp.int32, scores.shape, 1)
    back = own - key
    allowed = ((back >= 0) & (back <= pos) & (valid == 1)) | (back == 0)
    scores = jnp.where(allowed, scores, -1e30)
    exps = jnp.exp(scores - jnp.max(scores, axis=-1, keepdims=True))
    return exps * (1.0 / jnp.sum(exps, axis=-1, keepdims=True))


def attend_kernel(q_ref, k_ref, v_ref, pos_ref, valid_ref, out_ref):
    start = pl.multiple_of(pl.program_id(1) * QUERY_BLOCK, QUERY_BLOCK)
    window = pl.ds(start, WINDOW)
    probs = window_probs(q_ref[...], k_ref[window, :], pos_ref[...], valid_ref[0])
    out_ref[...] = dot(probs.astype(bf16), v_ref[window, :], ((1,), (0,))).astype(bf16)


def attend_back_kernel(q_ref, k_ref, v_ref, do_ref, pos_ref, valid_ref, dq_ref, dk_ref, dv_ref):
    start = pl.multiple_of(pl.program_id(1) * QUERY_BLOCK, QUERY_BLOCK)
    window = pl.ds(start, WINDOW)

    @pl.when(pl.program_id(1) == 0)
    def _():
        dk_ref[...] = jnp.zeros_like(dk_ref)
        dv_ref[...] = jnp.zeros_like(dv_ref)

    query, keys, out = q_ref[...], k_ref[window, :], do_ref[...]
    probs = window_probs(query, keys, pos_ref[...], valid_ref[0])
    dprob = dot(out, v_ref[window, :], ((1,), (1,)))
    dscore = probs * (dprob - jnp.sum(probs * dprob, axis=-1, keepdims=True))
    dscore = dscore.astype(bf16)
    dq_ref[...] = (dot(dscore, keys, ((1,), (0,))) * HEAD_DIM**-0.5).astype(bf16)
    dk_ref[window, :] += dot(dscore, query, ((0,), (0,))) * HEAD_DIM**-0.5
    dv_ref[window, :] += dot(probs.astype(bf16), out, ((0,), (0,)))


def attend_specs(rows):
    block = pl.BlockSpec((QUERY_BLOCK, HEAD_DIM), lambda h, i: (i, h))
    joined = (None, rows + MAX_DOCUMENT, HEAD_DIM)
    keys = pl.BlockSpec(joined, lambda h, i: (0, 0, h))
    vals = pl.BlockSpec(joined, lambda h, i: (1, 0, h))
    pos = pl.BlockSpec((QUERY_BLOCK, 1), lambda h, i: (i, 0))
    valid = pl.BlockSpec((1, 1, WINDOW), lambda h, i: (i, 0, 0))
    return block, keys, vals, pos, valid


def attend(query, keys_vals, pos, valid):
    rows, width = query.shape
    heads = width // HEAD_DIM
    block, keys_spec, vals_spec, pos_spec, valid_spec = attend_specs(rows)
    return pl.pallas_call(
        attend_kernel,
        grid=(heads, rows // QUERY_BLOCK),
        in_specs=[block, keys_spec, vals_spec, pos_spec, valid_spec],
        out_specs=block,
        out_shape=jax.ShapeDtypeStruct((rows, width), bf16),
        compiler_params=pltpu.CompilerParams(vmem_limit_bytes=16 << 20),
        name="attend",
    )(query, keys_vals, keys_vals, pos, valid)


def attend_back(query, keys_vals, out, pos, valid):
    rows, width = query.shape
    heads = width // HEAD_DIM
    block, keys_spec, vals_spec, pos_spec, valid_spec = attend_specs(rows)
    wide_shape = jax.ShapeDtypeStruct((rows + MAX_DOCUMENT, width), f32)
    grad_spec = pl.BlockSpec((rows + MAX_DOCUMENT, HEAD_DIM), lambda h, i: (0, h))
    return pl.pallas_call(
        attend_back_kernel,
        grid=(heads, rows // QUERY_BLOCK),
        in_specs=[block, keys_spec, vals_spec, block, pos_spec, valid_spec],
        out_specs=[block, grad_spec, grad_spec],
        out_shape=[jax.ShapeDtypeStruct((rows, width), bf16), wide_shape, wide_shape],
        compiler_params=pltpu.CompilerParams(vmem_limit_bytes=24 << 20),
        name="attend_back",
    )(query, keys_vals, keys_vals, out, pos, valid)


def tile_kernel(edge_ref, *refs):
    *parts, out_ref = refs
    half = len(parts) // 2
    for at in range(half):
        for edge, part in enumerate((parts[at], parts[at + half])):

            @pl.when((pl.program_id(0) == at) & (edge_ref[0] == edge))
            def _(part=part):
                out_ref[...] = part[...].astype(f32)


def tiled(edge, held, got, count, per_row, others=None):
    rows, cols = held[0].shape
    parts = list(held) + list(got)
    first = 0 if others is None else count - len(held)
    whole = pl.BlockSpec((rows, cols), lambda i: (0, 0), pipeline_mode=pl.Buffered(1))
    specs = [pl.BlockSpec(memory_space=pltpu.SMEM)] + [whole for _ in parts]
    args = [edge] + parts
    kernel = tile_kernel
    if others is not None:
        specs.append(pl.BlockSpec(memory_space=pl.ANY))
        args.append(others)

        def kernel(*refs):
            tile_kernel(*refs[:-2], refs[-1])

    return pl.pallas_call(
        kernel,
        grid=(len(held),),
        in_specs=specs,
        out_specs=pl.BlockSpec(
            (rows, cols), lambda i: ((i + first) // per_row, (i + first) % per_row)
        ),
        out_shape=jax.ShapeDtypeStruct((count // per_row * rows, per_row * cols), f32),
        input_output_aliases={} if others is None else {len(args) - 1: 0},
        compiler_params=pltpu.CompilerParams(vmem_limit_bytes=16 << 20),
        name="tiled",
    )(*args)


def on_device(
    layer_entry_input,
    ln1_gain,
    ln1_bias,
    w_qkv,
    b_qv,
    w_out,
    b_out,
    ln2_gain,
    ln2_bias,
    w_up,
    b_up,
    w_down,
    b_down,
    document_index,
    positions,
    valid,
    cotangent,
):
    rows, width = layer_entry_input.shape
    local_width = w_qkv.shape[2]
    hidden = w_up.shape[1]
    line = Line()
    start = line.at * rows
    ahead = [(i, i + 1) for i in range(line.count - 1)]
    behind = [(i + 1, i) for i in range(line.count - 1)]
    block_rows = rows // lax.axis_size("narrow")
    block_start = row_block() * block_rows

    def rows_of(value):
        return lax.dynamic_slice_in_dim(value, block_start, block_rows, 0)

    pos = lax.dynamic_slice_in_dim(positions, start, rows, 0).reshape(rows, 1)
    padded_valid = jnp.concatenate([jnp.zeros((MAX_DOCUMENT,), jnp.int32), valid])
    valid_near = lax.dynamic_slice_in_dim(padded_valid, start, rows + MAX_DOCUMENT, 0)
    valid_windows = jnp.stack(
        [valid_near[i : i + WINDOW] for i in range(0, rows, QUERY_BLOCK)]
    ).reshape(rows // QUERY_BLOCK, 1, WINDOW)

    normed_one = norm_rows(layer_entry_input, ln1_gain, ln1_bias)
    mixed = dot(normed_one, w_qkv[:, 1:], ((1,), (0,))).transpose(1, 0, 2)
    bias = jnp.stack([jnp.zeros_like(b_qv[1]), b_qv[1]])
    keys_vals = (mixed + bias[:, None, :]).astype(bf16)
    halo = lax.ppermute(keys_vals[:, rows - MAX_DOCUMENT :], "wide", ahead)
    query = (dot(normed_one, w_qkv[:, 0], ((1,), (0,))) + b_qv[0]).astype(bf16)
    grad_active = dot(cotangent, w_down, ((1,), (1,))).astype(bf16)
    halo, query, grad_active = lax.optimization_barrier((halo, query, grad_active))
    keys_vals = jnp.concatenate([halo, keys_vals], axis=1)
    attended = attend(query, keys_vals, pos, valid_windows)
    attn_part = dot(attended, w_out, ((1,), (0,))).astype(bf16)
    attn_total = reduce_rows(attn_part).astype(f32)
    inputs_rows = rows_of(layer_entry_input).astype(f32)
    after_attn = inputs_rows + b_out + attn_total
    raw_two, inv_two = norm_stats(after_attn)
    normed_two = gather_rows((raw_two * ln2_gain + ln2_bias).astype(bf16))

    upper = dot(normed_two, w_up, ((1,), (0,))) + b_up
    active, gelu_pull = jax.vjp(jax.nn.gelu, upper)
    active = active.astype(bf16)
    grad_upper = gelu_pull(grad_active.astype(f32))[0].astype(bf16)

    bulk = Stream(line, 12)
    step = width // 4
    places = [(i, j) for i in range(0, hidden, step) for j in range(0, width, hidden)]
    for i, j in places:
        part = dot(active[:, i : i + step], cotangent[:, j : j + hidden], ((0,), (0,)))
        bulk.feed(part.astype(bf16))
    bulk.begin()
    ups = [
        dot(normed_two[:, i * step : (i + 1) * step], grad_upper, ((0,), (0,))).astype(bf16)
        for i in range(4)
    ]
    for part in ups[:3]:
        bulk.feed(part)
    grad_b_up = jnp.sum(grad_upper.astype(f32), axis=0)
    back_part = dot(grad_upper, w_up, ((1,), (1,))).astype(bf16)
    grad_norm_two = reduce_rows(back_part, at_calls(bulk.sync, 0, 2)).astype(f32)
    grad_resid, grad_ln2_gain, grad_ln2_bias = norm_back(grad_norm_two, raw_two, inv_two, ln2_gain)
    grad_out_rows = rows_of(cotangent).astype(f32)
    grad_mid = grad_out_rows + grad_resid
    grad_mid_low = gather_rows(grad_mid.astype(bf16), at_calls(bulk.sync, 0))
    grad_attended = dot(grad_mid_low, w_out, ((1,), (1,))).astype(bf16)
    bulk.feed(
        jnp.concatenate(
            [
                dot(attended, grad_mid_low[:, j : j + hidden], ((0,), (0,))).astype(bf16)
                for j in range(0, width, hidden)
            ]
        ),
    )
    (grad_attended,) = bulk.sync(grad_attended)
    grad_query, grad_keys, grad_vals = attend_back(
        query, keys_vals, grad_attended, pos, valid_windows
    )
    grad_kv = jnp.concatenate([grad_keys, grad_vals], axis=1)
    got = lax.ppermute(grad_kv[:MAX_DOCUMENT].astype(bf16), "wide", behind)
    own = grad_kv[MAX_DOCUMENT:]
    own, active = bulk.sync(own, active)
    mlp_part = dot(active, w_down, ((1,), (0,))).astype(bf16)
    mlp_total = reduce_rows(mlp_part, at_calls(bulk.sync, 1)).astype(f32)
    own, got, mlp_total = bulk.sync(own, got, mlp_total)
    low = rows - MAX_DOCUMENT
    grad_kv = jnp.concatenate([own[:low], own[low:] + got.astype(f32)]).astype(bf16)
    grad_mixed = jnp.concatenate([grad_query, grad_kv], axis=1)
    parts = [
        dot(normed_one[:, i * step : (i + 1) * step], grad_mixed, ((0,), (0,))).astype(bf16)
        for i in range(3)
    ]
    rest = dot(normed_one[:, 3 * step :], grad_mixed, ((0,), (0,))).astype(bf16)
    for i in range(3):
        extra = rest[:, i * local_width : (i + 1) * local_width]
        bulk.feed(jnp.concatenate([parts[i], extra], axis=1))
    bulk.feed(ups[3])
    grad_b_qv = jnp.sum(grad_mixed.astype(f32), axis=0)
    grad_b_qv = [grad_b_qv[i * local_width : (i + 1) * local_width] for i in (0, 2)]
    grad_three = grad_mixed.reshape(rows, 3, local_width)
    back_part = dot(grad_three, w_qkv, ((1, 2), (1, 2))).astype(bf16)
    output = gather_rows((after_attn + b_down + mlp_total).astype(bf16))
    (back_part,) = bulk.sync(back_part)
    grad_norm_one = reduce_rows(back_part, at_calls(bulk.sync, 1, 2)).astype(f32)
    raw_rows, inv_rows = norm_stats(inputs_rows)
    grad_resid, grad_ln1_gain, grad_ln1_bias = norm_back(
        grad_norm_one, raw_rows, inv_rows, ln1_gain
    )
    grad_input = gather_rows((grad_mid + grad_resid).astype(bf16), at_calls(bulk.sync, 0, 1))

    sums = narrow_total(
        jnp.stack(
            [
                grad_ln2_gain,
                grad_ln2_bias,
                jnp.sum(grad_mid, axis=0),
                jnp.sum(grad_out_rows, axis=0),
                grad_ln1_gain,
                grad_ln1_bias,
            ]
        )
    )
    sums = jnp.concatenate([sums.reshape(-1), grad_b_up] + grad_b_qv)
    sums = line.whole(sums.reshape(-1, 128), bulk.sync).reshape(-1)
    bulk.finish()
    grad_ln2_gain, grad_ln2_bias, grad_b_out, grad_b_down, grad_ln1_gain, grad_ln1_bias = sums[
        : 6 * width
    ].reshape(6, width)
    grad_b_up = sums[6 * width : 6 * width + hidden]
    grad_b_qv = sums[6 * width + hidden :].reshape(2, local_width)

    done = [bulk.result(k).astype(f32) for k in range(7, 11)]
    per_row = width // hidden
    grad_w_down = bulk.tiles(range(4), 4, per_row)
    grad_w_up = bulk.last_tile(11, bulk.tiles(range(4, 7), 4, 1))
    grad_w_out = jnp.concatenate(
        [done[0][i * local_width : (i + 1) * local_width] for i in range(per_row)], axis=1
    )
    mixed_done = done[1:4]
    grad_w_qkv = jnp.stack(
        [
            jnp.concatenate(
                [value[:, c * local_width : (c + 1) * local_width] for value in mixed_done]
                + [mixed_done[c][:, 3 * local_width :]]
            )
            for c in range(3)
        ],
        axis=1,
    )
    return (
        output,
        grad_input,
        grad_ln1_gain,
        grad_ln1_bias,
        grad_w_qkv,
        grad_b_qv,
        grad_w_out,
        grad_b_out,
        grad_ln2_gain,
        grad_ln2_bias,
        grad_w_up,
        grad_b_up,
        grad_w_down,
        grad_b_down,
    )


def solution(mesh):
    return jax.shard_map(
        on_device,
        mesh=mesh,
        in_specs=(
            P("wide", None),
            P(),
            P(),
            P(None, None, "narrow"),
            P(None, "narrow"),
            P("narrow", None),
            P(),
            P(),
            P(),
            P(None, "narrow"),
            P("narrow"),
            P("narrow", None),
            P(),
            P(),
            P(),
            P(),
            P("wide", None),
        ),
        out_specs=(
            P("wide", None),
            P("wide", None),
            P(),
            P(),
            P(None, None, "narrow"),
            P(None, "narrow"),
            P("narrow", None),
            P(),
            P(),
            P(),
            P(None, "narrow"),
            P("narrow"),
            P("narrow", None),
            P(),
        ),
        check_vma=False,
    )
```

```python
import jax
import jax.numpy as jnp
from jax import lax
from jax.experimental import pallas as pl
from jax.experimental.pallas import tpu as pltpu
from jax.sharding import PartitionSpec as P


HEAD_DIM = 128
MAX_DOCUMENT = 768
QUERY_BLOCK = 256
WINDOW = MAX_DOCUMENT + QUERY_BLOCK
LAG = 3
f32 = jnp.float32
bf16 = jnp.bfloat16


def add_low(a, b):
    return (a.astype(f32) + b.astype(f32)).astype(a.dtype)


def pick(value, index, dim):
    return lax.dynamic_index_in_dim(value, index, dim, keepdims=False)


def narrow_bit(bit):
    return (lax.axis_index("narrow") >> bit) & 1


def narrow_bits():
    return lax.axis_size("narrow").bit_length() - 1


def swap(value, bit):
    count = lax.axis_size("narrow")
    return lax.ppermute(value, "narrow", [(i, i ^ (1 << bit)) for i in range(count)])


def bit_orders():
    later = list(range(1, narrow_bits()))
    return later, later[::-1]


def row_block():
    bits = narrow_bits()
    return sum(narrow_bit(b) << (bits - 1 - b) for b in range(bits))


def as_is(*values):
    return values


def at_calls(sync, *which):
    count = iter(range(99))
    return lambda *values: sync(*values) if next(count) in which else values


def reduce_rows(value, sync=as_is):
    bits = narrow_bits()
    rows, width = value.shape
    half_rows = rows >> (bits + 1)
    value = value.reshape(2, rows // 2, width)
    mine = narrow_bit(0)
    got = swap(pick(value, 1 - mine, 0), 0)
    value = add_low(pick(value, mine, 0), got)
    (value,) = sync(value)
    value = value.reshape((2,) * (bits - 1) + (2, half_rows, width))
    orders = bit_orders()
    parts = [lax.index_in_dim(value, half, bits - 1, keepdims=False) for half in range(2)]
    left = [list(range(1, bits)) for _ in orders]
    for step in range(bits - 1):
        for half, order in enumerate(orders):
            b = order[step]
            at = left[half].index(b)
            mine = narrow_bit(b)
            piece = parts[half]
            got = swap(pick(piece, 1 - mine, at), b)
            parts[half] = add_low(pick(piece, mine, at), got)
            left[half].pop(at)
        parts = list(sync(*parts))
    return jnp.concatenate(parts, axis=0)


def pair(value, other, bit, dim):
    return jnp.where(
        narrow_bit(bit) == 0, jnp.stack([value, other], axis=dim), jnp.stack([other, value], axis=dim)
    )


def gather_rows(block, sync=as_is):
    bits = narrow_bits()
    rows, width = block.shape
    orders = [order[::-1] for order in bit_orders()]
    parts = [block[half * (rows // 2) : (half + 1) * (rows // 2)] for half in range(2)]
    for step in range(bits - 1):
        for half, order in enumerate(orders):
            b = order[step]
            at = sum(1 for x in order[:step] if x < b)
            got = swap(parts[half], b)
            parts[half] = pair(parts[half], got, b, at)
        parts = list(sync(*parts))
    value = jnp.stack(parts, axis=bits - 1)
    got = swap(value, 0)
    value = pair(value, got, 0, 0)
    return value.reshape(rows << bits, width)


def narrow_total(value):
    for b in range(narrow_bits()):
        value = value + swap(value, b)
    return value


class Line:
    def __init__(self):
        self.count = lax.axis_size("wide")
        self.half = self.count // 2
        self.at = lax.axis_index("wide")
        self.depth = jnp.minimum(self.at, self.count - 1 - self.at)

    def exchange(self, value, kind):
        pairs = [(i, i + 1) for i in range(kind, self.count - 1, 2)]
        return lax.ppermute(value, "wide", pairs + [(b, a) for a, b in pairs])

    def swaps(self, kind, slot, count):
        n, half = self.count, self.half
        plan = []
        for e in range(half):
            if e % 2 == kind:
                sent = slot - LAG * (e // 2)
                add = e == half - 1
                got = sent if add else slot - LAG * ((n - 2 - e) // 2)
            elif e:
                sent, got, add = slot - LAG * ((n - 1 - e) // 2), slot - LAG * ((e - 1) // 2), True
            else:
                continue
            sent = sent if 0 <= sent < count else None
            got = got if 0 <= got < count else None
            plan.append((e, sent, got, add))
        return plan

    def whole(self, value, sync, middle):
        stream = Stream(self, 1)
        stream.feed(value)
        for slot in range(stream.slots()):
            for kind in range(2):
                stream.start(kind, slot)
                got = stream.waiting(kind, slot)
                if got:
                    stream.take(kind, slot, (middle if kind else sync)(*got))
        return stream.result(0)


class Stream:
    def __init__(self, line, count):
        self.line = line
        self.count = count
        self.chunks = []
        self.owed = None
        self.final = {}
        self.flying = {}
        self.turn = 0

    def slots(self):
        return self.count + LAG * ((self.line.count - 2) // 2)

    def feed(self, chunk):
        self.chunks.append(chunk)
        if self.owed == len(self.chunks) - 1:
            self.start(0, self.owed)

    def edge(self):
        return (self.line.depth == 0).astype(jnp.int32).reshape(1)

    def pair(self, k):
        return self.chunks[k], self.final.get(k, self.chunks[k])

    def result(self, k):
        held, got = self.pair(k)
        return held if held is got else jnp.where(self.line.depth == 0, got, held)

    def tiles(self, which, count, per_row):
        held, got = zip(*[self.pair(k) for k in which])
        return tiled(self.edge(), held, got, count, per_row)

    def last_tile(self, k, others):
        return tiled(self.edge(), *[[value] for value in self.pair(k)], 4, 1, others)

    def start(self, kind, slot):
        plan = self.line.swaps(kind, slot, self.count)
        sends = [(e, sent) for e, sent, _, _ in plan if sent is not None]
        if not sends:
            return
        value = self.chunks[sends[0][1]]
        for e, sent in sends[1:]:
            value = jnp.where(self.line.depth == e, self.chunks[sent], value)
        got = self.line.exchange(value, kind)
        self.flying[kind, slot] = got, plan

    def waiting(self, kind, slot):
        flight = self.flying.get((kind, slot))
        return () if flight is None else flight[:1]

    def take(self, kind, slot, values):
        short = self.line.half == 2
        for got in values:
            for e, _, k, add in self.flying[kind, slot][1]:
                if k is None:
                    continue
                held = self.chunks[k]
                if not add and short:
                    self.final[k] = got
                    continue
                new = add_low(held, got) if add else got
                if not short:
                    new = jnp.where(self.line.depth == e, new, held)
                self.chunks[k] = new

    def begin(self):
        self.start(0, 0)
        self.start(0, 1)

    def sync(self, *values):
        n = self.turn
        self.turn += 1
        outer = self.waiting(0, n)
        held = lax.optimization_barrier(outer + tuple(values))
        self.take(0, n, held[: len(outer)])
        self.start(1, n)
        self.take(1, n - 1, self.waiting(1, n - 1))
        if len(self.chunks) <= n + 2 < self.count:
            self.owed = n + 2
        else:
            self.start(0, n + 2)
        return held[len(outer) :]

    def finish(self):
        while self.turn < self.slots():
            self.sync()


def norm_stats(values):
    center = values - jnp.mean(values, axis=-1, keepdims=True)
    spread = jnp.mean(center * center, axis=-1, keepdims=True)
    inverse = lax.rsqrt(spread + 1e-05)
    return (center * inverse, inverse)


def norm_back(grad_out, normed_raw, inverse, gain):
    scaled = grad_out * gain
    grad_in = inverse * (
        scaled
        - jnp.mean(scaled, axis=-1, keepdims=True)
        - normed_raw * jnp.mean(scaled * normed_raw, axis=-1, keepdims=True)
    )
    return (grad_in, jnp.sum(grad_out * normed_raw, axis=0), jnp.sum(grad_out, axis=0))


def norm_kernel(x_ref, gain_ref, bias_ref, out_ref):
    normed, _ = norm_stats(x_ref[...].astype(f32))
    out_ref[...] = (normed * gain_ref[...] + bias_ref[...]).astype(bf16)


def norm_rows(values, gain, bias):
    rows, width = values.shape
    block = pl.BlockSpec((128, width), lambda i: (i, 0))
    param = pl.BlockSpec((1, width), lambda i: (0, 0))
    return pl.pallas_call(
        norm_kernel,
        grid=(rows // 128,),
        in_specs=[block, param, param],
        out_specs=block,
        out_shape=jax.ShapeDtypeStruct((rows, width), bf16),
        compiler_params=pltpu.CompilerParams(vmem_limit_bytes=16 << 20),
        name="norm_rows",
    )(values, gain.reshape(1, width), bias.reshape(1, width))


def dot(a, b, dims):
    return lax.dot_general(a, b, (dims, ((), ())), preferred_element_type=f32)


def window_probs(query, keys, pos, valid):
    scores = dot(query, keys, ((1,), (1,))) * HEAD_DIM**-0.5
    own = lax.broadcasted_iota(jnp.int32, scores.shape, 0) + MAX_DOCUMENT
    key = lax.broadcasted_iota(jnp.int32, scores.shape, 1)
    back = own - key
    allowed = ((back >= 0) & (back <= pos) & (valid == 1)) | (back == 0)
    scores = jnp.where(allowed, scores, -1e30)
    exps = jnp.exp(scores - jnp.max(scores, axis=-1, keepdims=True))
    return exps * (1.0 / jnp.sum(exps, axis=-1, keepdims=True))


def attend_kernel(q_ref, k_ref, v_ref, pos_ref, valid_ref, out_ref):
    start = pl.multiple_of(pl.program_id(1) * QUERY_BLOCK, QUERY_BLOCK)
    window = pl.ds(start, WINDOW)
    probs = window_probs(q_ref[...], k_ref[window, :], pos_ref[...], valid_ref[0])
    out_ref[...] = dot(probs.astype(bf16), v_ref[window, :], ((1,), (0,))).astype(bf16)


def attend_back_kernel(q_ref, k_ref, v_ref, do_ref, pos_ref, valid_ref, dq_ref, dk_ref, dv_ref):
    start = pl.multiple_of(pl.program_id(1) * QUERY_BLOCK, QUERY_BLOCK)
    window = pl.ds(start, WINDOW)

    @pl.when(pl.program_id(1) == 0)
    def _():
        dk_ref[...] = jnp.zeros_like(dk_ref)
        dv_ref[...] = jnp.zeros_like(dv_ref)

    query, keys, out = q_ref[...], k_ref[window, :], do_ref[...]
    probs = window_probs(query, keys, pos_ref[...], valid_ref[0])
    dprob = dot(out, v_ref[window, :], ((1,), (1,)))
    dscore = probs * (dprob - jnp.sum(probs * dprob, axis=-1, keepdims=True))
    dscore = dscore.astype(bf16)
    dq_ref[...] = (dot(dscore, keys, ((1,), (0,))) * HEAD_DIM**-0.5).astype(bf16)
    dk_ref[window, :] += dot(dscore, query, ((0,), (0,))) * HEAD_DIM**-0.5
    dv_ref[window, :] += dot(probs.astype(bf16), out, ((0,), (0,)))


def attend_specs(rows):
    block = pl.BlockSpec((QUERY_BLOCK, HEAD_DIM), lambda h, i: (i, h))
    joined = (None, rows + MAX_DOCUMENT, HEAD_DIM)
    keys = pl.BlockSpec(joined, lambda h, i: (0, 0, h))
    vals = pl.BlockSpec(joined, lambda h, i: (1, 0, h))
    pos = pl.BlockSpec((QUERY_BLOCK, 1), lambda h, i: (i, 0))
    valid = pl.BlockSpec((1, 1, WINDOW), lambda h, i: (i, 0, 0))
    return block, keys, vals, pos, valid


def attend(query, keys_vals, pos, valid):
    rows, width = query.shape
    heads = width // HEAD_DIM
    block, keys_spec, vals_spec, pos_spec, valid_spec = attend_specs(rows)
    return pl.pallas_call(
        attend_kernel,
        grid=(heads, rows // QUERY_BLOCK),
        in_specs=[block, keys_spec, vals_spec, pos_spec, valid_spec],
        out_specs=block,
        out_shape=jax.ShapeDtypeStruct((rows, width), bf16),
        compiler_params=pltpu.CompilerParams(vmem_limit_bytes=16 << 20),
        name="attend",
    )(query, keys_vals, keys_vals, pos, valid)


def attend_back(query, keys_vals, out, pos, valid):
    rows, width = query.shape
    heads = width // HEAD_DIM
    block, keys_spec, vals_spec, pos_spec, valid_spec = attend_specs(rows)
    wide_shape = jax.ShapeDtypeStruct((rows + MAX_DOCUMENT, width), f32)
    grad_spec = pl.BlockSpec((rows + MAX_DOCUMENT, HEAD_DIM), lambda h, i: (0, h))
    return pl.pallas_call(
        attend_back_kernel,
        grid=(heads, rows // QUERY_BLOCK),
        in_specs=[block, keys_spec, vals_spec, block, pos_spec, valid_spec],
        out_specs=[block, grad_spec, grad_spec],
        out_shape=[jax.ShapeDtypeStruct((rows, width), bf16), wide_shape, wide_shape],
        compiler_params=pltpu.CompilerParams(vmem_limit_bytes=24 << 20),
        name="attend_back",
    )(query, keys_vals, keys_vals, out, pos, valid)


def tile_kernel(edge_ref, *refs):
    *parts, out_ref = refs
    half = len(parts) // 2
    for at in range(half):
        for edge, part in enumerate((parts[at], parts[at + half])):

            @pl.when((pl.program_id(0) == at) & (edge_ref[0] == edge))
            def _(part=part):
                out_ref[...] = part[...].astype(f32)


def tiled(edge, held, got, count, per_row, others=None):
    rows, cols = held[0].shape
    parts = list(held) + list(got)
    first = 0 if others is None else count - len(held)
    whole = pl.BlockSpec((rows, cols), lambda i: (0, 0), pipeline_mode=pl.Buffered(1))
    specs = [pl.BlockSpec(memory_space=pltpu.SMEM)] + [whole for _ in parts]
    args = [edge] + parts
    kernel = tile_kernel
    if others is not None:
        specs.append(pl.BlockSpec(memory_space=pl.ANY))
        args.append(others)

        def kernel(*refs):
            tile_kernel(*refs[:-2], refs[-1])

    return pl.pallas_call(
        kernel,
        grid=(len(held),),
        in_specs=specs,
        out_specs=pl.BlockSpec(
            (rows, cols), lambda i: ((i + first) // per_row, (i + first) % per_row)
        ),
        out_shape=jax.ShapeDtypeStruct((count // per_row * rows, per_row * cols), f32),
        input_output_aliases={} if others is None else {len(args) - 1: 0},
        compiler_params=pltpu.CompilerParams(vmem_limit_bytes=16 << 20),
        name="tiled",
    )(*args)


def on_device(
    layer_entry_input,
    ln1_gain,
    ln1_bias,
    w_qkv,
    b_qv,
    w_out,
    b_out,
    ln2_gain,
    ln2_bias,
    w_up,
    b_up,
    w_down,
    b_down,
    document_index,
    positions,
    valid,
    cotangent,
):
    rows, width = layer_entry_input.shape
    local_width = w_qkv.shape[2]
    hidden = w_up.shape[1]
    line = Line()
    start = line.at * rows
    ahead = [(i, i + 1) for i in range(line.count - 1)]
    behind = [(i + 1, i) for i in range(line.count - 1)]
    block_rows = rows // lax.axis_size("narrow")
    block_start = row_block() * block_rows

    def rows_of(value):
        return lax.dynamic_slice_in_dim(value, block_start, block_rows, 0)

    pos = lax.dynamic_slice_in_dim(positions, start, rows, 0).reshape(rows, 1)
    padded_valid = jnp.concatenate([jnp.zeros((MAX_DOCUMENT,), jnp.int32), valid])
    valid_near = lax.dynamic_slice_in_dim(padded_valid, start, rows + MAX_DOCUMENT, 0)
    valid_windows = jnp.stack(
        [valid_near[i : i + WINDOW] for i in range(0, rows, QUERY_BLOCK)]
    ).reshape(rows // QUERY_BLOCK, 1, WINDOW)

    normed_one = norm_rows(layer_entry_input, ln1_gain, ln1_bias)
    mixed = dot(normed_one, w_qkv[:, 1:], ((1,), (0,))).transpose(1, 0, 2)
    bias = jnp.stack([jnp.zeros_like(b_qv[1]), b_qv[1]])
    keys_vals = (mixed + bias[:, None, :]).astype(bf16)
    halo = lax.ppermute(keys_vals[:, rows - MAX_DOCUMENT :], "wide", ahead)
    query = (dot(normed_one, w_qkv[:, 0], ((1,), (0,))) + b_qv[0]).astype(bf16)
    grad_active = dot(cotangent, w_down, ((1,), (1,))).astype(bf16)
    halo, query, grad_active = lax.optimization_barrier((halo, query, grad_active))
    keys_vals = jnp.concatenate([halo, keys_vals], axis=1)
    attended = attend(query, keys_vals, pos, valid_windows)
    attn_part = dot(attended, w_out, ((1,), (0,))).astype(bf16)
    attn_total = reduce_rows(attn_part).astype(f32)
    inputs_rows = rows_of(layer_entry_input).astype(f32)
    after_attn = inputs_rows + b_out + attn_total
    raw_two, inv_two = norm_stats(after_attn)
    normed_two = gather_rows((raw_two * ln2_gain + ln2_bias).astype(bf16))

    upper = dot(normed_two, w_up, ((1,), (0,))) + b_up
    active, gelu_pull = jax.vjp(jax.nn.gelu, upper)
    active = active.astype(bf16)
    grad_upper = gelu_pull(grad_active.astype(f32))[0].astype(bf16)

    bulk = Stream(line, 12)
    step = width // 4
    places = [(i, j) for i in range(0, hidden, step) for j in range(0, width, hidden)]
    for i, j in places:
        part = dot(active[:, i : i + step], cotangent[:, j : j + hidden], ((0,), (0,)))
        bulk.feed(part.astype(bf16))
    bulk.begin()
    ups = [
        dot(normed_two[:, i * step : (i + 1) * step], grad_upper, ((0,), (0,))).astype(bf16)
        for i in range(4)
    ]
    for part in ups[:3]:
        bulk.feed(part)
    grad_b_up = jnp.sum(grad_upper.astype(f32), axis=0)
    back_part = dot(grad_upper, w_up, ((1,), (1,))).astype(bf16)
    grad_norm_two = reduce_rows(back_part, at_calls(bulk.sync, 0, 2)).astype(f32)
    grad_resid, grad_ln2_gain, grad_ln2_bias = norm_back(grad_norm_two, raw_two, inv_two, ln2_gain)
    grad_out_rows = rows_of(cotangent).astype(f32)
    grad_mid = grad_out_rows + grad_resid
    grad_mid_low = gather_rows(grad_mid.astype(bf16), at_calls(bulk.sync, 0))
    grad_attended = dot(grad_mid_low, w_out, ((1,), (1,))).astype(bf16)
    bulk.feed(
        jnp.concatenate(
            [
                dot(attended, grad_mid_low[:, j : j + hidden], ((0,), (0,))).astype(bf16)
                for j in range(0, width, hidden)
            ]
        ),
    )
    (grad_attended,) = bulk.sync(grad_attended)
    grad_query, grad_keys, grad_vals = attend_back(
        query, keys_vals, grad_attended, pos, valid_windows
    )
    grad_kv = jnp.concatenate([grad_keys, grad_vals], axis=1)
    got = lax.ppermute(grad_kv[:MAX_DOCUMENT].astype(bf16), "wide", behind)
    own = grad_kv[MAX_DOCUMENT:]
    own, active = bulk.sync(own, active)
    mlp_part = dot(active, w_down, ((1,), (0,))).astype(bf16)
    held = [own, got]

    def sync_held(*values):
        *values, held[0], held[1] = bulk.sync(*values, *held)
        return values

    mlp_total = reduce_rows(mlp_part, at_calls(sync_held, 1)).astype(f32)
    own, got = held
    low = rows - MAX_DOCUMENT
    grad_kv = jnp.concatenate([own[:low], own[low:] + got.astype(f32)]).astype(bf16)
    grad_mixed = jnp.concatenate([grad_query, grad_kv], axis=1)
    parts = [
        dot(normed_one[:, i * step : (i + 1) * step], grad_mixed, ((0,), (0,))).astype(bf16)
        for i in range(3)
    ]
    rest = dot(normed_one[:, 3 * step :], grad_mixed, ((0,), (0,))).astype(bf16)
    for i in range(3):
        extra = rest[:, i * local_width : (i + 1) * local_width]
        bulk.feed(jnp.concatenate([parts[i], extra], axis=1))
    bulk.feed(ups[3])
    grad_mixed, mlp_total = bulk.sync(grad_mixed, mlp_total)
    grad_b_qv = jnp.sum(grad_mixed.astype(f32), axis=0)
    grad_b_qv = [grad_b_qv[i * local_width : (i + 1) * local_width] for i in (0, 2)]
    grad_three = grad_mixed.reshape(rows, 3, local_width)
    back_part = dot(grad_three, w_qkv, ((1, 2), (1, 2))).astype(bf16)
    output = gather_rows((after_attn + b_down + mlp_total).astype(bf16))
    (back_part,) = bulk.sync(back_part)
    grad_norm_one = reduce_rows(back_part, at_calls(bulk.sync, 1, 2)).astype(f32)
    raw_rows, inv_rows = norm_stats(inputs_rows)
    grad_resid, grad_ln1_gain, grad_ln1_bias = norm_back(
        grad_norm_one, raw_rows, inv_rows, ln1_gain
    )
    grad_input = gather_rows((grad_mid + grad_resid).astype(bf16), at_calls(bulk.sync, 0, 1))

    sums = narrow_total(
        jnp.stack(
            [
                grad_ln2_gain,
                grad_ln2_bias,
                jnp.sum(grad_mid, axis=0),
                jnp.sum(grad_out_rows, axis=0),
                grad_ln1_gain,
                grad_ln1_bias,
            ]
        )
    )
    sums = jnp.concatenate([sums.reshape(-1), grad_b_up] + grad_b_qv)
    ready = [grad_input]

    def sync_ready(value):
        value, ready[0] = bulk.sync(value, ready[0])
        return (value,)

    sums = line.whole(sums.reshape(-1, 128), bulk.sync, sync_ready).reshape(-1)
    (grad_input,) = ready
    bulk.finish()
    grad_ln2_gain, grad_ln2_bias, grad_b_out, grad_b_down, grad_ln1_gain, grad_ln1_bias = sums[
        : 6 * width
    ].reshape(6, width)
    grad_b_up = sums[6 * width : 6 * width + hidden]
    grad_b_qv = sums[6 * width + hidden :].reshape(2, local_width)

    done = [bulk.result(k).astype(f32) for k in range(7, 11)]
    per_row = width // hidden
    grad_w_down = bulk.tiles(range(4), 4, per_row)
    grad_w_up = bulk.last_tile(11, bulk.tiles(range(4, 7), 4, 1))
    grad_w_out = jnp.concatenate(
        [done[0][i * local_width : (i + 1) * local_width] for i in range(per_row)], axis=1
    )
    mixed_done = done[1:4]
    grad_w_qkv = jnp.stack(
        [
            jnp.concatenate(
                [value[:, c * local_width : (c + 1) * local_width] for value in mixed_done]
                + [mixed_done[c][:, 3 * local_width :]]
            )
            for c in range(3)
        ],
        axis=1,
    )
    return (
        output,
        grad_input,
        grad_ln1_gain,
        grad_ln1_bias,
        grad_w_qkv,
        grad_b_qv,
        grad_w_out,
        grad_b_out,
        grad_ln2_gain,
        grad_ln2_bias,
        grad_w_up,
        grad_b_up,
        grad_w_down,
        grad_b_down,
    )


def solution(mesh):
    return jax.shard_map(
        on_device,
        mesh=mesh,
        in_specs=(
            P("wide", None),
            P(),
            P(),
            P(None, None, "narrow"),
            P(None, "narrow"),
            P("narrow", None),
            P(),
            P(),
            P(),
            P(None, "narrow"),
            P("narrow"),
            P("narrow", None),
            P(),
            P(),
            P(),
            P(),
            P("wide", None),
        ),
        out_specs=(
            P("wide", None),
            P("wide", None),
            P(),
            P(),
            P(None, None, "narrow"),
            P(None, "narrow"),
            P("narrow", None),
            P(),
            P(),
            P(),
            P(None, "narrow"),
            P("narrow"),
            P("narrow", None),
            P(),
        ),
        check_vma=False,
    )
```
